32 devices in a mesh: win: 4 (over z), seq: 8 (over y, x, core).
Axes of the slice: x: 2, y: 2, z: 4, core: 2. Of those that a mesh axis runs over, the one named last changes fastest.
Arguments:
- layer_input: bfloat16 [8, 1024, 768], P('win', 'seq'), may hold values from -6 to 6
- d_out: bfloat16 [8, 1024, 768], P('win', 'seq'), may hold values from -13.5 to 13.5
- rand_ids: int32 [8, 16, 12, 3], P('win', 'seq'), may hold values from 0 to 15
- live_mask: int32 [8], P('win'), may hold values 0 or 1
- w_qkv: float32 [768, 2304], P('seq', 'win'), may hold values from -0.21875 to 0.21875
- w_out: float32 [768, 768], P('seq', 'win'), may hold values from -0.875 to 0.875
- w_up: float32 [768, 3072], P('seq', 'win'), may hold values from -0.25259074 to 0.25259074
- w_down: float32 [3072, 768], P('seq', 'win'), may hold values from -0.109375 to 0.109375
- norm_params: float32 [3072], P(('win', 'seq')), may hold values from -1.2 to 2, as said below
- m_qkv: float32 [768, 2304], P('seq', 'win'), may hold values from -0.0015031901 to 0.0015031901, as said below
- m_out: float32 [768, 768], P('seq', 'win'), may hold values from -0.0015031901 to 0.0015031901, as said below
- m_up: float32 [768, 3072], P('seq', 'win'), may hold values from -0.0015031901 to 0.0015031901, as said below
- m_down: float32 [3072, 768], P('seq', 'win'), may hold values from -0.0015031901 to 0.0015031901, as said below
- m_norm: float32 [3072], P(('win', 'seq')), may hold values from -0.0060127606 to 0.0060127606, as said below
- v_qkv: float32 [768, 2304], P('seq', 'win'), may hold values from 1.412238e-07 to 5.648952e-07
- v_out: float32 [768, 768], P('seq', 'win'), may hold values from 1.412238e-07 to 5.648952e-07
- v_up: float32 [768, 3072], P('seq', 'win'), may hold values from 1.412238e-07 to 5.648952e-07
- v_down: float32 [3072, 768], P('seq', 'win'), may hold values from 1.412238e-07 to 5.648952e-07
- v_norm: float32 [3072], P(('win', 'seq')), may hold values from 2.2595806e-06 to 9.0383225e-06
Outputs:
- output: bfloat16 [8, 1024, 768], P('win', 'seq')
- d_input: float32 [8, 1024, 768], P('win', 'seq')
- g_qkv: float32 [768, 2304], P('seq', 'win')
- g_out: float32 [768, 768], P('seq', 'win')
- g_up: float32 [768, 3072], P('seq', 'win')
- g_down: float32 [3072, 768], P('seq', 'win')
- g_norm: float32 [3072], P(('win', 'seq'))
- new_qkv: float32 [768, 2304], P('seq', 'win')
- new_out: float32 [768, 768], P('seq', 'win')
- new_up: float32 [768, 3072], P('seq', 'win')
- new_down: float32 [3072, 768], P('seq', 'win')
- new_norm: float32 [3072], P(('win', 'seq'))
- mom_qkv: float32 [768, 2304], P('seq', 'win')
- mom_out: float32 [768, 768], P('seq', 'win')
- mom_up: float32 [768, 3072], P('seq', 'win')
- mom_down: float32 [3072, 768], P('seq', 'win')
- mom_norm: float32 [3072], P(('win', 'seq'))
- sec_qkv: float32 [768, 2304], P('seq', 'win')
- sec_out: float32 [768, 768], P('seq', 'win')
- sec_up: float32 [768, 3072], P('seq', 'win')
- sec_down: float32 [3072, 768], P('seq', 'win')
- sec_norm: float32 [3072], P(('win', 'seq'))
- grad_norm: float32 [1], replicated
The draws below stay inside these ranges and needn't reach their ends.
Inputs may be any that keep to these rules, and one draw needn't show every extreme that they name: `norm_params`: gains about 1 in the first and third pieces, shifts of both signs in the second and fourth. `m_qkv`: of both signs. `m_out`: of both signs. `m_up`: of both signs. `m_down`: of both signs. `m_norm`: of both signs.
All inputs are finite; a program needn't handle non-finite values. No bound on the sum of `live_mask` on one device may be relied on, other than what follows from the above.
Results may differ from the reference program's by a relative error of at most 0.035.
Values may be sent and summed in bfloat16 or wider, within the bound.
A program may use at most 320 MiB of HBM per device.

```python
import math
import jax
import jax.numpy as jnp
from jax import lax

D = 768
H = 12
HD = 64
FF = 3072
BLK = 64
NRAND = 3
STEP = 3
WINDOWS = 8
NBLK = 16
WLEN = 1024
PARAMS = 7080960


def draw_d_out(key, part):
    lowest, highest = (0.6, 1.8)
    sample = jnp.clip(jax.random.normal(jax.random.fold_in(key, 401), (WINDOWS, WLEN, D), jnp.float32), -6.0, 6.0)
    place = jnp.arange(D, dtype=jnp.float32) / (D - 1.0)
    ramp = lowest * jnp.exp(place * math.log(highest / lowest))
    return (sample * ramp).astype(jnp.bfloat16)


def draw_w_up(key, part):
    noise = jnp.clip(jax.random.normal(jax.random.fold_in(key, 501), (D, FF), jnp.float32), -4.0, 4.0)
    common = 0.7 * jnp.clip(jax.random.normal(jax.random.fold_in(key, 502), (1, FF), jnp.float32), -4.0, 4.0)
    return (noise + common) * D ** (-0.5)


def draw_norm_params(key, part):
    gains = jnp.exp(jax.random.uniform(jax.random.fold_in(key, 101), (2, D), jnp.float32, math.log(0.5), math.log(2.0)))
    shifts = jnp.clip(0.3 * jax.random.normal(jax.random.fold_in(key, 102), (2, D), jnp.float32), -1.2, 1.2)
    return jnp.stack([gains[0], shifts[0], gains[1], shifts[1]]).reshape(4 * D)


def first_moment(key, tag, shape, factor):
    sample = jax.random.normal(jax.random.fold_in(key, tag), shape, jnp.float32)
    return factor * PARAMS ** (-0.5) * jnp.clip(sample, -4.0, 4.0)


def second_moment(key, tag, shape, factor):
    sample = jax.random.uniform(jax.random.fold_in(key, tag), shape, jnp.float32, 0.0, math.log(4.0))
    return factor * (1.0 / PARAMS) * jnp.exp(sample)


def draw_m_qkv(key, part):
    return first_moment(key, 201, (D, 3 * D), 1.0)


def draw_m_out(key, part):
    return first_moment(key, 202, (D, D), 1.0)


def draw_m_up(key, part):
    return first_moment(key, 203, (D, FF), 1.0)


def draw_m_down(key, part):
    return first_moment(key, 204, (FF, D), 1.0)


def draw_m_norm(key, part):
    return first_moment(key, 205, (4 * D,), 4.0)


def draw_v_qkv(key, part):
    return second_moment(key, 301, (D, 3 * D), 1.0)


def draw_v_out(key, part):
    return second_moment(key, 302, (D, D), 1.0)


def draw_v_up(key, part):
    return second_moment(key, 303, (D, FF), 1.0)


def draw_v_down(key, part):
    return second_moment(key, 304, (FF, D), 1.0)


def draw_v_norm(key, part):
    return second_moment(key, 305, (4 * D,), 16.0)


def place_ends(values, own_key, low, largest):
    shape = values.shape
    index_at = [jax.random.randint(jax.random.fold_in(own_key, axis), (), 0, shape[axis]) for axis in range(len(shape))]
    values = values.at[tuple(index_at)].set(low)
    longest = shape.index(max(shape))
    index_at[longest] = (index_at[longest] + 1) % shape[longest]
    return values.at[tuple(index_at)].set(largest)


def block_scale(key, extent, shards, least, high):
    loudness = 1.0
    for axis_at, parts in shards:
        draws = jax.random.uniform(jax.random.fold_in(jax.random.fold_in(key, 6), axis_at), (parts,), jnp.float32, least / len(shards), high / len(shards))
        loudness = loudness * jnp.repeat(jnp.exp(draws), extent[axis_at] // parts).reshape((-1,) + (1,) * (len(extent) - 1 - axis_at))
    return loudness


def scatter_about(key, shape, deviation, reach, cuts=(), kind=jnp.bfloat16):
    level = block_scale(key, shape, cuts, -0.22, 0.18) if cuts else 1.0
    values = jax.random.normal(key, shape, jnp.float32) * deviation * level
    return jnp.minimum(jnp.maximum(values, -reach), reach).astype(kind)


def setup_inputs(seed: int = 0) -> dict:
    streams_of = jax.random.split(jax.random.key(seed), 20)
    return {
        "layer_input": scatter_about(streams_of[0], (WINDOWS, WLEN, D), 1.0, 6.0, ((0, 4), (1, 8))),
        "d_out": draw_d_out(jax.random.fold_in(streams_of[19], 71), 0),
        "rand_ids": place_ends(jax.random.randint(streams_of[2], (WINDOWS, NBLK, H, NRAND), 0, NBLK), jax.random.fold_in(streams_of[2], 1), 0, NBLK - 1).astype(jnp.int32),
        "live_mask": place_ends((jax.random.randint(streams_of[3], (WINDOWS,), 0, 4) < 3).astype(jnp.int32), jax.random.fold_in(streams_of[3], 1), 0, 1),
        "w_qkv": scatter_about(streams_of[4], (D, 3 * D), D ** -0.5, 0.21875, ((0, 8), (1, 4)), jnp.float32),
        "w_out": scatter_about(streams_of[5], (D, D), (D // 16) ** -0.5, 0.875, ((0, 8), (1, 4)), jnp.float32),
        "w_up": draw_w_up(jax.random.fold_in(streams_of[19], 71), 0),
        "w_down": scatter_about(streams_of[7], (FF, D), FF ** -0.5, 0.109375, ((0, 8), (1, 4)), jnp.float32),
        "norm_params": draw_norm_params(jax.random.fold_in(streams_of[19], 71), 0),
        "m_qkv": draw_m_qkv(jax.random.fold_in(streams_of[19], 71), 0),
        "m_out": draw_m_out(jax.random.fold_in(streams_of[19], 71), 0),
        "m_up": draw_m_up(jax.random.fold_in(streams_of[19], 71), 0),
        "m_down": draw_m_down(jax.random.fold_in(streams_of[19], 71), 0),
        "m_norm": draw_m_norm(jax.random.fold_in(streams_of[19], 71), 0),
        "v_qkv": draw_v_qkv(jax.random.fold_in(streams_of[19], 71), 0),
        "v_out": draw_v_out(jax.random.fold_in(streams_of[19], 71), 0),
        "v_up": draw_v_up(jax.random.fold_in(streams_of[19], 71), 0),
        "v_down": draw_v_down(jax.random.fold_in(streams_of[19], 71), 0),
        "v_norm": draw_v_norm(jax.random.fold_in(streams_of[19], 71), 0),
    }


HIGH = lax.Precision.HIGHEST
NEG = -1e+30
ln_eps = 1e-05
beta_one = 0.5
beta_two = 0.5
adam_eps = 1e-08
decay_rate = 0.1
rate_matrix = 0.04
rate_output = 0.16
rate_norm = 0.6

@jax.custom_vjp
def low(v):
    return lax.optimization_barrier(v.astype(jnp.bfloat16)).astype(jnp.float32)

@jax.custom_vjp
def low_back(v):
    return v

def low_keep(v):
    return (low(v), None)

def low_pass(kept, grad):
    return (grad,)

def back_keep(v):
    return (v, None)

def back_low(kept, grad):
    return (low(grad),)
low.defvjp(low_keep, low_pass)
low_back.defvjp(back_keep, back_low)

def layer_norm(values, gain, shift):
    centre = values - lax.optimization_barrier(jnp.mean(values, axis=-1, keepdims=True))
    spread = lax.optimization_barrier(jnp.mean(centre * centre, axis=-1, keepdims=True))
    return centre * lax.rsqrt(spread + ln_eps) * gain + shift

def slot_blocks(rand_window):
    block_count = rand_window.shape[0]
    here = jnp.arange(block_count, dtype=jnp.int32)
    fixed = jnp.stack([jnp.maximum(here - 1, 0), here, jnp.minimum(here + 1, block_count - 1), jnp.zeros_like(here), jnp.full_like(here, block_count - 1)], axis=1)
    fixed = jnp.broadcast_to(fixed[:, None, :], (block_count, rand_window.shape[1], 5))
    slot_ids = jnp.concatenate([fixed, rand_window.astype(jnp.int32)], axis=2)
    always = jnp.ones((block_count, 1), dtype=bool)
    valid = jnp.concatenate([(here > 0)[:, None], always, (here < block_count - 1)[:, None], jnp.ones((block_count, 2 + rand_window.shape[2]), dtype=bool)], axis=1)
    return (slot_ids, valid)

def layer(window_x, w_qkv, w_out, w_up, w_down, norm_params, slot_ids, valid):
    gains = low(norm_params).reshape(4, D)
    h_one = low(layer_norm(window_x, gains[0], gains[1]))
    qkv = jnp.dot(h_one, low(w_qkv), precision=HIGH)
    queries = low_back(low(qkv[:, :D]))
    keys = low_back(low(qkv[:, D:2 * D]))
    values = low_back(low(qkv[:, 2 * D:]))
    block_count = window_x.shape[0] // BLK
    q_blocks = queries.reshape(block_count, BLK, H, HD).transpose(0, 2, 1, 3)
    k_blocks = keys.reshape(block_count, BLK, H, HD)
    v_blocks = values.reshape(block_count, BLK, H, HD)
    group = math.gcd(block_count, max(1, 512 // BLK))
    head_ix = jnp.arange(H, dtype=jnp.int32)[None, :, None]
    inv_root = 1.0 / math.sqrt(HD)

    def attend(pieces):
        q_group, id_group, valid_group = pieces
        slot_keys = k_blocks[id_group, :, head_ix]
        slot_vals = v_blocks[id_group, :, head_ix]
        raw = jnp.einsum('ghqd,ghskd->ghqsk', q_group, slot_keys, precision=HIGH) * inv_root
        raw = low_back(raw)
        raw = jnp.where(valid_group[:, None, None, :, None], raw, NEG)
        flat = raw.reshape(raw.shape[0], H, BLK, -1)
        prob = low(jax.nn.softmax(flat, axis=-1)).reshape(raw.shape)
        return jnp.einsum('ghqsk,ghskd->ghqd', prob, slot_vals, precision=HIGH)
    turns = block_count // group
    heads_out = lax.map(jax.checkpoint(attend), (q_blocks.reshape(turns, group, H, BLK, HD), slot_ids.reshape(turns, group, H, slot_ids.shape[2]), valid.reshape(turns, group, valid.shape[1])))
    attended = heads_out.reshape(block_count, H, BLK, HD).transpose(0, 2, 1, 3).reshape(-1, D)
    attended = low_back(low(attended))
    branch = low_back(jnp.dot(attended, low(w_out), precision=HIGH))
    middle = window_x + branch
    h_two = low(layer_norm(middle, gains[2], gains[3]))
    up_proj = low_back(jnp.dot(h_two, low(w_up), precision=HIGH))
    active = low(jax.nn.gelu(up_proj))
    feed = low_back(jnp.dot(active, low(w_down), precision=HIGH))
    return middle + feed

def adam_update(weight, grad, first, second, rate, decay, fix_one, fix_two):
    first_new = beta_one * first + (1.0 - beta_one) * grad
    second_new = beta_two * second + (1.0 - beta_two) * grad * grad
    stride = first_new / fix_one / (jnp.sqrt(second_new / fix_two) + adam_eps)
    return (weight - rate * (stride + decay * weight), first_new, second_new)

def reference(layer_input, d_out, rand_ids, live_mask, w_qkv, w_out, w_up, w_down, norm_params, m_qkv, m_out, m_up, m_down, m_norm, v_qkv, v_out, v_up, v_down, v_norm):
    loss_weight = live_mask.astype(jnp.float32)
    params = (w_qkv, w_out, w_up, w_down, norm_params)

    def one_window(carry, items):
        window_x, window_dout, window_rand, window_weight = items
        slot_ids, valid = slot_blocks(window_rand)

        def run(xa, wa, wb, wc, wd, we):
            return layer(xa, wa, wb, wc, wd, we, slot_ids, valid)
        result, pull = jax.vjp(run, window_x.astype(jnp.float32), *params)
        grads = pull(window_dout.astype(jnp.float32) * window_weight)
        carry = tuple((acc + new for acc, new in zip(carry, grads[1:])))
        return (carry, (result.astype(jnp.bfloat16), grads[0]))
    zeros = tuple((jnp.zeros_like(param) for param in params))
    sums, (output, d_input) = lax.scan(one_window, zeros, (layer_input, d_out, rand_ids, loss_weight))
    squares = jnp.float32(0.0)
    for grad in sums:
        squares = squares + jnp.sum(grad * grad)
    grad_norm = jnp.sqrt(squares)
    factor = 1.0 / jnp.maximum(grad_norm, 1.0)
    clipped = tuple((grad * factor for grad in sums))
    count = jnp.float32(STEP)
    fix_one = 1.0 - jnp.power(jnp.float32(beta_one), count)
    fix_two = 1.0 - jnp.power(jnp.float32(beta_two), count)
    firsts = (m_qkv, m_out, m_up, m_down, m_norm)
    seconds = (v_qkv, v_out, v_up, v_down, v_norm)
    rates = (rate_matrix, rate_output, rate_matrix, rate_matrix, rate_norm)
    news, moms, secs = ([], [], [])
    for index in range(5):
        decay = 0.0 if index == 4 else decay_rate
        new_w, new_m, new_v = adam_update(params[index], clipped[index], firsts[index], seconds[index], rates[index], decay, fix_one, fix_two)
        news.append(new_w)
        moms.append(new_m)
        secs.append(new_v)
    return (output, d_input, clipped[0], clipped[1], clipped[2], clipped[3], clipped[4], news[0], news[1], news[2], news[3], news[4], moms[0], moms[1], moms[2], moms[3], moms[4], secs[0], secs[1], secs[2], secs[3], secs[4], grad_norm.reshape(1))
```

```python
import math

import jax
import jax.numpy as jnp
from jax import lax
from jax.sharding import PartitionSpec as P

H = 12
HD = 64
BLK = 64
STEP = 3


NEG = -1e30
ln_eps = 1e-05
beta_one = 0.5
beta_two = 0.5
adam_eps = 1e-08
decay_rate = 0.1
rate_matrix = 0.04
rate_output = 0.16
rate_norm = 0.6


def layer_norm(values, gain, shift):
    centre = values - jnp.mean(values, axis=-1, keepdims=True)
    spread = jnp.mean(centre * centre, axis=-1, keepdims=True)
    return centre * lax.rsqrt(spread + ln_eps) * gain + shift


def slot_counts(rand_ids, first_block, block_count):
    blocks_dev = rand_ids.shape[1]
    here = (first_block + jnp.arange(blocks_dev, dtype=jnp.int32))[:, None]
    every = jnp.arange(block_count, dtype=jnp.int32)[None, :]
    near = (jnp.abs(here - every) <= 1).astype(jnp.float32)
    ends = (every == 0).astype(jnp.float32) + (every == block_count - 1).astype(jnp.float32)
    drawn = jnp.sum((rand_ids[..., None] == every[0]).astype(jnp.float32), axis=3)
    return (near + ends)[None, :, None, :] + drawn


def adam_update(weight, grad, first, second, rate, decay, fix_one, fix_two):
    first_new = beta_one * first + (1.0 - beta_one) * grad
    second_new = beta_two * second + (1.0 - beta_two) * grad * grad
    stride = first_new / fix_one / (jnp.sqrt(second_new / fix_two) + adam_eps)
    return (weight - rate * (stride + decay * weight), first_new, second_new)


def per_device(
    layer_input,
    d_out,
    rand_ids,
    live_mask,
    w_qkv,
    w_out,
    w_up,
    w_down,
    norm_params,
    m_qkv,
    m_out,
    m_up,
    m_down,
    m_norm,
    v_qkv,
    v_out,
    v_up,
    v_down,
    v_norm,
):
    wins, local_len, width = layer_input.shape
    blocks_dev = local_len // BLK
    block_count = blocks_dev * lax.axis_size("seq")
    first_block = lax.axis_index("seq") * blocks_dev
    inv_root = 1.0 / math.sqrt(HD)
    rows = wins * local_len
    low_qkv = w_qkv.astype(jnp.bfloat16)
    low_out = w_out.astype(jnp.bfloat16)
    low_up = w_up.astype(jnp.bfloat16)
    low_down = w_down.astype(jnp.bfloat16)
    low_norm = norm_params.astype(jnp.bfloat16)
    full_qkv, full_out, full_up, full_down = (
        lax.all_gather(lax.all_gather(low, "win", axis=1, tiled=True), "seq", axis=0, tiled=True)
        for low in (low_qkv, low_out, low_up, low_down)
    )
    full_norm = lax.all_gather(low_norm, ("win", "seq"), axis=0, tiled=True)
    gains = full_norm.astype(jnp.float32).reshape(4, width)
    loss_weight = live_mask.astype(jnp.float32)
    counts = slot_counts(rand_ids, first_block, block_count)
    bias = jnp.where(counts > 0, jnp.log(jnp.maximum(counts, 1.0)), NEG)
    bias = jnp.repeat(bias, BLK, axis=3)[:, :, :, None, :]
    tokens = layer_input.astype(jnp.float32).reshape(rows, width)
    h_one = layer_norm(tokens, gains[0], gains[1]).astype(jnp.bfloat16)
    qkv = jnp.dot(h_one, full_qkv, preferred_element_type=jnp.float32)
    q_heads = qkv[:, :width].astype(jnp.bfloat16).reshape(wins, blocks_dev, BLK, H, HD)
    keyval = qkv[:, width:].astype(jnp.bfloat16).reshape(wins, local_len, 2 * width)
    window = lax.all_gather(keyval, "seq", axis=1, tiled=True)
    shaped = window.reshape(wins, block_count * BLK, 2, H, HD)
    keys, values = shaped[:, :, 0], shaped[:, :, 1]
    scores = (
        jnp.einsum("wbqhd,wkhd->wbhqk", q_heads, keys, preferred_element_type=jnp.float32)
        * inv_root
        + bias
    )
    top = jnp.max(scores, axis=-1, keepdims=True)
    log_total = top + jnp.log(jnp.sum(jnp.exp(scores - top), axis=-1, keepdims=True))
    prob = jnp.exp(scores - log_total).astype(jnp.bfloat16)
    heads_out = jnp.einsum("wbhqk,wkhd->wbqhd", prob, values, preferred_element_type=jnp.float32)
    attended = heads_out.astype(jnp.bfloat16).reshape(rows, width)
    middle = tokens + jnp.dot(attended, full_out, preferred_element_type=jnp.float32)
    h_two = layer_norm(middle, gains[2], gains[3]).astype(jnp.bfloat16)
    up_proj = jnp.dot(h_two, full_up, preferred_element_type=jnp.float32)
    active = jax.nn.gelu(up_proj).astype(jnp.bfloat16)
    result = middle + jnp.dot(active, full_down, preferred_element_type=jnp.float32)
    output = result.astype(jnp.bfloat16).reshape(wins, local_len, width)
    grad_y = (d_out.astype(jnp.float32) * loss_weight[:, None, None]).reshape(rows, width)
    grad_ffn = grad_y.astype(jnp.bfloat16)
    raw_down = jnp.einsum("tf,td->fd", active, grad_ffn, preferred_element_type=jnp.float32)
    grad_act = jnp.einsum("td,fd->tf", grad_ffn, full_down, preferred_element_type=jnp.float32)
    gelu_pull = jax.vjp(jax.nn.gelu, up_proj)[1]
    grad_up = gelu_pull(grad_act)[0].astype(jnp.bfloat16)
    raw_up = jnp.einsum("td,tf->df", h_two, grad_up, preferred_element_type=jnp.float32)
    grad_h_two = jnp.einsum("tf,df->td", grad_up, full_up, preferred_element_type=jnp.float32)
    norm_pull = jax.vjp(layer_norm, middle, gains[2], gains[3])[1]
    grad_mid_ln, raw_gain_two, raw_shift_two = norm_pull(grad_h_two)
    grad_mid = grad_y + grad_mid_ln
    grad_att = grad_mid.astype(jnp.bfloat16)
    raw_out = jnp.einsum("td,te->de", attended, grad_att, preferred_element_type=jnp.float32)
    grad_o = jnp.einsum("te,de->td", grad_att, full_out, preferred_element_type=jnp.float32)
    grad_o = grad_o.astype(jnp.bfloat16).reshape(wins, blocks_dev, BLK, H, HD)
    grad_p = jnp.einsum("wbqhd,wkhd->wbhqk", grad_o, values, preferred_element_type=jnp.float32)
    prob_f = prob.astype(jnp.float32)
    inner = jnp.sum(prob_f * grad_p, axis=-1, keepdims=True)
    grad_s = (prob_f * (grad_p - inner)).astype(jnp.bfloat16)
    grad_q = (
        jnp.einsum("wbhqk,wkhd->wbqhd", grad_s, keys, preferred_element_type=jnp.float32)
        * inv_root
    )
    grad_v = jnp.einsum("wbhqk,wbqhd->wkhd", prob, grad_o, preferred_element_type=jnp.float32)
    grad_k = (
        jnp.einsum("wbhqk,wbqhd->wkhd", grad_s, q_heads, preferred_element_type=jnp.float32)
        * inv_root
    )
    grad_kv = jnp.stack([grad_k, grad_v], axis=2).astype(jnp.bfloat16)
    grad_kv = lax.psum_scatter(
        grad_kv.reshape(wins, block_count * BLK, 2 * width),
        "seq",
        scatter_dimension=1,
        tiled=True,
    ).reshape(rows, 2 * width)
    grad_qkv = jnp.concatenate(
        [grad_q.reshape(rows, width).astype(jnp.bfloat16), grad_kv], axis=1
    )
    raw_qkv = jnp.einsum("td,te->de", h_one, grad_qkv, preferred_element_type=jnp.float32)
    grad_h_one = jnp.einsum("te,de->td", grad_qkv, full_qkv, preferred_element_type=jnp.float32)
    first_pull = jax.vjp(layer_norm, tokens, gains[0], gains[1])[1]
    grad_tok_ln, raw_gain_one, raw_shift_one = first_pull(grad_h_one)
    d_input = (grad_mid + grad_tok_ln).reshape(wins, local_len, width)
    raw_norm = jnp.concatenate([raw_gain_one, raw_shift_one, raw_gain_two, raw_shift_two])
    red_qkv, red_out, red_up, red_down = (
        lax.psum_scatter(
            lax.psum_scatter(raw.astype(jnp.bfloat16), "seq", scatter_dimension=0, tiled=True),
            "win",
            scatter_dimension=1,
            tiled=True,
        ).astype(jnp.float32)
        for raw in (raw_qkv, raw_out, raw_up, raw_down)
    )
    red_norm = lax.psum_scatter(raw_norm, ("win", "seq"), scatter_dimension=0, tiled=True)
    reduced = (red_qkv, red_out, red_up, red_down, red_norm)
    local_squares = jnp.float32(0.0)
    for grad in reduced:
        local_squares = local_squares + jnp.sum(grad * grad)
    grad_norm = jnp.sqrt(lax.psum(local_squares, ("win", "seq")))
    factor = 1.0 / jnp.maximum(grad_norm, 1.0)
    clipped = tuple((grad * factor for grad in reduced))
    count = jnp.float32(STEP)
    fix_one = 1.0 - jnp.power(jnp.float32(beta_one), count)
    fix_two = 1.0 - jnp.power(jnp.float32(beta_two), count)
    params = (w_qkv, w_out, w_up, w_down, norm_params)
    firsts = (m_qkv, m_out, m_up, m_down, m_norm)
    seconds = (v_qkv, v_out, v_up, v_down, v_norm)
    rates = (rate_matrix, rate_output, rate_matrix, rate_matrix, rate_norm)
    news, moms, secs = ([], [], [])
    for index in range(5):
        decay = 0.0 if index == 4 else decay_rate
        new_w, new_m, new_v = adam_update(
            params[index],
            clipped[index],
            firsts[index],
            seconds[index],
            rates[index],
            decay,
            fix_one,
            fix_two,
        )
        news.append(new_w)
        moms.append(new_m)
        secs.append(new_v)
    return (
        output,
        d_input,
        clipped[0],
        clipped[1],
        clipped[2],
        clipped[3],
        clipped[4],
        news[0],
        news[1],
        news[2],
        news[3],
        news[4],
        moms[0],
        moms[1],
        moms[2],
        moms[3],
        moms[4],
        secs[0],
        secs[1],
        secs[2],
        secs[3],
        secs[4],
        grad_norm.reshape(1),
    )


def solution(mesh):
    placed = (
        P("win", "seq", None),
        P("win", "seq", None),
        P("win", "seq", None, None),
        P("win"),
        P("seq", "win"),
        P("seq", "win"),
        P("seq", "win"),
        P("seq", "win"),
        P(("win", "seq")),
        P("seq", "win"),
        P("seq", "win"),
        P("seq", "win"),
        P("seq", "win"),
        P(("win", "seq")),
        P("seq", "win"),
        P("seq", "win"),
        P("seq", "win"),
        P("seq", "win"),
        P(("win", "seq")),
    )
    return jax.shard_map(
        per_device,
        mesh=mesh,
        in_specs=placed,
        out_specs=(
            P("win", "seq", None),
            P("win", "seq", None),
            P("seq", "win"),
            P("seq", "win"),
            P("seq", "win"),
            P("seq", "win"),
            P(("win", "seq")),
            P("seq", "win"),
            P("seq", "win"),
            P("seq", "win"),
            P("seq", "win"),
            P(("win", "seq")),
            P("seq", "win"),
            P("seq", "win"),
            P("seq", "win"),
            P("seq", "win"),
            P(("win", "seq")),
            P("seq", "win"),
            P("seq", "win"),
            P("seq", "win"),
            P("seq", "win"),
            P(("win", "seq")),
            P(),
        ),
        check_vma=False,
    )
```

```python
import functools
import math
from typing import Any, NamedTuple

import jax
import jax.numpy as jnp
from jax import lax
from jax.experimental import pallas as pl
from jax.experimental.pallas import tpu as pltpu
from jax.sharding import PartitionSpec as P

H = 12
HD = 64
BLK = 64
STEP = 3


NEG = -1e30
ln_eps = 1e-05
beta_one = 0.5
beta_two = 0.5
adam_eps = 1e-08
decay_rate = 0.1
rate_matrix = 0.04
rate_output = 0.16
rate_norm = 0.6
VMEM_LIMIT = 63 << 20


def layer_norm(values, gain, shift):
    centre = values - jnp.mean(values, axis=-1, keepdims=True)
    spread = jnp.mean(centre * centre, axis=-1, keepdims=True)
    return centre * lax.rsqrt(spread + ln_eps) * gain + shift


def slot_counts(rand_ids, first_block, block_count):
    blocks_dev = rand_ids.shape[1]
    here = (first_block + jnp.arange(blocks_dev, dtype=jnp.int32))[:, None]
    every = jnp.arange(block_count, dtype=jnp.int32)[None, :]
    near = (jnp.abs(here - every) <= 1).astype(jnp.float32)
    ends = (every == 0).astype(jnp.float32) + (every == block_count - 1).astype(jnp.float32)
    drawn = jnp.sum((rand_ids[..., None] == every[0]).astype(jnp.float32), axis=3)
    return (near + ends)[None, :, None, :] + drawn


def adam_update(weight, grad, first, second, rate, decay, fix_one, fix_two):
    first_new = beta_one * first + (1.0 - beta_one) * grad
    second_new = beta_two * second + (1.0 - beta_two) * grad * grad
    stride = first_new / fix_one / (jnp.sqrt(second_new / fix_two) + adam_eps)
    return (weight - rate * (stride + decay * weight), first_new, second_new)


def per_device(
    layer_input,
    d_out,
    rand_ids,
    live_mask,
    w_qkv,
    w_out,
    w_up,
    w_down,
    norm_params,
    m_qkv,
    m_out,
    m_up,
    m_down,
    m_norm,
    v_qkv,
    v_out,
    v_up,
    v_down,
    v_norm,
):
    wins, local_len, width = layer_input.shape
    blocks_dev = local_len // BLK
    block_count = blocks_dev * lax.axis_size("seq")
    first_block = lax.axis_index("seq") * blocks_dev
    inv_root = 1.0 / math.sqrt(HD)
    rows = wins * local_len
    low_qkv = w_qkv.astype(jnp.bfloat16)
    low_out = w_out.astype(jnp.bfloat16)
    low_up = w_up.astype(jnp.bfloat16)
    low_down = w_down.astype(jnp.bfloat16)
    low_norm = norm_params.astype(jnp.bfloat16)
    full_qkv, full_out, full_up, full_down = (
        lax.all_gather(lax.all_gather(low, "win", axis=1, tiled=True), "seq", axis=0, tiled=True)
        for low in (low_qkv, low_out, low_up, low_down)
    )
    full_norm = lax.all_gather(low_norm, ("win", "seq"), axis=0, tiled=True)
    gains = full_norm.astype(jnp.float32).reshape(4, width)
    loss_weight = live_mask.astype(jnp.float32)
    counts = slot_counts(rand_ids, first_block, block_count)
    bias = jnp.where(counts > 0, jnp.log(jnp.maximum(counts, 1.0)), NEG)
    bias = jnp.repeat(bias, BLK, axis=3)[:, :, :, None, :]
    tokens = layer_input.astype(jnp.float32).reshape(rows, width)
    h_one = layer_norm(tokens, gains[0], gains[1]).astype(jnp.bfloat16)
    qkv = jnp.dot(h_one, full_qkv, preferred_element_type=jnp.float32)
    q_heads = qkv[:, :width].astype(jnp.bfloat16).reshape(wins, blocks_dev, BLK, H, HD)
    keyval = qkv[:, width:].astype(jnp.bfloat16).reshape(wins, local_len, 2 * width)
    window = lax.all_gather(keyval, "seq", axis=1, tiled=True)
    shaped = window.reshape(wins, block_count * BLK, 2, H, HD)
    keys, values = shaped[:, :, 0], shaped[:, :, 1]
    scores = (
        jnp.einsum("wbqhd,wkhd->wbhqk", q_heads, keys, preferred_element_type=jnp.float32)
        * inv_root
        + bias
    )
    top = jnp.max(scores, axis=-1, keepdims=True)
    log_total = top + jnp.log(jnp.sum(jnp.exp(scores - top), axis=-1, keepdims=True))
    prob = jnp.exp(scores - log_total).astype(jnp.bfloat16)
    heads_out = jnp.einsum("wbhqk,wkhd->wbqhd", prob, values, preferred_element_type=jnp.float32)
    attended = heads_out.astype(jnp.bfloat16).reshape(rows, width)
    middle = tokens + jnp.dot(attended, full_out, preferred_element_type=jnp.float32)
    h_two = layer_norm(middle, gains[2], gains[3]).astype(jnp.bfloat16)
    up_proj = jnp.dot(h_two, full_up, preferred_element_type=jnp.float32)
    active = jax.nn.gelu(up_proj).astype(jnp.bfloat16)
    result = middle + jnp.dot(active, full_down, preferred_element_type=jnp.float32)
    output = result.astype(jnp.bfloat16).reshape(wins, local_len, width)
    grad_y = (d_out.astype(jnp.float32) * loss_weight[:, None, None]).reshape(rows, width)
    grad_ffn = grad_y.astype(jnp.bfloat16)
    raw_down = jnp.einsum("tf,td->fd", active, grad_ffn, preferred_element_type=jnp.float32)
    grad_act = jnp.einsum("td,fd->tf", grad_ffn, full_down, preferred_element_type=jnp.float32)
    gelu_pull = jax.vjp(jax.nn.gelu, up_proj)[1]
    grad_up = gelu_pull(grad_act)[0].astype(jnp.bfloat16)
    raw_up = jnp.einsum("td,tf->df", h_two, grad_up, preferred_element_type=jnp.float32)
    grad_h_two = jnp.einsum("tf,df->td", grad_up, full_up, preferred_element_type=jnp.float32)
    norm_pull = jax.vjp(layer_norm, middle, gains[2], gains[3])[1]
    grad_mid_ln, raw_gain_two, raw_shift_two = norm_pull(grad_h_two)
    grad_mid = grad_y + grad_mid_ln
    grad_att = grad_mid.astype(jnp.bfloat16)
    raw_out = jnp.einsum("td,te->de", attended, grad_att, preferred_element_type=jnp.float32)
    grad_o = jnp.einsum("te,de->td", grad_att, full_out, preferred_element_type=jnp.float32)
    grad_o = grad_o.astype(jnp.bfloat16).reshape(wins, blocks_dev, BLK, H, HD)
    grad_p = jnp.einsum("wbqhd,wkhd->wbhqk", grad_o, values, preferred_element_type=jnp.float32)
    prob_f = prob.astype(jnp.float32)
    inner = jnp.sum(prob_f * grad_p, axis=-1, keepdims=True)
    grad_s = (prob_f * (grad_p - inner)).astype(jnp.bfloat16)
    grad_q = (
        jnp.einsum("wbhqk,wkhd->wbqhd", grad_s, keys, preferred_element_type=jnp.float32)
        * inv_root
    )
    grad_v = jnp.einsum("wbhqk,wbqhd->wkhd", prob, grad_o, preferred_element_type=jnp.float32)
    grad_k = (
        jnp.einsum("wbhqk,wbqhd->wkhd", grad_s, q_heads, preferred_element_type=jnp.float32)
        * inv_root
    )
    grad_kv = jnp.stack([grad_k, grad_v], axis=2).astype(jnp.bfloat16)
    grad_kv = lax.psum_scatter(
        grad_kv.reshape(wins, block_count * BLK, 2 * width),
        "seq",
        scatter_dimension=1,
        tiled=True,
    ).reshape(rows, 2 * width)
    grad_qkv = jnp.concatenate(
        [grad_q.reshape(rows, width).astype(jnp.bfloat16), grad_kv], axis=1
    )
    raw_qkv = jnp.einsum("td,te->de", h_one, grad_qkv, preferred_element_type=jnp.float32)
    grad_h_one = jnp.einsum("te,de->td", grad_qkv, full_qkv, preferred_element_type=jnp.float32)
    first_pull = jax.vjp(layer_norm, tokens, gains[0], gains[1])[1]
    grad_tok_ln, raw_gain_one, raw_shift_one = first_pull(grad_h_one)
    d_input = (grad_mid + grad_tok_ln).reshape(wins, local_len, width)
    raw_norm = jnp.concatenate([raw_gain_one, raw_shift_one, raw_gain_two, raw_shift_two])
    red_qkv, red_out, red_up, red_down = (
        lax.psum_scatter(
            lax.psum_scatter(raw.astype(jnp.bfloat16), "seq", scatter_dimension=0, tiled=True),
            "win",
            scatter_dimension=1,
            tiled=True,
        ).astype(jnp.float32)
        for raw in (raw_qkv, raw_out, raw_up, raw_down)
    )
    red_norm = lax.psum_scatter(raw_norm, ("win", "seq"), scatter_dimension=0, tiled=True)
    reduced = (red_qkv, red_out, red_up, red_down, red_norm)
    local_squares = jnp.float32(0.0)
    for grad in reduced:
        local_squares = local_squares + jnp.sum(grad * grad)
    grad_norm = jnp.sqrt(lax.psum(local_squares, ("win", "seq")))
    factor = 1.0 / jnp.maximum(grad_norm, 1.0)
    clipped = tuple((grad * factor for grad in reduced))
    count = jnp.float32(STEP)
    fix_one = 1.0 - jnp.power(jnp.float32(beta_one), count)
    fix_two = 1.0 - jnp.power(jnp.float32(beta_two), count)
    params = (w_qkv, w_out, w_up, w_down, norm_params)
    firsts = (m_qkv, m_out, m_up, m_down, m_norm)
    seconds = (v_qkv, v_out, v_up, v_down, v_norm)
    rates = (rate_matrix, rate_output, rate_matrix, rate_matrix, rate_norm)
    news, moms, secs = ([], [], [])
    for index in range(5):
        decay = 0.0 if index == 4 else decay_rate
        new_w, new_m, new_v = adam_update(
            params[index],
            clipped[index],
            firsts[index],
            seconds[index],
            rates[index],
            decay,
            fix_one,
            fix_two,
        )
        news.append(new_w)
        moms.append(new_m)
        secs.append(new_v)
    return (
        output,
        d_input,
        clipped[0],
        clipped[1],
        clipped[2],
        clipped[3],
        clipped[4],
        news[0],
        news[1],
        news[2],
        news[3],
        news[4],
        moms[0],
        moms[1],
        moms[2],
        moms[3],
        moms[4],
        secs[0],
        secs[1],
        secs[2],
        secs[3],
        secs[4],
        grad_norm.reshape(1),
    )


MESH = pl.DeviceIdType.MESH
F32, BF16 = jnp.float32, jnp.bfloat16
GELU_C = math.sqrt(2.0 / math.pi)
NT = (((1,), (1,)), ((), ()))
TN = (((0,), (0,)), ((), ()))


def dot(a, b):
    return jnp.dot(a, b, preferred_element_type=F32)


def dot_nt(a, b):
    return lax.dot_general(a, b, NT, preferred_element_type=F32)


def dot_tn(a, b):
    return lax.dot_general(a, b, TN, preferred_element_type=F32)


def remote(src, dst, sems, k, dev):
    return pltpu.make_async_remote_copy(
        src_ref=src, dst_ref=dst, send_sem=sems[0].at[k], recv_sem=sems[1].at[k], device_id=dev, device_id_type=MESH
    )


class Place:
    def __init__(self):
        self.w = lax.axis_index("win")
        self.s = s = lax.axis_index("seq")
        self.c = c = s % 2
        x = (s // 2) % 2
        y = s // 4
        dx, dy = 2 - 4 * x, 4 - 8 * y
        self.turn = 1 - 2 * c
        self.n1 = s + (1 - c) * dx + c * dy
        self.n2 = s + (1 - c) * dy + c * dx
        self.nd = s + dx + dy
        self.par = s + self.turn
        self.roles = (s, self.n1, self.n2, self.nd)
        self.par_roles = tuple(r + self.turn for r in (s, self.n2, self.n1, self.nd))


class Blocks:
    def __init__(self, buf, seq_first=False, start=0, count=None):
        self.buf, self.seq_first, self.rows = buf, seq_first, pl.ds(start, buf.shape[3] if count is None else count)

    def block(self, w, s):
        return self.buf.at[(s // 2, s % 2, w, self.rows) if self.seq_first else (w, s // 2, s % 2, self.rows)]

    def read(self, w, s):
        return self.buf[(s // 2, s % 2, w, self.rows) if self.seq_first else (w, s // 2, s % 2, self.rows)]

    def group(self, s):
        every = slice(None)
        return self.buf.at[(s // 2, s % 2, every, self.rows) if self.seq_first else (every, s // 2, s % 2, self.rows)]

    def core(self, c, w=slice(None)):
        return self.buf.at[:, c, w, self.rows]


class Gather:
    def __init__(self, place, blocks, sems):
        self.p, self.b, self.sems = place, blocks, sems

    def push(self, s, k, to):
        remote(self.b.group(s), self.b.group(s), self.sems, k, (self.p.w, to)).start()

    def got(self, s, k):
        remote(self.b.group(s), self.b.group(s), self.sems, k, (self.p.w, self.p.par)).wait_recv()

    def along(self, dz, w):
        block = self.b.block(w, self.p.s)
        return remote(block, block, self.sems, dz - 1, ((self.p.w + dz) % 4, self.p.s))

    def z_send(self):
        for dz in (1, 2, 3):
            self.along(dz, self.p.w).start()

    def stage1(self):
        p = self.p
        for dz in (1, 2, 3):
            self.along(dz, (p.w + 4 - dz) % 4).wait_recv()
        self.push(p.s, 3, p.n1)
        self.push(p.s, 4, p.n2)
        self.push(p.s, 6, p.par)

    def stage2(self):
        p = self.p
        self.got(p.n1, 3)
        self.push(p.n1, 5, p.n2)
        self.push(p.n1, 7, p.par)

    def stage3(self):
        p = self.p
        self.got(p.n2, 4)
        self.push(p.n2, 8, p.par)
        self.got(p.nd, 5)
        self.push(p.nd, 9, p.par)

    def finish(self):
        for k in range(4):
            self.got(self.p.par_roles[k], 6 + k)

    def drain(self):
        p = self.p
        for dz in (1, 2, 3):
            self.along(dz, p.w).wait_send()
        for k, s in ((3, p.s), (4, p.s), (6, p.s), (5, p.n1), (7, p.n1), (8, p.n2), (9, p.nd)):
            remote(self.b.group(s), self.b.group(s), self.sems, k, (p.w, p.par)).wait_send()


class PlaneGather:
    def __init__(self, place, blocks, sems):
        self.p, self.b, self.sems = place, blocks, sems

    def one(self, s, k, to):
        return remote(self.b.block(self.p.w, s), self.b.block(self.p.w, s), self.sems, k, (self.p.w, to))

    def layer(self, c, w, k, dev):
        return remote(self.b.core(c, w), self.b.core(c, w), self.sems, k, dev)

    def stage1(self):
        p = self.p
        self.one(p.s, 3, p.n1).start()
        self.one(p.s, 4, p.n2).start()

    def stage2(self):
        p = self.p
        self.one(p.n1, 3, p.n1).wait_recv()
        self.one(p.n1, 5, p.n2).start()

    def stage3(self):
        p = self.p
        self.one(p.n2, 4, p.n2).wait_recv()
        self.one(p.nd, 5, p.n2).wait_recv()
        for dz in (1, 2, 3):
            self.layer(p.c, p.w, dz - 1, ((p.w + dz) % 4, p.s)).start()
        self.layer(p.c, p.w, 6, (p.w, p.par)).start()

    def stage4(self):
        p = self.p
        for dz in (1, 2, 3):
            w = (p.w + 4 - dz) % 4
            self.layer(p.c, w, dz - 1, (w, p.s)).wait_recv()
            self.layer(p.c, w, 6 + dz, (p.w, p.par)).start()

    def finish(self):
        p = self.p
        for dz in range(4):
            self.layer(1 - p.c, (p.w + 4 - dz) % 4, 6 + dz, (p.w, p.par)).wait_recv()

    def drain(self):
        p = self.p
        self.one(p.s, 3, p.n1).wait_send()
        self.one(p.s, 4, p.n2).wait_send()
        self.one(p.n1, 5, p.n2).wait_send()
        for dz in (1, 2, 3):
            self.layer(p.c, p.w, dz - 1, ((p.w + dz) % 4, p.s)).wait_send()
        for dz in range(4):
            self.layer(p.c, (p.w + 4 - dz) % 4, 6 + dz, (p.w, p.par)).wait_send()


class Scatter:
    def __init__(self, place, blocks, space, sems):
        self.p, self.b, self.sems = place, blocks, sems
        self.c, self.d, self.e, self.f = space

    def copies_c(self):
        p = self.p
        return [remote(self.b.group(p.par_roles[k]), self.c.at[k], self.sems, k, (p.w, p.par)) for k in range(4)]

    def copies_d(self):
        p = self.p
        return [remote(self.c.at[2 + k], self.d.at[k], self.sems, 4 + k, (p.w, p.n2)) for k in range(2)]

    def copy_e(self):
        p = self.p
        return remote(self.c.at[1], self.e, self.sems, 6, (p.w, p.n1))

    def copies_f(self):
        p = self.p
        return [
            remote(self.c.at[0, (p.w + dz) % 4], self.f.at[dz - 1], self.sems, 6 + dz, ((p.w + dz) % 4, p.s))
            for dz in (1, 2, 3)
        ]

    def stage_c(self):
        for copy in self.copies_c():
            copy.start()

    def stage_d(self):
        waits, sends = self.copies_c(), self.copies_d()
        for k in (2, 3, 0, 1):
            waits[k].wait_recv()
            for w in range(4):
                self.c[k, w] = self.c[k, w] + self.b.read(w, self.p.roles[k])
            if k >= 2:
                sends[k - 2].start()

    def stage_e(self):
        waits = self.copies_d()
        for k in (1, 0):
            waits[k].wait_recv()
            for w in range(4):
                self.c[k, w] = self.c[k, w] + self.d[k, w]
            if k == 1:
                self.copy_e().start()

    def stage_f(self):
        self.copy_e().wait_recv()
        for w in range(4):
            self.c[0, w] = self.c[0, w] + self.e[w]
        for copy in self.copies_f():
            copy.start()

    def finish(self):
        total = self.c[0, self.p.w].astype(F32)
        for k, copy in enumerate(self.copies_f()):
            copy.wait_recv()
            total = total + self.f[k].astype(F32)
        return total

    def drain(self):
        for copy in (*self.copies_c(), *self.copies_d(), self.copy_e(), *self.copies_f()):
            copy.wait_send()


class PlaneScatter:
    def __init__(self, place, blocks, space, sems):
        self.p, self.b, self.sems = place, blocks, sems
        self.c, self.z, self.d, self.e = space

    def copy_c(self):
        p = self.p
        return remote(self.b.core(1 - p.c), self.c, self.sems, 0, (p.w, p.par))

    def copies_z(self):
        p = self.p
        return [
            remote(self.c.at[:, (p.w + dz) % 4], self.z.at[dz - 1], self.sems, dz, ((p.w + dz) % 4, p.s)) for dz in (1, 2, 3)
        ]

    def copies_d(self):
        p = self.p
        return [remote(self.c.at[r // 2, p.w], self.d.at[k], self.sems, 4 + k, (p.w, p.n2)) for k, r in enumerate((p.n2, p.nd))]

    def copy_e(self):
        p = self.p
        return remote(self.c.at[p.n1 // 2, p.w], self.e, self.sems, 6, (p.w, p.n1))

    def stage_c(self):
        self.copy_c().start()

    def stage_z(self):
        p = self.p
        self.copy_c().wait_recv()
        for w in range(4):
            for chip in range(4):
                self.c[chip, w] = self.c[chip, w] + self.b.read(w, 2 * chip + p.c)
        for copy in self.copies_z():
            copy.start()

    def stage_d(self):
        p = self.p
        for k, copy in enumerate(self.copies_z()):
            copy.wait_recv()
            for chip in range(4):
                self.c[chip, p.w] = self.c[chip, p.w] + self.z[k, chip]
        for copy in self.copies_d():
            copy.start()

    def stage_e(self):
        p = self.p
        waits = self.copies_d()
        for k, r in ((1, p.n1), (0, p.s)):
            waits[k].wait_recv()
            self.c[r // 2, p.w] = self.c[r // 2, p.w] + self.d[k]
            if k == 1:
                self.copy_e().start()

    def finish(self):
        p = self.p
        self.copy_e().wait_recv()
        return self.c[p.s // 2, p.w].astype(F32) + self.e[...].astype(F32)

    def drain(self):
        for copy in (self.copy_c(), *self.copies_z(), *self.copies_d(), self.copy_e()):
            copy.wait_send()


class Exchange:
    def __init__(self, place, src, dst, sems):
        self.p, self.src, self.dst, self.sems = place, src, dst, sems

    def copy(self, ds):
        p = self.p
        to = (p.s + ds) % 8
        return remote(self.src.at[to], self.dst.at[p.s], self.sems, ds, (p.w, to))

    def own(self):
        return pltpu.make_async_copy(self.src.at[self.p.s], self.dst.at[self.p.s], self.sems[1].at[0])

    def start(self):
        for ds in (6, 5, 3, 7, 4, 2, 1):
            self.copy(ds).start()
        self.own().start()

    def wait(self):
        p = self.p
        self.own().wait()
        for ds in range(1, 8):
            back = (p.s + 8 - ds) % 8
            remote(self.src.at[back], self.dst.at[back], self.sems, ds, (p.w, back)).wait_recv()

    def drain(self):
        for ds in range(1, 8):
            self.copy(ds).wait_send()


def norm_stats(values):
    centre = values - jnp.mean(values, axis=-1, keepdims=True)
    rstd = lax.rsqrt(jnp.mean(centre * centre, axis=-1, keepdims=True) + ln_eps)
    return centre * rstd, rstd


def norm_back(grad, hat, rstd, gain):
    scaled = grad * gain
    return rstd * (
        scaled - jnp.mean(scaled, axis=-1, keepdims=True) - hat * jnp.mean(scaled * hat, axis=-1, keepdims=True)
    )


def rows_of(ref, index, rows):
    value = ref[index]
    return value.reshape(rows, value.shape[-1])


def turned(value):
    return jnp.transpose(value.astype(F32)).astype(BF16)


class Space(NamedTuple):
    gn: Any
    gq: Any
    go: Any
    gu: Any
    gd: Any
    rn: Any
    sn: Any
    sq: Any
    sr: Any
    so: Any
    su: Any
    sd: Any
    sp: Any
    gather_sems: Any
    scatter_sems: Any
    exchange_sems: Any
    sum_sems: Any
    count_out: Any
    counts: Any
    bias: Any
    sb: Any
    rb: Any
    qh: Any
    kh: Any
    vh: Any
    prob: Any
    ab: Any
    at: Any
    gor: Any
    gb: Any
    att: Any
    wout: Any
    turned: Any
    turned_b: Any
    gains: Any
    hat_a: Any
    hat_b: Any
    rstd_a: Any
    rstd_b: Any
    h: Any
    wide: Any
    y: Any
    gy: Any
    back: Any
    mid_grad: Any
    gk: Any
    gv: Any
    square: Any
    squares: Any


def scratch():
    def scatter(*block, kind=BF16):
        return tuple(pltpu.VMEM((*lead, *block), kind) for lead in ((4, 4), (2, 4), (4,), (3,)))

    def sems(count):
        return (pltpu.SemaphoreType.DMA((count,)),) * 2

    half = (96, 384)
    rows, wide = (256, 768), (8, 64, 1152)
    return Space(
        gn=pltpu.VMEM((4, 4, 2, 8, 128), F32),
        gq=pltpu.VMEM((4, 4, 2, 96, 576), BF16),
        go=pltpu.VMEM((4, 4, 2, 48, 384), BF16),
        gu=pltpu.VMEM((4, 4, 2, 96, 768), BF16),
        gd=pltpu.VMEM((4, 2, 4, 192, 384), BF16),
        rn=pltpu.VMEM((4, 4, 2, 8, 128), F32),
        sn=scatter(8, 128, kind=F32),
        sq=scatter(48, 576),
        sr=scatter(48, 576),
        so=scatter(48, 384),
        su=scatter(96, 768),
        sd=scatter(*half),
        sp=tuple(pltpu.VMEM((*lead, *half), BF16) for lead in ((4, 4), (3, 4), (2,), ())),
        gather_sems=tuple(sems(10) for _ in range(7)),
        scatter_sems=tuple(sems(10) for _ in range(7)),
        exchange_sems=tuple(sems(8) for _ in range(5)),
        sum_sems=sems(32),
        count_out=pltpu.VMEM((8, 8, 128), F32),
        counts=pltpu.VMEM((8, 8, 128), F32),
        bias=pltpu.VMEM((3, 4, 4, 1024), F32),
        sb=pltpu.VMEM(wide, BF16),
        rb=pltpu.VMEM(wide, BF16),
        qh=pltpu.VMEM((3, 1024, 64), BF16),
        kh=pltpu.VMEM((3, 1024, 64), BF16),
        vh=pltpu.VMEM((3, 1024, 64), BF16),
        prob=pltpu.VMEM((3, 1024, 1024), BF16),
        ab=pltpu.VMEM((8, 64, 384), BF16),
        at=pltpu.VMEM((8, 64, 384), BF16),
        gor=pltpu.VMEM((8, 64, 384), BF16),
        gb=pltpu.VMEM(wide, BF16),
        att=pltpu.VMEM(rows, BF16),
        wout=pltpu.VMEM((4, 2, 2, 48, 768), BF16),
        turned=pltpu.VMEM((768, 256), BF16),
        turned_b=pltpu.VMEM((768, 256), BF16),
        gains=pltpu.VMEM((32, 768), F32),
        hat_a=pltpu.VMEM(rows, F32),
        hat_b=pltpu.VMEM(rows, F32),
        rstd_a=pltpu.VMEM((256, 1), F32),
        rstd_b=pltpu.VMEM((256, 1), F32),
        h=pltpu.VMEM(rows, BF16),
        wide=pltpu.VMEM((256, 2304), BF16),
        y=pltpu.VMEM(rows, F32),
        gy=pltpu.VMEM(rows, BF16),
        back=pltpu.VMEM(rows, F32),
        mid_grad=pltpu.VMEM(rows, F32),
        gk=pltpu.VMEM((64, 1024), F32),
        gv=pltpu.VMEM((64, 1024), F32),
        square=pltpu.VMEM((8, 128), F32),
        squares=pltpu.VMEM((32, 8, 128), F32),
    )


def kernel(tree, live, rand_ids, x, d_out, w_qkv, w_out, w_up, w_down, norm, output, d_input, red_q, red_o, red_u, red_d, red_n, total, *rest):
    r = jax.tree.unflatten(tree, rest)
    p = Place()
    barrier = pltpu.get_barrier_semaphore()

    def greet(k, _):
        to = ((p.w + k // 8) % 4, (p.s + k % 8) % 8)
        pl.semaphore_signal(barrier, inc=1, device_id=to, device_id_type=MESH)
        return 0

    lax.fori_loop(1, 32, greet, 0)

    all_n, all_q, all_r = Blocks(r.gn), Blocks(r.gq, count=48), Blocks(r.gq, start=48, count=48)
    all_o, all_u = Blocks(r.go), Blocks(r.gu)
    all_d, all_p = Blocks(r.gd, True, count=96), Blocks(r.gd, True, start=96, count=96)
    gathers = [Gather(p, b, m) for b, m in zip((all_n, all_q, all_r, all_o, all_u, all_d), r.gather_sems)]
    gather_n, gather_q, gather_r, gather_o, gather_u, gather_d = gathers
    gather_p = PlaneGather(p, all_p, r.gather_sems[6])
    scatters = [
        Scatter(p, b, space, m)
        for b, space, m in zip(
            (Blocks(r.rn), all_q, all_r, all_o, all_u, all_d), (r.sn, r.sq, r.sr, r.so, r.su, r.sd), r.scatter_sems
        )
    ]
    scatter_n, scatter_q, scatter_r, scatter_o, scatter_u, scatter_d = scatters
    scatter_p = PlaneScatter(p, all_p, r.sp, r.scatter_sems[6])
    count_x = Exchange(p, r.count_out, r.counts, r.exchange_sems[0])
    qkv_x = Exchange(p, r.sb, r.rb, r.exchange_sems[1])
    att_x = Exchange(p, r.ab, r.at, r.exchange_sems[2])
    gro_x = Exchange(p, r.ab, r.gor, r.exchange_sems[3])
    gqkv_x = Exchange(p, r.sb, r.gb, r.exchange_sems[4])
    chip, core = p.s // 2, p.c

    r.gn[p.w, chip, core] = jnp.zeros((8, 128), F32)
    r.gn[p.w, chip, core, 0:1, 0:96] = norm[...].astype(BF16).astype(F32)
    r.gq[p.w, chip, core] = w_qkv[...].astype(BF16)
    r.gd[chip, core, p.w] = w_down[...].astype(BF16)
    pl.semaphore_wait(barrier, 31)
    gather_n.z_send()
    gather_q.z_send()
    gather_r.z_send()
    gather_p.stage1()
    for k in range(2):
        r.go[p.w, chip, core, :, 192 * k : 192 * k + 192] = w_out[48 * k : 48 * k + 48].astype(BF16)
    gather_o.z_send()

    lane = lax.broadcasted_iota(jnp.int32, (8, 128), 1)
    sub = lax.broadcasted_iota(jnp.int32, (8, 128), 0)
    here = 2 * p.s + sub % 2
    fixed = (jnp.abs(lane - here) <= 1).astype(F32) + (lane == 0).astype(F32) + (lane == 15).astype(F32)
    for v in range(2):
        for group in range(4):
            counts = fixed
            for row in range(6):
                head = 3 * group + row // 2
                for k in range(3):
                    drawn = rand_ids[v * 12 + head, 2 * k + row % 2]
                    counts = counts + ((sub == row) & (lane == drawn)).astype(F32)
            r.count_out[4 * v + group] = counts
    count_x.start()
    r.gu[p.w, chip, core] = w_up[...].astype(BF16)
    gather_u.z_send()
    gather_d.z_send()

    hat, rstd = norm_stats(x[...].astype(F32))
    r.hat_a[...] = hat
    r.rstd_a[...] = rstd
    gather_n.stage1()
    gather_p.stage2()
    gather_q.stage1()

    count_x.wait()
    spread = (
        lax.broadcasted_iota(jnp.int32, (128, 1024), 1) // 64 == lax.broadcasted_iota(jnp.int32, (128, 1024), 0)
    ).astype(BF16)
    wide = dot(r.counts[...].reshape(64, 128).astype(BF16), spread)
    wide = jnp.where(wide > 0.5, jnp.log(jnp.maximum(wide, 1.0)), NEG)
    for src in range(8):
        for head in range(3):
            row = src * 8 + head * 2
            at = 2 * (src % 2)
            r.bias[head, src // 2, at : at + 2] = wide[row : row + 2]

    gather_n.stage2()
    gather_r.stage1()
    gather_q.stage2()
    gather_n.stage3()
    gather_n.finish()
    lane = lax.broadcasted_iota(jnp.int32, (128, 768), 1)
    sub = lax.broadcasted_iota(jnp.int32, (128, 768), 0)
    gains = jnp.zeros((32, 768), F32)
    for s in range(8):
        place = ((lane == sub + 96 * s) & (sub < 96)).astype(BF16)
        gains = gains + dot(r.gn[:, s // 2, s % 2].reshape(32, 128).astype(BF16), place)
    r.gains[...] = gains
    r.h[...] = (r.hat_a[...] * r.gains[0:1] + r.gains[8:9]).astype(BF16)
    gather_r.stage2()
    gather_o.stage1()
    gather_q.stage3()
    gather_r.stage3()
    gather_q.finish()
    gather_r.finish()

    for w in range(4):
        part = dot(r.h[...], rows_of(r.gq, w, 768)).astype(BF16)
        for k in range(3):
            kind, group = divmod(3 * w + k, 4)
            for v in range(2):
                for j in range(2):
                    row, at = 128 * v + 64 * j, 576 * j + 192 * kind
                    r.sb[4 * v + group, :, at : at + 192] = part[row : row + 64, 192 * k : 192 * k + 192]
    qkv_x.start()
    gather_u.stage1()
    gather_p.stage3()
    gather_o.stage2()
    gather_o.stage3()
    gather_d.stage1()
    qkv_x.wait()
    for src in range(8):
        for head in range(3):
            for kind, ref in enumerate((r.qh, r.kh, r.vh)):
                for j in range(2):
                    row, at = 128 * src + 64 * j, 576 * j + 192 * kind + 64 * head
                    ref[head, row : row + 64] = r.rb[src, :, at : at + 64]

    for head in range(3):

        def attend(c, _, head=head):
            q0 = pl.multiple_of(c * 256, 256)
            raw = dot_nt(r.qh[head, pl.ds(q0, 256)], r.kh[head]) * (1.0 / math.sqrt(HD))
            score = (raw.reshape(4, 64, 1024) + r.bias[head, c][:, None, :]).reshape(256, 1024)
            prob = jnp.exp(score - jnp.max(score, axis=-1, keepdims=True))
            prob = (prob * (1.0 / jnp.sum(prob, axis=-1, keepdims=True))).astype(BF16)
            r.prob[head, pl.ds(q0, 256)] = prob
            got = dot(prob, r.vh[head]).astype(BF16).reshape(2, 2, 64, 64)
            for j in range(2):
                at = 192 * j + 64 * head
                r.ab[pl.ds(2 * c, 2), :, at : at + 64] = got[:, j]
            return 0

        lax.fori_loop(0, 4, attend, 0)
        if head == 0:
            gather_u.stage2()
        if head == 1:
            gather_d.stage2()
    att_x.start()
    gather_u.stage3()
    gather_d.stage3()
    gather_o.finish()
    for w in range(4):
        for k in range(2):
            r.wout[:, :, k, :, 192 * w : 192 * w + 192] = r.go[w, :, :, :, 192 * k : 192 * k + 192]
    for v in range(2):
        rows = pl.ds(128 * v, 128)
        r.gy[rows] = (d_out[rows].astype(F32) * live[v].astype(F32)).astype(BF16)
    r.turned[...] = turned(r.gy[...])
    att_x.wait()
    for v in range(2):
        for group in range(4):
            for j in range(2):
                row = 128 * v + 64 * j
                r.att[row : row + 64, 192 * group : 192 * group + 192] = r.at[4 * v + group, :, 192 * j : 192 * j + 192]
    mid = x[...].astype(F32) + dot(r.att[...], r.wout[...].reshape(768, 768))
    r.y[...] = mid
    hat, rstd = norm_stats(mid)
    r.hat_b[...] = hat
    r.rstd_b[...] = rstd
    hidden = hat * r.gains[16:17] + r.gains[24:25]
    r.h[...] = hidden.astype(BF16)
    r.turned_b[...] = turned(hidden)
    r.back[...] = jnp.zeros((256, 768), F32)
    gather_p.stage4()
    gather_u.finish()
    gather_d.finish()
    gather_p.finish()
    for g in (*gathers, gather_p):
        g.drain()

    def feed(f, _):
        w_up_f = rows_of(r.gu, f, 768)
        up = dot(r.h[...], w_up_f)
        square = up * up
        bend = jnp.tanh(GELU_C * (up + 0.044715 * up * square))
        act = (0.5 * up * (1.0 + bend)).astype(BF16)
        slope = 0.5 * (1.0 + bend) + 0.5 * up * (1.0 - bend * bend) * (GELU_C * (1.0 + 0.134145 * square))
        grads = []
        for k in range(2):
            w_down_f = rows_of(r.gd, (f, k), 768)
            act_k = act[:, 384 * k : 384 * k + 384]
            r.y[...] += dot_nt(act_k, w_down_f)
            grads.append((dot(r.gy[...], w_down_f) * slope[:, 384 * k : 384 * k + 384]).astype(BF16))
            r.gd[f, k] = dot(r.turned[...], act_k).astype(BF16).reshape(4, 192, 384)
        grad_up = jnp.concatenate(grads, axis=1)
        r.back[...] += dot_nt(grad_up, w_up_f)
        r.gu[f] = dot(r.turned_b[...], grad_up).astype(BF16).reshape(4, 2, 96, 768)
        return 0

    lax.fori_loop(0, 4, feed, 0)
    scatter_p.stage_c()
    scatter_d.stage_c()
    scatter_u.stage_c()
    output[...] = r.y[...].astype(BF16)

    grad_h = r.back[...]
    r.rn[...] = jnp.zeros((4, 4, 2, 8, 128), F32)

    def put_norm(w, row):
        for s in range(8):
            r.rn[w, s // 2, s % 2, 0:1, 0:96] = row[:, 96 * s : 96 * s + 96]

    put_norm(2, jnp.sum(grad_h * r.hat_b[...], axis=0, keepdims=True))
    put_norm(3, jnp.sum(grad_h, axis=0, keepdims=True))
    mid_grad = norm_back(grad_h, r.hat_b[...], r.rstd_b[...], r.gains[16:17])
    for v in range(2):
        rows = slice(128 * v, 128 * v + 128)
        r.mid_grad[rows] = mid_grad[rows] + d_out[rows].astype(F32) * live[v].astype(F32)
    r.h[...] = r.mid_grad[...].astype(BF16)
    att_x.drain()
    grad_o = dot_nt(r.h[...], r.wout[...].reshape(768, 768)).astype(BF16)
    for v in range(2):
        for group in range(4):
            for j in range(2):
                row = 128 * v + 64 * j
                r.ab[4 * v + group, :, 192 * j : 192 * j + 192] = grad_o[row : row + 64, 192 * group : 192 * group + 192]
    gro_x.start()
    scatter_p.stage_z()
    scatter_d.stage_d()
    scatter_u.stage_d()
    r.turned[...] = turned(r.att[...])
    for w in range(4):
        raw = dot(r.turned[...], r.h[:, 192 * w : 192 * w + 192]).astype(BF16).reshape(4, 2, 2, 48, 192)
        for k in range(2):
            r.go[w, :, :, :, 192 * k : 192 * k + 192] = raw[:, :, k]
    scatter_o.stage_c()
    qkv_x.drain()
    gro_x.wait()

    for head in range(3):
        r.gk[...] = jnp.zeros((64, 1024), F32)
        r.gv[...] = jnp.zeros((64, 1024), F32)

        def attend_back(c, _, head=head):
            q0 = pl.multiple_of(c * 256, 256)
            halves = []
            for j in range(2):
                at = 192 * j + 64 * head
                halves.append(r.gor[pl.ds(2 * c, 2), :, at : at + 64].reshape(2, 1, 64, 64))
            grad = jnp.concatenate(halves, axis=1).reshape(256, 64)
            prob = r.prob[head, pl.ds(q0, 256)]
            grad_p = dot_nt(grad, r.vh[head])
            prob_f = prob.astype(F32)
            inner = jnp.sum(prob_f * grad_p, axis=-1, keepdims=True)
            grad_s = (prob_f * (grad_p - inner)).astype(BF16)
            grad_q = (dot(grad_s, r.kh[head]) * (1.0 / math.sqrt(HD))).astype(BF16).reshape(2, 2, 64, 64)
            for j in range(2):
                at = 576 * j + 64 * head
                r.sb[pl.ds(2 * c, 2), :, at : at + 64] = grad_q[:, j]
            r.gk[...] += dot_tn(r.qh[head, pl.ds(q0, 256)], grad_s)
            r.gv[...] += dot_tn(grad, prob)
            return 0

        lax.fori_loop(0, 4, attend_back, 0)
        for kind, grad in ((1, r.gk[...] * (1.0 / math.sqrt(HD))), (2, r.gv[...])):
            grad = jnp.transpose(grad).astype(BF16).reshape(8, 2, 64, 64)
            for j in range(2):
                at = 576 * j + 192 * kind + 64 * head
                r.sb[:, :, at : at + 64] = grad[:, j]
        if head == 0:
            scatter_d.stage_e()
        if head == 1:
            scatter_u.stage_e()
    gqkv_x.start()
    scatter_o.stage_d()
    scatter_p.stage_d()
    scatter_d.stage_f()
    scatter_u.stage_f()
    hidden = r.hat_a[...] * r.gains[0:1] + r.gains[8:9]
    r.turned[...] = turned(hidden)
    r.back[...] = jnp.zeros((256, 768), F32)
    gqkv_x.wait()
    for v in range(2):
        for group in range(4):
            for kind in range(3):
                for j in range(2):
                    row, at = 128 * v + 64 * j, 576 * j + 192 * kind
                    to = 768 * kind + 192 * group
                    r.wide[row : row + 64, to : to + 192] = r.gb[4 * v + group, :, at : at + 192]
    for w in range(4):
        grad = r.wide[:, 576 * w : 576 * w + 576]
        r.back[...] += dot_nt(grad, rows_of(r.gq, w, 768))
        r.gq[w] = dot(r.turned[...], grad).astype(BF16).reshape(4, 2, 96, 576)
    scatter_q.stage_c()
    scatter_r.stage_c()
    grad_h = r.back[...]
    put_norm(0, jnp.sum(grad_h * r.hat_a[...], axis=0, keepdims=True))
    put_norm(1, jnp.sum(grad_h, axis=0, keepdims=True))
    scatter_n.stage_c()
    scatter_q.stage_d()
    scatter_r.stage_d()
    scatter_n.stage_d()
    scatter_o.stage_e()
    scatter_p.stage_e()
    d_input[...] = r.mid_grad[...] + norm_back(grad_h, r.hat_a[...], r.rstd_a[...], r.gains[0:1])
    red_d[0:96] = scatter_d.finish()
    red_u[...] = scatter_u.finish()
    red_d[96:192] = scatter_p.finish()
    scatter_o.stage_f()
    scatter_q.stage_e()
    scatter_n.stage_e()
    scatter_r.stage_e()
    scatter_q.stage_f()
    scatter_n.stage_f()
    scatter_r.stage_f()
    red_o[...] = scatter_o.finish()
    red_q[0:48] = scatter_q.finish()
    red_n[...] = scatter_n.finish()
    red_q[48:96] = scatter_r.finish()
    local = jnp.zeros((8, 128), F32)
    for ref in (red_q, red_o, red_u, red_d, red_n):
        local = local + jnp.sum(ref[...] * ref[...])
    r.square[...] = local
    r.squares[0] = local

    def share(k):
        to = ((p.w + k // 8) % 4, (p.s + k % 8) % 8)
        return remote(r.square, r.squares.at[k], r.sum_sems, k, to)

    def share_start(k, _):
        share(k).start()
        return 0

    def share_wait(k, _):
        share(k).wait()
        return 0

    lax.fori_loop(1, 32, share_start, 0)
    for part in (count_x, gro_x, gqkv_x, *scatters, scatter_p):
        part.drain()
    lax.fori_loop(1, 32, share_wait, 0)
    total[...] = jnp.sum(r.squares[...], axis=0)


def adam_kernel(*refs):
    passed, state, outs = refs[0:2], refs[2:23], refs[23:46]
    here, sems = refs[46:67], refs[67]
    through = [pltpu.make_async_copy(a, b, sems.at[21 + k]) for k, (a, b) in enumerate(zip(passed, outs[21:23]))]
    loads = [pltpu.make_async_copy(a, b, sems.at[k]) for k, (a, b) in enumerate(zip(state, here))]
    for copy in (*loads, *through):
        copy.start()
    fix_one = 1.0 - beta_one**STEP
    fix_two = 1.0 - beta_two**STEP
    rates = (rate_matrix, rate_output, rate_matrix, rate_matrix, rate_norm)
    loads[20].wait()
    norm = jnp.sqrt(here[20][0:1, 0:1])
    factor = 1.0 / jnp.maximum(norm, 1.0)
    outs[20][...] = norm
    for k in range(5):
        for part in range(4):
            loads[5 * part + k].wait()
        raw = here[k][...]
        if k == 1:
            raw = jnp.concatenate([raw[:, 0:192], raw[:, 192:384]], axis=0)
        if k == 4:
            raw = raw[0:1, 0:96]
        grad = raw * factor
        weight = here[5 + k][...]
        first = beta_one * here[10 + k][...] + (1.0 - beta_one) * grad
        second = beta_two * here[15 + k][...] + (1.0 - beta_two) * grad * grad
        stride = first / fix_one / (jnp.sqrt(second / fix_two) + adam_eps)
        decay = 0.0 if k == 4 else decay_rate
        outs[k][...] = grad
        outs[5 + k][...] = weight - rates[k] * (stride + decay * weight)
        outs[10 + k][...] = first
        outs[15 + k][...] = second
    for copy in through:
        copy.wait()


def fused_device(
    layer_input, d_out, rand_ids, live_mask, w_qkv, w_out, w_up, w_down, norm_params,
    m_qkv, m_out, m_up, m_down, m_norm, v_qkv, v_out, v_up, v_down, v_norm,
):
    vmem, smem, anywhere = (pl.BlockSpec(memory_space=kind) for kind in (pltpu.VMEM, pltpu.SMEM, pl.ANY))
    ids = rand_ids.transpose(0, 2, 3, 1).reshape(24, 6)
    leaves, tree = jax.tree.flatten(scratch())
    reduced = [(96, 576), (48, 384), (96, 768), (192, 384), (8, 128), (8, 128)]
    shape = jax.ShapeDtypeStruct
    output, d_input, *grads, total = pl.pallas_call(
        functools.partial(kernel, tree),
        out_shape=[shape((256, 768), BF16), shape((256, 768), F32)] + [shape(dims, F32) for dims in reduced],
        in_specs=[smem, smem] + [vmem] * 7,
        out_specs=[vmem] * 8,
        scratch_shapes=leaves,
        compiler_params=pltpu.CompilerParams(collective_id=0, has_side_effects=True, vmem_limit_bytes=VMEM_LIMIT),
    )(
        live_mask, ids, layer_input.reshape(256, 768), d_out.reshape(256, 768), w_qkv, w_out, w_up, w_down.T,
        norm_params.reshape(1, 96),
    )
    state = (
        *grads,
        w_qkv, w_out, w_up, w_down.T, norm_params.reshape(1, 96),
        m_qkv, m_out, m_up, m_down.T, m_norm.reshape(1, 96),
        v_qkv, v_out, v_up, v_down.T, v_norm.reshape(1, 96),
        total,
    )
    made = pl.pallas_call(
        adam_kernel,
        out_shape=[shape(w.shape, F32) for w in state[5:10]] * 4
        + [shape((1, 1), F32), shape(output.shape, BF16), shape(d_input.shape, F32)],
        in_specs=[anywhere] * 23,
        out_specs=[vmem] * 23,
        scratch_shapes=[pltpu.VMEM(a.shape, F32) for a in state] + [pltpu.SemaphoreType.DMA((23,))],
        compiler_params=pltpu.CompilerParams(vmem_limit_bytes=VMEM_LIMIT),
    )(output, d_input, *state)
    updated = [m.T if k % 5 == 3 else m.reshape(-1) if k % 5 == 4 else m for k, m in enumerate(made[:20])]
    return (made[21].reshape(2, 128, 768), made[22].reshape(2, 128, 768), *updated, made[20].reshape(1))


def solution(mesh):
    placed = (
        P("win", "seq", None),
        P("win", "seq", None),
        P("win", "seq", None, None),
        P("win"),
        P("seq", "win"),
        P("seq", "win"),
        P("seq", "win"),
        P("seq", "win"),
        P(("win", "seq")),
        P("seq", "win"),
        P("seq", "win"),
        P("seq", "win"),
        P("seq", "win"),
        P(("win", "seq")),
        P("seq", "win"),
        P("seq", "win"),
        P("seq", "win"),
        P("seq", "win"),
        P(("win", "seq")),
    )
    fused = mesh.shape["win"] == 4 and mesh.shape["seq"] == 8
    return jax.shard_map(
        fused_device if fused else per_device,
        mesh=mesh,
        in_specs=placed,
        out_specs=(
            P("win", "seq", None),
            P("win", "seq", None),
            P("seq", "win"),
            P("seq", "win"),
            P("seq", "win"),
            P("seq", "win"),
            P(("win", "seq")),
            P("seq", "win"),
            P("seq", "win"),
            P("seq", "win"),
            P("seq", "win"),
            P(("win", "seq")),
            P("seq", "win"),
            P("seq", "win"),
            P("seq", "win"),
            P("seq", "win"),
            P(("win", "seq")),
            P("seq", "win"),
            P("seq", "win"),
            P("seq", "win"),
            P("seq", "win"),
            P(("win", "seq")),
            P(),
        ),
        check_vma=False,
    )
```

```python
import functools
import math
from typing import Any, NamedTuple

import jax
import jax.numpy as jnp
from jax import lax
from jax.experimental import pallas as pl
from jax.experimental.pallas import tpu as pltpu
from jax.sharding import PartitionSpec as P

H = 12
HD = 64
BLK = 64
STEP = 3


NEG = -1e30
ln_eps = 1e-05
beta_one = 0.5
beta_two = 0.5
adam_eps = 1e-08
decay_rate = 0.1
rate_matrix = 0.04
rate_output = 0.16
rate_norm = 0.6
VMEM_LIMIT = 63 << 20


def layer_norm(values, gain, shift):
    centre = values - jnp.mean(values, axis=-1, keepdims=True)
    spread = jnp.mean(centre * centre, axis=-1, keepdims=True)
    return centre * lax.rsqrt(spread + ln_eps) * gain + shift


def slot_counts(rand_ids, first_block, block_count):
    blocks_dev = rand_ids.shape[1]
    here = (first_block + jnp.arange(blocks_dev, dtype=jnp.int32))[:, None]
    every = jnp.arange(block_count, dtype=jnp.int32)[None, :]
    near = (jnp.abs(here - every) <= 1).astype(jnp.float32)
    ends = (every == 0).astype(jnp.float32) + (every == block_count - 1).astype(jnp.float32)
    drawn = jnp.sum((rand_ids[..., None] == every[0]).astype(jnp.float32), axis=3)
    return (near + ends)[None, :, None, :] + drawn


def adam_update(weight, grad, first, second, rate, decay, fix_one, fix_two):
    first_new = beta_one * first + (1.0 - beta_one) * grad
    second_new = beta_two * second + (1.0 - beta_two) * grad * grad
    stride = first_new / fix_one / (jnp.sqrt(second_new / fix_two) + adam_eps)
    return (weight - rate * (stride + decay * weight), first_new, second_new)


def per_device(
    layer_input,
    d_out,
    rand_ids,
    live_mask,
    w_qkv,
    w_out,
    w_up,
    w_down,
    norm_params,
    m_qkv,
    m_out,
    m_up,
    m_down,
    m_norm,
    v_qkv,
    v_out,
    v_up,
    v_down,
    v_norm,
):
    wins, local_len, width = layer_input.shape
    blocks_dev = local_len // BLK
    block_count = blocks_dev * lax.axis_size("seq")
    first_block = lax.axis_index("seq") * blocks_dev
    inv_root = 1.0 / math.sqrt(HD)
    rows = wins * local_len
    low_qkv = w_qkv.astype(jnp.bfloat16)
    low_out = w_out.astype(jnp.bfloat16)
    low_up = w_up.astype(jnp.bfloat16)
    low_down = w_down.astype(jnp.bfloat16)
    low_norm = norm_params.astype(jnp.bfloat16)
    full_qkv, full_out, full_up, full_down = (
        lax.all_gather(lax.all_gather(low, "win", axis=1, tiled=True), "seq", axis=0, tiled=True)
        for low in (low_qkv, low_out, low_up, low_down)
    )
    full_norm = lax.all_gather(low_norm, ("win", "seq"), axis=0, tiled=True)
    gains = full_norm.astype(jnp.float32).reshape(4, width)
    loss_weight = live_mask.astype(jnp.float32)
    counts = slot_counts(rand_ids, first_block, block_count)
    bias = jnp.where(counts > 0, jnp.log(jnp.maximum(counts, 1.0)), NEG)
    bias = jnp.repeat(bias, BLK, axis=3)[:, :, :, None, :]
    tokens = layer_input.astype(jnp.float32).reshape(rows, width)
    h_one = layer_norm(tokens, gains[0], gains[1]).astype(jnp.bfloat16)
    qkv = jnp.dot(h_one, full_qkv, preferred_element_type=jnp.float32)
    q_heads = qkv[:, :width].astype(jnp.bfloat16).reshape(wins, blocks_dev, BLK, H, HD)
    keyval = qkv[:, width:].astype(jnp.bfloat16).reshape(wins, local_len, 2 * width)
    window = lax.all_gather(keyval, "seq", axis=1, tiled=True)
    shaped = window.reshape(wins, block_count * BLK, 2, H, HD)
    keys, values = shaped[:, :, 0], shaped[:, :, 1]
    scores = (
        jnp.einsum("wbqhd,wkhd->wbhqk", q_heads, keys, preferred_element_type=jnp.float32)
        * inv_root
        + bias
    )
    top = jnp.max(scores, axis=-1, keepdims=True)
    log_total = top + jnp.log(jnp.sum(jnp.exp(scores - top), axis=-1, keepdims=True))
    prob = jnp.exp(scores - log_total).astype(jnp.bfloat16)
    heads_out = jnp.einsum("wbhqk,wkhd->wbqhd", prob, values, preferred_element_type=jnp.float32)
    attended = heads_out.astype(jnp.bfloat16).reshape(rows, width)
    middle = tokens + jnp.dot(attended, full_out, preferred_element_type=jnp.float32)
    h_two = layer_norm(middle, gains[2], gains[3]).astype(jnp.bfloat16)
    up_proj = jnp.dot(h_two, full_up, preferred_element_type=jnp.float32)
    active = jax.nn.gelu(up_proj).astype(jnp.bfloat16)
    result = middle + jnp.dot(active, full_down, preferred_element_type=jnp.float32)
    output = result.astype(jnp.bfloat16).reshape(wins, local_len, width)
    grad_y = (d_out.astype(jnp.float32) * loss_weight[:, None, None]).reshape(rows, width)
    grad_ffn = grad_y.astype(jnp.bfloat16)
    raw_down = jnp.einsum("tf,td->fd", active, grad_ffn, preferred_element_type=jnp.float32)
    grad_act = jnp.einsum("td,fd->tf", grad_ffn, full_down, preferred_element_type=jnp.float32)
    gelu_pull = jax.vjp(jax.nn.gelu, up_proj)[1]
    grad_up = gelu_pull(grad_act)[0].astype(jnp.bfloat16)
    raw_up = jnp.einsum("td,tf->df", h_two, grad_up, preferred_element_type=jnp.float32)
    grad_h_two = jnp.einsum("tf,df->td", grad_up, full_up, preferred_element_type=jnp.float32)
    norm_pull = jax.vjp(layer_norm, middle, gains[2], gains[3])[1]
    grad_mid_ln, raw_gain_two, raw_shift_two = norm_pull(grad_h_two)
    grad_mid = grad_y + grad_mid_ln
    grad_att = grad_mid.astype(jnp.bfloat16)
    raw_out = jnp.einsum("td,te->de", attended, grad_att, preferred_element_type=jnp.float32)
    grad_o = jnp.einsum("te,de->td", grad_att, full_out, preferred_element_type=jnp.float32)
    grad_o = grad_o.astype(jnp.bfloat16).reshape(wins, blocks_dev, BLK, H, HD)
    grad_p = jnp.einsum("wbqhd,wkhd->wbhqk", grad_o, values, preferred_element_type=jnp.float32)
    prob_f = prob.astype(jnp.float32)
    inner = jnp.sum(prob_f * grad_p, axis=-1, keepdims=True)
    grad_s = (prob_f * (grad_p - inner)).astype(jnp.bfloat16)
    grad_q = (
        jnp.einsum("wbhqk,wkhd->wbqhd", grad_s, keys, preferred_element_type=jnp.float32)
        * inv_root
    )
    grad_v = jnp.einsum("wbhqk,wbqhd->wkhd", prob, grad_o, preferred_element_type=jnp.float32)
    grad_k = (
        jnp.einsum("wbhqk,wbqhd->wkhd", grad_s, q_heads, preferred_element_type=jnp.float32)
        * inv_root
    )
    grad_kv = jnp.stack([grad_k, grad_v], axis=2).astype(jnp.bfloat16)
    grad_kv = lax.psum_scatter(
        grad_kv.reshape(wins, block_count * BLK, 2 * width),
        "seq",
        scatter_dimension=1,
        tiled=True,
    ).reshape(rows, 2 * width)
    grad_qkv = jnp.concatenate(
        [grad_q.reshape(rows, width).astype(jnp.bfloat16), grad_kv], axis=1
    )
    raw_qkv = jnp.einsum("td,te->de", h_one, grad_qkv, preferred_element_type=jnp.float32)
    grad_h_one = jnp.einsum("te,de->td", grad_qkv, full_qkv, preferred_element_type=jnp.float32)
    first_pull = jax.vjp(layer_norm, tokens, gains[0], gains[1])[1]
    grad_tok_ln, raw_gain_one, raw_shift_one = first_pull(grad_h_one)
    d_input = (grad_mid + grad_tok_ln).reshape(wins, local_len, width)
    raw_norm = jnp.concatenate([raw_gain_one, raw_shift_one, raw_gain_two, raw_shift_two])
    red_qkv, red_out, red_up, red_down = (
        lax.psum_scatter(
            lax.psum_scatter(raw.astype(jnp.bfloat16), "seq", scatter_dimension=0, tiled=True),
            "win",
            scatter_dimension=1,
            tiled=True,
        ).astype(jnp.float32)
        for raw in (raw_qkv, raw_out, raw_up, raw_down)
    )
    red_norm = lax.psum_scatter(raw_norm, ("win", "seq"), scatter_dimension=0, tiled=True)
    reduced = (red_qkv, red_out, red_up, red_down, red_norm)
    local_squares = jnp.float32(0.0)
    for grad in reduced:
        local_squares = local_squares + jnp.sum(grad * grad)
    grad_norm = jnp.sqrt(lax.psum(local_squares, ("win", "seq")))
    factor = 1.0 / jnp.maximum(grad_norm, 1.0)
    clipped = tuple((grad * factor for grad in reduced))
    count = jnp.float32(STEP)
    fix_one = 1.0 - jnp.power(jnp.float32(beta_one), count)
    fix_two = 1.0 - jnp.power(jnp.float32(beta_two), count)
    params = (w_qkv, w_out, w_up, w_down, norm_params)
    firsts = (m_qkv, m_out, m_up, m_down, m_norm)
    seconds = (v_qkv, v_out, v_up, v_down, v_norm)
    rates = (rate_matrix, rate_output, rate_matrix, rate_matrix, rate_norm)
    news, moms, secs = ([], [], [])
    for index in range(5):
        decay = 0.0 if index == 4 else decay_rate
        new_w, new_m, new_v = adam_update(
            params[index],
            clipped[index],
            firsts[index],
            seconds[index],
            rates[index],
            decay,
            fix_one,
            fix_two,
        )
        news.append(new_w)
        moms.append(new_m)
        secs.append(new_v)
    return (
        output,
        d_input,
        clipped[0],
        clipped[1],
        clipped[2],
        clipped[3],
        clipped[4],
        news[0],
        news[1],
        news[2],
        news[3],
        news[4],
        moms[0],
        moms[1],
        moms[2],
        moms[3],
        moms[4],
        secs[0],
        secs[1],
        secs[2],
        secs[3],
        secs[4],
        grad_norm.reshape(1),
    )


MESH = pl.DeviceIdType.MESH
F32, BF16 = jnp.float32, jnp.bfloat16
GELU_C = math.sqrt(2.0 / math.pi)
NT = (((1,), (1,)), ((), ()))
TN = (((0,), (0,)), ((), ()))


def dot(a, b):
    return jnp.dot(a, b, preferred_element_type=F32)


def dot_nt(a, b):
    return lax.dot_general(a, b, NT, preferred_element_type=F32)


def dot_tn(a, b):
    return lax.dot_general(a, b, TN, preferred_element_type=F32)


def remote(src, dst, sems, k, dev):
    return pltpu.make_async_remote_copy(
        src_ref=src, dst_ref=dst, send_sem=sems[0].at[k], recv_sem=sems[1].at[k], device_id=dev, device_id_type=MESH
    )


class Place:
    def __init__(self):
        self.w = lax.axis_index("win")
        self.s = s = lax.axis_index("seq")
        self.c = c = s % 2
        x = (s // 2) % 2
        y = s // 4
        dx, dy = 2 - 4 * x, 4 - 8 * y
        self.turn = 1 - 2 * c
        self.n1 = s + (1 - c) * dx + c * dy
        self.n2 = s + (1 - c) * dy + c * dx
        self.nd = s + dx + dy
        self.par = s + self.turn
        self.roles = (s, self.n1, self.n2, self.nd)
        self.par_roles = tuple(r + self.turn for r in (s, self.n2, self.n1, self.nd))
        self.x, self.y = x, y
        self.mate = (self.w + 1 - 2 * (self.w % 2), s)

    def chip(self, k):
        x = self.x + (1 - k % 2) * (1 - 2 * self.x)
        y = self.y + (1 - k // 2) * (1 - 2 * self.y)
        return 2 * y + x

    def role_for_partner(self, chip):
        dx = (chip % 2 - self.x) * (chip % 2 - self.x)
        dy = (chip // 2 - self.y) * (chip // 2 - self.y)
        return self.c * (dx + 2 * dy) + (1 - self.c) * (dy + 2 * dx)


class Blocks:
    def __init__(self, buf, seq_first=False, start=0, count=None):
        self.buf, self.seq_first, self.rows = buf, seq_first, pl.ds(start, buf.shape[3] if count is None else count)

    def block(self, w, s):
        return self.buf.at[(s // 2, s % 2, w, self.rows) if self.seq_first else (w, s // 2, s % 2, self.rows)]

    def read(self, w, s):
        return self.buf[(s // 2, s % 2, w, self.rows) if self.seq_first else (w, s // 2, s % 2, self.rows)]

    def group(self, s):
        every = slice(None)
        return self.buf.at[(s // 2, s % 2, every, self.rows) if self.seq_first else (every, s // 2, s % 2, self.rows)]


class Gather:
    def __init__(self, place, blocks, sems, staged=None):
        self.p, self.b, self.sems, self.staged = place, blocks, sems, staged

    def push(self, s, k, to):
        remote(self.b.group(s), self.b.group(s), self.sems, k, (self.p.w, to)).start()

    def got(self, s, k):
        remote(self.b.group(s), self.b.group(s), self.sems, k, (self.p.w, self.p.par)).wait_recv()

    def along(self, dz, w):
        p, block = self.p, self.b.block(w, self.p.s)
        source = block if self.staged is None else self.staged.at[(p.w + dz) % 2, self.b.rows]
        return remote(source, block, self.sems, dz - 1, ((p.w + dz) % 4, p.s))

    def z_send(self):
        for dz in (1, 2, 3):
            self.along(dz, self.p.w).start()

    def stage1(self):
        p = self.p
        for dz in (1, 2, 3):
            self.along(dz, (p.w + 4 - dz) % 4).wait_recv()
        self.push(p.s, 3, p.n1)
        self.push(p.s, 4, p.n2)
        self.push(p.s, 6, p.par)

    def stage2(self):
        p = self.p
        self.got(p.n1, 3)
        self.push(p.n1, 5, p.n2)
        self.push(p.n1, 7, p.par)

    def stage3(self):
        p = self.p
        self.got(p.n2, 4)
        self.push(p.n2, 8, p.par)
        self.got(p.nd, 5)
        self.push(p.nd, 9, p.par)

    def finish(self):
        for k in range(4):
            self.got(self.p.par_roles[k], 6 + k)

    def drain(self):
        p = self.p
        for dz in (1, 2, 3):
            self.along(dz, p.w).wait_send()
        for k, s in ((3, p.s), (4, p.s), (6, p.s), (5, p.n1), (7, p.n1), (8, p.n2), (9, p.nd)):
            remote(self.b.group(s), self.b.group(s), self.sems, k, (p.w, p.par)).wait_send()


class Scatter:
    def __init__(self, place, blocks, space, sems):
        self.p, self.b, self.sems = place, blocks, sems
        self.c, self.d, self.e, self.f = space

    def copies_c(self):
        p = self.p
        return [remote(self.b.group(p.par_roles[k]), self.c.at[k], self.sems, k, (p.w, p.par)) for k in range(4)]

    def copies_d(self):
        p = self.p
        return [remote(self.c.at[2 + k], self.d.at[k], self.sems, 4 + k, (p.w, p.n2)) for k in range(2)]

    def copy_e(self):
        p = self.p
        return remote(self.c.at[1], self.e, self.sems, 6, (p.w, p.n1))

    def copies_f(self):
        p = self.p
        return [
            remote(self.c.at[0, (p.w + dz) % 4], self.f.at[dz - 1], self.sems, 6 + dz, ((p.w + dz) % 4, p.s))
            for dz in (1, 2, 3)
        ]

    def stage_c(self):
        for copy in self.copies_c():
            copy.start()

    def stage_c_of(self, chip):
        p = self.p
        role = p.role_for_partner(chip)
        remote(self.b.group(2 * chip + 1 - p.c), self.c.at[role], self.sems, role, (p.w, p.par)).start()

    def stage_d(self):
        waits, sends = self.copies_c(), self.copies_d()
        for k in (2, 3, 0, 1):
            waits[k].wait_recv()
            for w in range(4):
                self.c[k, w] = self.c[k, w] + self.b.read(w, self.p.roles[k])
            if k >= 2:
                sends[k - 2].start()

    def stage_e(self):
        waits = self.copies_d()
        for k in (1, 0):
            waits[k].wait_recv()
            for w in range(4):
                self.c[k, w] = self.c[k, w] + self.d[k, w]
            if k == 1:
                self.copy_e().start()

    def stage_f(self):
        self.copy_e().wait_recv()
        for w in range(4):
            self.c[0, w] = self.c[0, w] + self.e[w]
        for copy in self.copies_f():
            copy.start()

    def finish(self):
        total = self.c[0, self.p.w].astype(F32)
        for k, copy in enumerate(self.copies_f()):
            copy.wait_recv()
            total = total + self.f[k].astype(F32)
        return total

    def finish_halves(self):
        p = self.p
        for copy in self.copies_f():
            copy.wait_recv()
        alike = self.c[0, p.w].astype(F32) + self.f[1].astype(F32)
        other = self.f[0].astype(F32) + self.f[2].astype(F32)
        even = p.w % 2 == 0
        return jnp.where(even, alike, other), jnp.where(even, other, alike)

    def drain(self):
        for copy in (*self.copies_c(), *self.copies_d(), self.copy_e(), *self.copies_f()):
            copy.wait_send()


class Exchange:
    def __init__(self, place, src, dst, sems):
        self.p, self.src, self.dst, self.sems = place, src, dst, sems

    def copy(self, ds):
        p = self.p
        to = (p.s + ds) % 8
        return remote(self.src.at[to], self.dst.at[p.s], self.sems, ds, (p.w, to))

    def own(self):
        return pltpu.make_async_copy(self.src.at[self.p.s], self.dst.at[self.p.s], self.sems[1].at[0])

    def start(self):
        for ds in (6, 5, 3, 7, 4, 2, 1):
            self.copy(ds).start()
        self.own().start()

    def wait(self):
        p = self.p
        self.own().wait()
        for ds in range(1, 8):
            back = (p.s + 8 - ds) % 8
            remote(self.src.at[back], self.dst.at[back], self.sems, ds, (p.w, back)).wait_recv()

    def drain(self):
        for ds in range(1, 8):
            self.copy(ds).wait_send()


def norm_stats(values):
    centre = values - jnp.mean(values, axis=-1, keepdims=True)
    rstd = lax.rsqrt(jnp.mean(centre * centre, axis=-1, keepdims=True) + ln_eps)
    return centre * rstd, rstd


def norm_back(grad, hat, rstd, gain):
    scaled = grad * gain
    return rstd * (
        scaled - jnp.mean(scaled, axis=-1, keepdims=True) - hat * jnp.mean(scaled * hat, axis=-1, keepdims=True)
    )


def rows_of(ref, index, rows):
    value = ref[index]
    return value.reshape(rows, value.shape[-1])


def turned(value):
    return jnp.transpose(value.astype(F32)).astype(BF16)


GIVEN = (
    ((256, 768), BF16), ((256, 768), BF16), ((96, 576), F32), ((96, 192), F32), ((96, 768), F32), ((192, 384), F32), ((1, 96), F32),
)
KEPT = (
    ((256, 768), BF16), ((256, 768), F32), ((96, 576), F32), ((48, 384), F32), ((96, 768), F32), ((192, 384), F32), ((8, 128), F32), ((8, 128), F32),
)


class Space(NamedTuple):
    gn: Any
    gq: Any
    go: Any
    gu: Any
    gd: Any
    rn: Any
    sn: Any
    sq: Any
    so: Any
    su: Any
    sd: Any
    half_u: Any
    half_d: Any
    wd: Any
    gather_sems: Any
    scatter_sems: Any
    exchange_sems: Any
    sum_sems: Any
    count_out: Any
    counts: Any
    bias: Any
    sb: Any
    rb: Any
    qh: Any
    kh: Any
    vh: Any
    prob: Any
    ab: Any
    at: Any
    gor: Any
    gb: Any
    att: Any
    wout: Any
    turned: Any
    turned_h: Any
    turned_g: Any
    gains: Any
    hat_a: Any
    hat_b: Any
    rstd_a: Any
    rstd_b: Any
    h: Any
    hb: Any
    hs: Any
    gys: Any
    back_out: Any
    back_in: Any
    y_out: Any
    y_in: Any
    mate_sems: Any
    wide: Any
    y: Any
    back: Any
    mid_grad: Any
    gk: Any
    gv: Any
    act: Any
    slope: Any
    square: Any
    squares: Any
    given: Any
    kept: Any
    io_sems: Any


def scratch():
    def scatter(*block, kind=BF16):
        return tuple(pltpu.VMEM((*lead, *block), kind) for lead in ((4, 4), (2, 4), (4,), (3,)))

    def sems(count):
        return (pltpu.SemaphoreType.DMA((count,)),) * 2

    rows, wide = (256, 768), (3, 8, 64, 384)
    return Space(
        gn=pltpu.VMEM((4, 4, 2, 8, 128), F32),
        gq=pltpu.VMEM((4, 4, 2, 96, 576), BF16),
        go=pltpu.VMEM((4, 4, 2, 48, 384), BF16),
        gu=pltpu.VMEM((4, 4, 2, 96, 384), BF16),
        gd=pltpu.VMEM((4, 2, 4, 96, 384), BF16),
        rn=pltpu.VMEM((4, 4, 2, 8, 128), F32),
        sn=scatter(8, 128, kind=F32),
        sq=tuple(scatter(32, 576) for _ in range(3)),
        so=scatter(48, 384),
        su=tuple(scatter(48, 384) for _ in range(2)),
        sd=tuple(scatter(48, 384) for _ in range(2)),
        half_u=pltpu.VMEM((2, 96, 384), BF16),
        half_d=pltpu.VMEM((2, 96, 384), BF16),
        wd=pltpu.VMEM((4, 4, 2, 96, 384), BF16),
        gather_sems=tuple(sems(10) for _ in range(9)),
        scatter_sems=tuple(sems(10) for _ in range(9)),
        exchange_sems=tuple(sems(8) for _ in range(9)),
        sum_sems=sems(32),
        count_out=pltpu.VMEM((8, 8, 128), F32),
        counts=pltpu.VMEM((8, 8, 128), F32),
        bias=pltpu.VMEM((3, 4, 4, 1024), F32),
        sb=pltpu.VMEM(wide, BF16),
        rb=pltpu.VMEM(wide, BF16),
        qh=pltpu.VMEM((3, 1024, 64), BF16),
        kh=pltpu.VMEM((3, 1024, 64), BF16),
        vh=pltpu.VMEM((3, 1024, 64), BF16),
        prob=pltpu.VMEM((3, 1024, 1024), BF16),
        ab=pltpu.VMEM((8, 64, 384), BF16),
        at=pltpu.VMEM((8, 64, 384), BF16),
        gor=pltpu.VMEM((8, 64, 384), BF16),
        gb=pltpu.VMEM(wide, BF16),
        att=pltpu.VMEM(rows, BF16),
        wout=pltpu.VMEM((4, 2, 2, 48, 768), BF16),
        turned=pltpu.VMEM((768, 256), BF16),
        turned_h=pltpu.VMEM((768, 512), BF16),
        turned_g=pltpu.VMEM((768, 512), BF16),
        gains=pltpu.VMEM((32, 768), F32),
        hat_a=pltpu.VMEM(rows, F32),
        hat_b=pltpu.VMEM(rows, F32),
        rstd_a=pltpu.VMEM((256, 1), F32),
        rstd_b=pltpu.VMEM((256, 1), F32),
        h=pltpu.VMEM(rows, BF16),
        hb=pltpu.VMEM(rows, BF16),
        hs=pltpu.VMEM((2, *rows), BF16),
        gys=pltpu.VMEM((2, *rows), BF16),
        back_out=pltpu.VMEM(rows, BF16),
        back_in=pltpu.VMEM(rows, BF16),
        y_out=pltpu.VMEM(rows, BF16),
        y_in=pltpu.VMEM(rows, BF16),
        mate_sems=sems(4),
        wide=pltpu.VMEM((256, 2304), BF16),
        y=pltpu.VMEM((512, 768), F32),
        back=pltpu.VMEM((512, 768), F32),
        mid_grad=pltpu.VMEM(rows, F32),
        gk=pltpu.VMEM((64, 1024), F32),
        gv=pltpu.VMEM((64, 1024), F32),
        act=pltpu.VMEM((4, 512, 384), BF16),
        slope=pltpu.VMEM((4, 512, 384), BF16),
        square=pltpu.VMEM((8, 128), F32),
        squares=pltpu.VMEM((32, 8, 128), F32),
        given=tuple(pltpu.VMEM(dims, kind) for dims, kind in GIVEN),
        kept=tuple(pltpu.VMEM(dims, kind) for dims, kind in KEPT),
        io_sems=pltpu.SemaphoreType.DMA((15,)),
    )


def kernel(tree, live, rand_ids, *refs):
    r = jax.tree.unflatten(tree, refs[15:])
    x, d_out, w_qkv, w_out, w_up, w_down, norm = r.given
    output, d_input, red_q, red_o, red_u, red_d, red_n, total = r.kept
    loads = [pltpu.make_async_copy(a, b, r.io_sems.at[k]) for k, (a, b) in enumerate(zip(refs[:7], r.given))]
    stores = [pltpu.make_async_copy(a, b, r.io_sems.at[7 + k]) for k, (a, b) in enumerate(zip(r.kept, refs[7:15]))]
    for k in (6, 2, 5, 3, 4, 0, 1):
        loads[k].start()
    p = Place()
    barrier = pltpu.get_barrier_semaphore()

    def greet(k, _):
        to = ((p.w + k // 8) % 4, (p.s + k % 8) % 8)
        pl.semaphore_signal(barrier, inc=1, device_id=to, device_id_type=MESH)
        return 0

    lax.fori_loop(1, 32, greet, 0)

    blocks_q = [Blocks(r.gq, start=32 * k, count=32) for k in range(3)]
    blocks_u = [Blocks(r.gu, start=48 * k, count=48) for k in range(2)]
    blocks_d = [Blocks(r.gd, True, start=48 * k, count=48) for k in range(2)]
    every = (*blocks_q, Blocks(r.go), *blocks_u, *blocks_d)
    staged = (None,) * 4 + (r.half_u,) * 2 + (r.half_d,) * 2
    gathers = [Gather(p, Blocks(r.gn), r.gather_sems[8])]
    gathers += [Gather(p, b, m, half) for b, m, half in zip(every, r.gather_sems, staged)]
    gn, gq0, gq1, gq2, go, gu0, gu1, gd0, gd1 = gathers
    scatters = [Scatter(p, Blocks(r.rn), r.sn, r.scatter_sems[8])]
    scatters += [Scatter(p, b, space, m) for b, space, m in zip(every, (*r.sq, r.so, *r.su, *r.sd), r.scatter_sems)]
    sn, sq0, sq1, sq2, so, su0, su1, sd0, sd1 = scatters
    mate_h = remote(r.hs.at[0], r.hs.at[1], r.mate_sems, 0, p.mate)
    mate_g = remote(r.gys.at[0], r.gys.at[1], r.mate_sems, 1, p.mate)
    mate_back = remote(r.back_out, r.back_in, r.mate_sems, 2, p.mate)
    mate_y = remote(r.y_out, r.y_in, r.mate_sems, 3, p.mate)
    count_x = Exchange(p, r.count_out, r.counts, r.exchange_sems[0])
    att_x = Exchange(p, r.ab, r.at, r.exchange_sems[1])
    gro_x = Exchange(p, r.ab, r.gor, r.exchange_sems[2])
    qkv_x = [Exchange(p, r.sb.at[h], r.rb.at[h], r.exchange_sems[3 + h]) for h in range(3)]
    gqkv_x = [Exchange(p, r.sb.at[h], r.gb.at[h], r.exchange_sems[6 + h]) for h in range(3)]
    chip, core = p.s // 2, p.c

    r.gn[p.w, chip, core] = jnp.zeros((8, 128), F32)
    loads[6].wait()
    r.gn[p.w, chip, core, 0:1, 0:96] = norm[...].astype(BF16).astype(F32)
    loads[2].wait()
    r.gq[p.w, chip, core] = w_qkv[...].astype(BF16)
    pl.semaphore_wait(barrier, 31)
    gq0.z_send()
    gn.z_send()
    gq1.z_send()
    gq2.z_send()
    loads[3].wait()
    for k in range(2):
        r.go[p.w, chip, core, :, 192 * k : 192 * k + 192] = w_out[48 * k : 48 * k + 48].astype(BF16)

    lane = lax.broadcasted_iota(jnp.int32, (8, 128), 1)
    sub = lax.broadcasted_iota(jnp.int32, (8, 128), 0)
    here = 2 * p.s + sub % 2
    fixed = (jnp.abs(lane - here) <= 1).astype(F32) + (lane == 0).astype(F32) + (lane == 15).astype(F32)
    for v in range(2):
        for group in range(4):
            counts = fixed
            for row in range(6):
                head = 3 * group + row // 2
                for k in range(3):
                    drawn = rand_ids[v * 12 + head, 2 * k + row % 2]
                    counts = counts + ((sub == row) & (lane == drawn)).astype(F32)
            r.count_out[4 * v + group] = counts
    count_x.start()
    loads[4].wait()
    loads[5].wait()
    for half in range(2):
        for k in range(2):
            at, row = slice(192 * k, 192 * k + 192), 96 * k
            r.half_u[half, :, at] = w_up[:, 384 * k + 192 * half : 384 * k + 192 * half + 192].astype(BF16)
            r.half_d[half, :, at] = w_down[row : row + 96, 192 * half : 192 * half + 192].astype(BF16)
    r.gu[p.w, chip, core] = r.half_u[p.w % 2]
    r.gd[chip, core, p.w] = r.half_d[p.w % 2]
    gq0.stage1()
    loads[0].wait()
    hat, rstd = norm_stats(x[...].astype(F32))
    r.hat_a[...] = hat
    r.rstd_a[...] = rstd
    loads[1].wait()
    for v in range(2):
        rows = slice(128 * v, 128 * v + 128)
        r.gys[0, rows] = (d_out[rows].astype(F32) * live[v].astype(F32)).astype(BF16)
    gn.stage1()
    gq1.stage1()
    gq0.stage2()
    go.z_send()

    count_x.wait()
    spread = (
        lax.broadcasted_iota(jnp.int32, (128, 1024), 1) // 64 == lax.broadcasted_iota(jnp.int32, (128, 1024), 0)
    ).astype(BF16)
    wide = dot(r.counts[...].reshape(64, 128).astype(BF16), spread)
    wide = jnp.where(wide > 0.5, jnp.log(jnp.maximum(wide, 1.0)), NEG)
    for src in range(8):
        for head in range(3):
            row = src * 8 + head * 2
            at = 2 * (src % 2)
            r.bias[head, src // 2, at : at + 2] = wide[row : row + 2]

    gu0.z_send()
    gq2.stage1()
    gn.stage2()
    gq1.stage2()
    gq0.stage3()
    gn.stage3()
    gq2.stage2()
    gn.finish()
    mate_g.start()
    lane = lax.broadcasted_iota(jnp.int32, (128, 768), 1)
    sub = lax.broadcasted_iota(jnp.int32, (128, 768), 0)
    gains = jnp.zeros((32, 768), F32)
    for s in range(8):
        place = ((lane == sub + 96 * s) & (sub < 96)).astype(BF16)
        gains = gains + dot(r.gn[:, s // 2, s % 2].reshape(32, 128).astype(BF16), place)
    r.gains[...] = gains
    r.h[...] = (r.hat_a[...] * r.gains[0:1] + r.gains[8:9]).astype(BF16)
    go.stage1()
    gq1.stage3()
    gq2.stage3()
    gq0.finish()
    gu0.stage1()
    gd1.z_send()
    gq1.finish()
    gq2.finish()
    go.stage2()

    for w in range(4):
        part = dot(r.h[...], rows_of(r.gq, w, 768)).astype(BF16)
        for k in range(3):
            kind, group = divmod(3 * w + k, 4)
            for v in range(2):
                for j in range(2):
                    for head in range(3):
                        row, at, col = 128 * v + 64 * j, 192 * j + 64 * kind, 192 * k + 64 * head
                        r.sb[head, 4 * v + group, :, at : at + 64] = part[row : row + 64, col : col + 64]
    gu1.z_send()
    qkv_x[0].start()
    go.stage3()
    qkv_x[1].start()
    qkv_x[2].start()

    for head in range(3):
        qkv_x[head].wait()
        for src in range(8):
            for kind, ref in enumerate((r.qh, r.kh, r.vh)):
                for j in range(2):
                    row, at = 128 * src + 64 * j, 192 * j + 64 * kind
                    ref[head, row : row + 64] = r.rb[head, src, :, at : at + 64]

        def attend(c, _, head=head):
            q0 = pl.multiple_of(c * 256, 256)
            raw = dot_nt(r.qh[head, pl.ds(q0, 256)], r.kh[head]) * (1.0 / math.sqrt(HD))
            score = (raw.reshape(4, 64, 1024) + r.bias[head, c][:, None, :]).reshape(256, 1024)
            prob = jnp.exp(score - jnp.max(score, axis=-1, keepdims=True))
            prob = (prob * (1.0 / jnp.sum(prob, axis=-1, keepdims=True))).astype(BF16)
            r.prob[head, pl.ds(q0, 256)] = prob
            got = dot(prob, r.vh[head]).astype(BF16).reshape(2, 2, 64, 64)
            for j in range(2):
                at = 192 * j + 64 * head
                r.ab[pl.ds(2 * c, 2), :, at : at + 64] = got[:, j]
            return 0

        lax.fori_loop(0, 4, attend, 0)
        if head == 0:
            go.finish()
            gd0.z_send()
        if head == 1:
            gu1.stage1()
    att_x.start()
    gu0.stage2()
    gu1.stage2()
    for w in range(4):
        for k in range(2):
            r.wout[:, :, k, :, 192 * w : 192 * w + 192] = r.go[w, :, :, :, 192 * k : 192 * k + 192]
    gd0.stage1()
    mate_g.wait_recv()
    for k in range(2):
        r.turned_g[:, 256 * k : 256 * k + 256] = turned(r.gys[k])
    att_x.wait()
    for v in range(2):
        for group in range(4):
            for j in range(2):
                row = 128 * v + 64 * j
                r.att[row : row + 64, 192 * group : 192 * group + 192] = r.at[4 * v + group, :, 192 * j : 192 * j + 192]
    mid = x[...].astype(F32) + dot(r.att[...], r.wout[...].reshape(768, 768))
    r.y[0:256] = mid
    r.y[256:512] = jnp.zeros((256, 768), F32)
    hat, rstd = norm_stats(mid)
    r.hat_b[...] = hat
    r.rstd_b[...] = rstd
    r.hs[0] = (hat * r.gains[16:17] + r.gains[24:25]).astype(BF16)
    mate_h.start()
    gd0.stage2()
    gu1.stage3()
    gd1.stage1()
    gu0.stage3()
    r.back[...] = jnp.zeros((512, 768), F32)
    r.turned_h[:, 0:256] = turned(r.hs[0])
    gu0.finish()
    gu1.finish()

    for k in range(2):
        if k == 1:
            gd0.stage3()
            gd1.stage2()
            gd0.finish()
            mate_h.wait_recv()
            gd1.stage3()
            r.turned_h[:, 256:512] = turned(r.hs[1])

        def feed_up(f, _, k=k):
            up = dot(r.hs[k], rows_of(r.gu, f, 768))
            square = up * up
            bend = jnp.tanh(GELU_C * (up + 0.044715 * up * square))
            slope = 0.5 * (1.0 + bend) + 0.5 * up * (1.0 - bend * bend) * (GELU_C * (1.0 + 0.134145 * square))
            r.act[f, 256 * k : 256 * k + 256] = (0.5 * up * (1.0 + bend)).astype(BF16)
            r.slope[f, 256 * k : 256 * k + 256] = slope.astype(BF16)
            return 0

        lax.fori_loop(0, 4, feed_up, 0)
    gd1.finish()
    for g in gathers:
        g.drain()

    def unpack(f, _):
        for c in range(2):
            for j in range(2):
                r.wd[f, :, j, :, 192 * c : 192 * c + 192] = r.gd[f, c, :, :, 192 * j : 192 * j + 192]
        return 0

    lax.fori_loop(0, 4, unpack, 0)
    for k in (1, 0):

        def feed_back(f, _, k=k):
            rows = slice(256 * k, 256 * k + 256)
            grad_up = (dot(r.gys[k], rows_of(r.wd, f, 768)) * r.slope[f, rows].astype(F32)).astype(BF16)
            r.slope[f, rows] = grad_up
            r.back[rows] += dot_nt(grad_up, rows_of(r.gu, f, 768))
            return 0

        lax.fori_loop(0, 4, feed_back, 0)
        if k == 1:
            r.back_out[...] = r.back[256:512].astype(BF16)
            mate_back.start()

    def feed_raw(k, _):
        f = p.chip(k)
        act = r.act[f]
        r.y[...] += dot_nt(act, rows_of(r.wd, f, 768))
        raw_down = dot(r.turned_g[...], act).astype(BF16).reshape(4, 2, 96, 384)
        for c in range(2):
            for j in range(2):
                r.gd[f, c, :, :, 192 * j : 192 * j + 192] = raw_down[:, j, :, 192 * c : 192 * c + 192]
        sd0.stage_c_of(f)
        sd1.stage_c_of(f)
        r.gu[f] = dot(r.turned_h[...], r.slope[f]).astype(BF16).reshape(4, 2, 96, 384)
        return 0

    lax.fori_loop(0, 4, feed_raw, 0)
    su0.stage_c()
    sd0.stage_d()
    r.y_out[...] = r.y[256:512].astype(BF16)
    mate_back.wait_recv()
    su0.stage_d()
    sd0.stage_e()

    r.back[0:256] += r.back_in[...].astype(F32)
    mid_grad = norm_back(r.back[0:256], r.hat_b[...], r.rstd_b[...], r.gains[16:17])
    for v in range(2):
        rows = slice(128 * v, 128 * v + 128)
        r.mid_grad[rows] = mid_grad[rows] + d_out[rows].astype(F32) * live[v].astype(F32)
    r.hb[...] = r.mid_grad[...].astype(BF16)
    att_x.drain()
    grad_o = dot_nt(r.hb[...], r.wout[...].reshape(768, 768)).astype(BF16)
    for v in range(2):
        for group in range(4):
            for j in range(2):
                row = 128 * v + 64 * j
                r.ab[4 * v + group, :, 192 * j : 192 * j + 192] = grad_o[row : row + 64, 192 * group : 192 * group + 192]
    gro_x.start()
    sd1.stage_d()
    r.rn[...] = jnp.zeros((4, 4, 2, 8, 128), F32)

    def put_norm(w, row):
        for s in range(8):
            r.rn[w, s // 2, s % 2, 0:1, 0:96] = row[:, 96 * s : 96 * s + 96]

    put_norm(2, jnp.sum(r.back[0:256] * r.hat_b[...], axis=0, keepdims=True))
    put_norm(3, jnp.sum(r.back[0:256], axis=0, keepdims=True))
    su1.stage_c()
    r.turned[...] = turned(r.att[...])
    for w in range(4):
        raw = dot(r.turned[...], r.hb[:, 192 * w : 192 * w + 192]).astype(BF16).reshape(4, 2, 2, 48, 192)
        for k in range(2):
            r.go[w, :, :, :, 192 * k : 192 * k + 192] = raw[:, :, k]
    for exchange in qkv_x:
        exchange.drain()
    gro_x.wait()
    so.stage_c()
    su0.stage_e()

    for head in range(3):
        r.gk[...] = jnp.zeros((64, 1024), F32)
        r.gv[...] = jnp.zeros((64, 1024), F32)

        def attend_back(c, _, head=head):
            q0 = pl.multiple_of(c * 256, 256)
            halves = []
            for j in range(2):
                at = 192 * j + 64 * head
                halves.append(r.gor[pl.ds(2 * c, 2), :, at : at + 64].reshape(2, 1, 64, 64))
            grad = jnp.concatenate(halves, axis=1).reshape(256, 64)
            prob = r.prob[head, pl.ds(q0, 256)]
            grad_p = dot_nt(grad, r.vh[head])
            prob_f = prob.astype(F32)
            inner = jnp.sum(prob_f * grad_p, axis=-1, keepdims=True)
            grad_s = (prob_f * (grad_p - inner)).astype(BF16)
            grad_q = (dot(grad_s, r.kh[head]) * (1.0 / math.sqrt(HD))).astype(BF16).reshape(2, 2, 64, 64)
            for j in range(2):
                r.sb[head, pl.ds(2 * c, 2), :, 192 * j : 192 * j + 64] = grad_q[:, j]
            r.gk[...] += dot_tn(r.qh[head, pl.ds(q0, 256)], grad_s)
            r.gv[...] += dot_tn(grad, prob)
            return 0

        lax.fori_loop(0, 4, attend_back, 0)
        for kind, grad in ((1, r.gk[...] * (1.0 / math.sqrt(HD))), (2, r.gv[...])):
            grad = jnp.transpose(grad).astype(BF16).reshape(8, 2, 64, 64)
            for j in range(2):
                at = 192 * j + 64 * kind
                r.sb[head, :, :, at : at + 64] = grad[:, j]
        if head == 1:
            mate_y.start()
        if head == 2:
            sd0.stage_f()
        gqkv_x[head].start()
    su0.stage_f()
    hidden = r.hat_a[...] * r.gains[0:1] + r.gains[8:9]
    r.turned[...] = turned(hidden)
    r.back[0:256] = jnp.zeros((256, 768), F32)
    for head in range(3):
        gqkv_x[head].wait()
        for v in range(2):
            for group in range(4):
                for kind in range(3):
                    for j in range(2):
                        row, at, to = 128 * v + 64 * j, 192 * j + 64 * kind, 768 * kind + 192 * group + 64 * head
                        r.wide[row : row + 64, to : to + 64] = r.gb[head, 4 * v + group, :, at : at + 64]
        if head == 0:
            so.stage_d()
            su1.stage_d()
        if head == 1:
            sd1.stage_e()
    for w in range(4):
        grad = r.wide[:, 576 * w : 576 * w + 576]
        r.back[0:256] += dot_nt(grad, rows_of(r.gq, w, 768))
        r.gq[w] = dot(r.turned[...], grad).astype(BF16).reshape(4, 2, 96, 576)
    sd1.stage_f()
    sq2.stage_c()
    sq1.stage_c()

    def put_down(k, halves):
        for half, value in enumerate(halves):
            for j in range(2):
                row, at = 96 * j + 48 * k, 192 * half
                red_d[row : row + 48, at : at + 192] = value[:, 192 * j : 192 * j + 192]

    def put_up(k, halves):
        for half, value in enumerate(halves):
            for j in range(2):
                at = 384 * j + 192 * half
                red_u[48 * k : 48 * k + 48, at : at + 192] = value[:, 192 * j : 192 * j + 192]

    put_down(0, sd0.finish_halves())
    so.stage_e()
    su1.stage_e()
    grad_h = r.back[0:256]
    put_norm(0, jnp.sum(grad_h * r.hat_a[...], axis=0, keepdims=True))
    put_norm(1, jnp.sum(grad_h, axis=0, keepdims=True))
    put_down(1, sd1.finish_halves())
    stores[5].start()
    sq2.stage_d()
    sq1.stage_d()
    sq0.stage_c()
    sq0.stage_d()
    so.stage_f()
    sq2.stage_e()
    sq1.stage_e()
    su1.stage_f()
    sn.stage_c()
    d_input[...] = r.mid_grad[...] + norm_back(grad_h, r.hat_a[...], r.rstd_a[...], r.gains[0:1])
    stores[1].start()
    sn.stage_d()
    red_o[...] = so.finish()
    stores[3].start()
    mate_y.wait_recv()
    output[...] = (r.y[0:256] + r.y_in[...].astype(F32)).astype(BF16)
    stores[0].start()
    sq2.stage_f()
    sq1.stage_f()
    sq0.stage_e()
    sn.stage_e()
    sq0.stage_f()
    sn.stage_f()
    put_up(1, su1.finish_halves())
    put_up(0, su0.finish_halves())
    stores[4].start()
    red_q[64:96] = sq2.finish()
    red_q[32:64] = sq1.finish()
    red_q[0:32] = sq0.finish()
    stores[2].start()
    red_n[...] = sn.finish()
    stores[6].start()
    local = jnp.zeros((8, 128), F32)
    for ref in (red_q, red_o, red_u, red_d, red_n):
        local = local + jnp.sum(ref[...] * ref[...])
    r.square[...] = local
    r.squares[0] = local

    def share(k):
        to = ((p.w + k // 8) % 4, (p.s + k % 8) % 8)
        return remote(r.square, r.squares.at[k], r.sum_sems, k, to)

    def share_start(k, _):
        share(k).start()
        return 0

    def share_wait(k, _):
        share(k).wait()
        return 0

    lax.fori_loop(1, 32, share_start, 0)
    for part in (count_x, gro_x, *gqkv_x, *scatters):
        part.drain()
    for copy in (mate_h, mate_g, mate_back, mate_y):
        copy.wait_send()
    lax.fori_loop(1, 32, share_wait, 0)
    total[...] = jnp.sum(r.squares[...], axis=0)
    stores[7].start()
    for copy in stores:
        copy.wait()


def adam_kernel(*refs):
    given, made, here, there, sems = refs[0:23], refs[23:46], refs[46:69], refs[69:90], refs[90]
    loads = [pltpu.make_async_copy(a, b, sems.at[k]) for k, (a, b) in enumerate(zip(given, here))]
    stores = [pltpu.make_async_copy(a, b, sems.at[23 + k]) for k, (a, b) in enumerate(zip((*there, *here[21:23]), made))]
    order = (2, 3, 0, 1, 4)
    loads[20].start()
    for k in order:
        for part in range(4):
            loads[5 * part + k].start()
    for k in (22, 21):
        loads[k].start()
    fix_one = 1.0 - beta_one**STEP
    fix_two = 1.0 - beta_two**STEP
    rates = (rate_matrix, rate_output, rate_matrix, rate_matrix, rate_norm)
    loads[20].wait()
    norm = jnp.sqrt(here[20][0:1, 0:1])
    factor = 1.0 / jnp.maximum(norm, 1.0)
    there[20][...] = norm
    stores[20].start()
    for k in order:
        for part in range(4):
            loads[5 * part + k].wait()
        raw = here[k][...]
        if k == 1:
            raw = jnp.concatenate([raw[:, 0:192], raw[:, 192:384]], axis=0)
        if k == 4:
            raw = raw[0:1, 0:96]
        grad = raw * factor
        weight = here[5 + k][...]
        first = beta_one * here[10 + k][...] + (1.0 - beta_one) * grad
        second = beta_two * here[15 + k][...] + (1.0 - beta_two) * grad * grad
        stride = first / fix_one / (jnp.sqrt(second / fix_two) + adam_eps)
        decay = 0.0 if k == 4 else decay_rate
        there[k][...] = grad
        there[5 + k][...] = weight - rates[k] * (stride + decay * weight)
        there[10 + k][...] = first
        there[15 + k][...] = second
        for part in range(4):
            stores[5 * part + k].start()
        if k == 2:
            for j in (22, 21):
                loads[j].wait()
                stores[j].start()
    for copy in stores:
        copy.wait()


def fused_device(
    layer_input, d_out, rand_ids, live_mask, w_qkv, w_out, w_up, w_down, norm_params,
    m_qkv, m_out, m_up, m_down, m_norm, v_qkv, v_out, v_up, v_down, v_norm,
):
    smem, anywhere = (pl.BlockSpec(memory_space=kind) for kind in (pltpu.SMEM, pl.ANY))
    ids = rand_ids.transpose(0, 2, 3, 1).reshape(24, 6)
    leaves, tree = jax.tree.flatten(scratch())
    shape = jax.ShapeDtypeStruct
    output, d_input, *grads, total = pl.pallas_call(
        functools.partial(kernel, tree),
        out_shape=[shape(*leaf) for leaf in KEPT],
        in_specs=[smem, smem] + [anywhere] * 7,
        out_specs=[anywhere] * 8,
        scratch_shapes=leaves,
        compiler_params=pltpu.CompilerParams(collective_id=0, has_side_effects=True, vmem_limit_bytes=VMEM_LIMIT),
    )(
        live_mask, ids, layer_input.reshape(256, 768), d_out.reshape(256, 768), w_qkv, w_out, w_up, w_down.T,
        norm_params.reshape(1, 96),
    )
    state = (
        *grads,
        w_qkv, w_out, w_up, w_down.T, norm_params.reshape(1, 96),
        m_qkv, m_out, m_up, m_down.T, m_norm.reshape(1, 96),
        v_qkv, v_out, v_up, v_down.T, v_norm.reshape(1, 96),
        total, output, d_input,
    )
    results = [shape(w.shape, F32) for w in state[5:10]] * 4
    results += [shape((1, 1), F32), shape(output.shape, BF16), shape(d_input.shape, F32)]
    made = pl.pallas_call(
        adam_kernel,
        out_shape=results,
        in_specs=[anywhere] * 23,
        out_specs=[anywhere] * 23,
        scratch_shapes=[pltpu.VMEM(a.shape, a.dtype) for a in (*state, *results[:21])] + [pltpu.SemaphoreType.DMA((46,))],
        compiler_params=pltpu.CompilerParams(vmem_limit_bytes=VMEM_LIMIT),
    )(*state)
    updated = [m.T if k % 5 == 3 else m.reshape(-1) if k % 5 == 4 else m for k, m in enumerate(made[:20])]
    return (made[21].reshape(2, 128, 768), made[22].reshape(2, 128, 768), *updated, made[20].reshape(1))


def solution(mesh):
    placed = (
        P("win", "seq", None),
        P("win", "seq", None),
        P("win", "seq", None, None),
        P("win"),
        P("seq", "win"),
        P("seq", "win"),
        P("seq", "win"),
        P("seq", "win"),
        P(("win", "seq")),
        P("seq", "win"),
        P("seq", "win"),
        P("seq", "win"),
        P("seq", "win"),
        P(("win", "seq")),
        P("seq", "win"),
        P("seq", "win"),
        P("seq", "win"),
        P("seq", "win"),
        P(("win", "seq")),
    )
    fused = mesh.shape["win"] == 4 and mesh.shape["seq"] == 8
    return jax.shard_map(
        fused_device if fused else per_device,
        mesh=mesh,
        in_specs=placed,
        out_specs=(
            P("win", "seq", None),
            P("win", "seq", None),
            P("seq", "win"),
            P("seq", "win"),
            P("seq", "win"),
            P("seq", "win"),
            P(("win", "seq")),
            P("seq", "win"),
            P("seq", "win"),
            P("seq", "win"),
            P("seq", "win"),
            P(("win", "seq")),
            P("seq", "win"),
            P("seq", "win"),
            P("seq", "win"),
            P("seq", "win"),
            P(("win", "seq")),
            P("seq", "win"),
            P("seq", "win"),
            P("seq", "win"),
            P("seq", "win"),
            P(("win", "seq")),
            P(),
        ),
        check_vma=False,
    )
```

```python
import functools
import math
from typing import Any, NamedTuple

import jax
import jax.numpy as jnp
from jax import lax
from jax.experimental import pallas as pl
from jax.experimental.pallas import tpu as pltpu
from jax.sharding import PartitionSpec as P

H = 12
HD = 64
BLK = 64
STEP = 3


NEG = -1e30
ln_eps = 1e-05
beta_one = 0.5
beta_two = 0.5
adam_eps = 1e-08
decay_rate = 0.1
rate_matrix = 0.04
rate_output = 0.16
rate_norm = 0.6
VMEM_LIMIT = 63 << 20


def layer_norm(values, gain, shift):
    centre = values - jnp.mean(values, axis=-1, keepdims=True)
    spread = jnp.mean(centre * centre, axis=-1, keepdims=True)
    return centre * lax.rsqrt(spread + ln_eps) * gain + shift


def slot_counts(rand_ids, first_block, block_count):
    blocks_dev = rand_ids.shape[1]
    here = (first_block + jnp.arange(blocks_dev, dtype=jnp.int32))[:, None]
    every = jnp.arange(block_count, dtype=jnp.int32)[None, :]
    near = (jnp.abs(here - every) <= 1).astype(jnp.float32)
    ends = (every == 0).astype(jnp.float32) + (every == block_count - 1).astype(jnp.float32)
    drawn = jnp.sum((rand_ids[..., None] == every[0]).astype(jnp.float32), axis=3)
    return (near + ends)[None, :, None, :] + drawn


def adam_update(weight, grad, first, second, rate, decay, fix_one, fix_two):
    first_new = beta_one * first + (1.0 - beta_one) * grad
    second_new = beta_two * second + (1.0 - beta_two) * grad * grad
    stride = first_new / fix_one / (jnp.sqrt(second_new / fix_two) + adam_eps)
    return (weight - rate * (stride + decay * weight), first_new, second_new)


def per_device(
    layer_input,
    d_out,
    rand_ids,
    live_mask,
    w_qkv,
    w_out,
    w_up,
    w_down,
    norm_params,
    m_qkv,
    m_out,
    m_up,
    m_down,
    m_norm,
    v_qkv,
    v_out,
    v_up,
    v_down,
    v_norm,
):
    wins, local_len, width = layer_input.shape
    blocks_dev = local_len // BLK
    block_count = blocks_dev * lax.axis_size("seq")
    first_block = lax.axis_index("seq") * blocks_dev
    inv_root = 1.0 / math.sqrt(HD)
    rows = wins * local_len
    low_qkv = w_qkv.astype(jnp.bfloat16)
    low_out = w_out.astype(jnp.bfloat16)
    low_up = w_up.astype(jnp.bfloat16)
    low_down = w_down.astype(jnp.bfloat16)
    low_norm = norm_params.astype(jnp.bfloat16)
    full_qkv, full_out, full_up, full_down = (
        lax.all_gather(lax.all_gather(low, "win", axis=1, tiled=True), "seq", axis=0, tiled=True)
        for low in (low_qkv, low_out, low_up, low_down)
    )
    full_norm = lax.all_gather(low_norm, ("win", "seq"), axis=0, tiled=True)
    gains = full_norm.astype(jnp.float32).reshape(4, width)
    loss_weight = live_mask.astype(jnp.float32)
    counts = slot_counts(rand_ids, first_block, block_count)
    bias = jnp.where(counts > 0, jnp.log(jnp.maximum(counts, 1.0)), NEG)
    bias = jnp.repeat(bias, BLK, axis=3)[:, :, :, None, :]
    tokens = layer_input.astype(jnp.float32).reshape(rows, width)
    h_one = layer_norm(tokens, gains[0], gains[1]).astype(jnp.bfloat16)
    qkv = jnp.dot(h_one, full_qkv, preferred_element_type=jnp.float32)
    q_heads = qkv[:, :width].astype(jnp.bfloat16).reshape(wins, blocks_dev, BLK, H, HD)
    keyval = qkv[:, width:].astype(jnp.bfloat16).reshape(wins, local_len, 2 * width)
    window = lax.all_gather(keyval, "seq", axis=1, tiled=True)
    shaped = window.reshape(wins, block_count * BLK, 2, H, HD)
    keys, values = shaped[:, :, 0], shaped[:, :, 1]
    scores = (
        jnp.einsum("wbqhd,wkhd->wbhqk", q_heads, keys, preferred_element_type=jnp.float32)
        * inv_root
        + bias
    )
    top = jnp.max(scores, axis=-1, keepdims=True)
    log_total = top + jnp.log(jnp.sum(jnp.exp(scores - top), axis=-1, keepdims=True))
    prob = jnp.exp(scores - log_total).astype(jnp.bfloat16)
    heads_out = jnp.einsum("wbhqk,wkhd->wbqhd", prob, values, preferred_element_type=jnp.float32)
    attended = heads_out.astype(jnp.bfloat16).reshape(rows, width)
    middle = tokens + jnp.dot(attended, full_out, preferred_element_type=jnp.float32)
    h_two = layer_norm(middle, gains[2], gains[3]).astype(jnp.bfloat16)
    up_proj = jnp.dot(h_two, full_up, preferred_element_type=jnp.float32)
    active = jax.nn.gelu(up_proj).astype(jnp.bfloat16)
    result = middle + jnp.dot(active, full_down, preferred_element_type=jnp.float32)
    output = result.astype(jnp.bfloat16).reshape(wins, local_len, width)
    grad_y = (d_out.astype(jnp.float32) * loss_weight[:, None, None]).reshape(rows, width)
    grad_ffn = grad_y.astype(jnp.bfloat16)
    raw_down = jnp.einsum("tf,td->fd", active, grad_ffn, preferred_element_type=jnp.float32)
    grad_act = jnp.einsum("td,fd->tf", grad_ffn, full_down, preferred_element_type=jnp.float32)
    gelu_pull = jax.vjp(jax.nn.gelu, up_proj)[1]
    grad_up = gelu_pull(grad_act)[0].astype(jnp.bfloat16)
    raw_up = jnp.einsum("td,tf->df", h_two, grad_up, preferred_element_type=jnp.float32)
    grad_h_two = jnp.einsum("tf,df->td", grad_up, full_up, preferred_element_type=jnp.float32)
    norm_pull = jax.vjp(layer_norm, middle, gains[2], gains[3])[1]
    grad_mid_ln, raw_gain_two, raw_shift_two = norm_pull(grad_h_two)
    grad_mid = grad_y + grad_mid_ln
    grad_att = grad_mid.astype(jnp.bfloat16)
    raw_out = jnp.einsum("td,te->de", attended, grad_att, preferred_element_type=jnp.float32)
    grad_o = jnp.einsum("te,de->td", grad_att, full_out, preferred_element_type=jnp.float32)
    grad_o = grad_o.astype(jnp.bfloat16).reshape(wins, blocks_dev, BLK, H, HD)
    grad_p = jnp.einsum("wbqhd,wkhd->wbhqk", grad_o, values, preferred_element_type=jnp.float32)
    prob_f = prob.astype(jnp.float32)
    inner = jnp.sum(prob_f * grad_p, axis=-1, keepdims=True)
    grad_s = (prob_f * (grad_p - inner)).astype(jnp.bfloat16)
    grad_q = (
        jnp.einsum("wbhqk,wkhd->wbqhd", grad_s, keys, preferred_element_type=jnp.float32)
        * inv_root
    )
    grad_v = jnp.einsum("wbhqk,wbqhd->wkhd", prob, grad_o, preferred_element_type=jnp.float32)
    grad_k = (
        jnp.einsum("wbhqk,wbqhd->wkhd", grad_s, q_heads, preferred_element_type=jnp.float32)
        * inv_root
    )
    grad_kv = jnp.stack([grad_k, grad_v], axis=2).astype(jnp.bfloat16)
    grad_kv = lax.psum_scatter(
        grad_kv.reshape(wins, block_count * BLK, 2 * width),
        "seq",
        scatter_dimension=1,
        tiled=True,
    ).reshape(rows, 2 * width)
    grad_qkv = jnp.concatenate(
        [grad_q.reshape(rows, width).astype(jnp.bfloat16), grad_kv], axis=1
    )
    raw_qkv = jnp.einsum("td,te->de", h_one, grad_qkv, preferred_element_type=jnp.float32)
    grad_h_one = jnp.einsum("te,de->td", grad_qkv, full_qkv, preferred_element_type=jnp.float32)
    first_pull = jax.vjp(layer_norm, tokens, gains[0], gains[1])[1]
    grad_tok_ln, raw_gain_one, raw_shift_one = first_pull(grad_h_one)
    d_input = (grad_mid + grad_tok_ln).reshape(wins, local_len, width)
    raw_norm = jnp.concatenate([raw_gain_one, raw_shift_one, raw_gain_two, raw_shift_two])
    red_qkv, red_out, red_up, red_down = (
        lax.psum_scatter(
            lax.psum_scatter(raw.astype(jnp.bfloat16), "seq", scatter_dimension=0, tiled=True),
            "win",
            scatter_dimension=1,
            tiled=True,
        ).astype(jnp.float32)
        for raw in (raw_qkv, raw_out, raw_up, raw_down)
    )
    red_norm = lax.psum_scatter(raw_norm, ("win", "seq"), scatter_dimension=0, tiled=True)
    reduced = (red_qkv, red_out, red_up, red_down, red_norm)
    local_squares = jnp.float32(0.0)
    for grad in reduced:
        local_squares = local_squares + jnp.sum(grad * grad)
    grad_norm = jnp.sqrt(lax.psum(local_squares, ("win", "seq")))
    factor = 1.0 / jnp.maximum(grad_norm, 1.0)
    clipped = tuple((grad * factor for grad in reduced))
    count = jnp.float32(STEP)
    fix_one = 1.0 - jnp.power(jnp.float32(beta_one), count)
    fix_two = 1.0 - jnp.power(jnp.float32(beta_two), count)
    params = (w_qkv, w_out, w_up, w_down, norm_params)
    firsts = (m_qkv, m_out, m_up, m_down, m_norm)
    seconds = (v_qkv, v_out, v_up, v_down, v_norm)
    rates = (rate_matrix, rate_output, rate_matrix, rate_matrix, rate_norm)
    news, moms, secs = ([], [], [])
    for index in range(5):
        decay = 0.0 if index == 4 else decay_rate
        new_w, new_m, new_v = adam_update(
            params[index],
            clipped[index],
            firsts[index],
            seconds[index],
            rates[index],
            decay,
            fix_one,
            fix_two,
        )
        news.append(new_w)
        moms.append(new_m)
        secs.append(new_v)
    return (
        output,
        d_input,
        clipped[0],
        clipped[1],
        clipped[2],
        clipped[3],
        clipped[4],
        news[0],
        news[1],
        news[2],
        news[3],
        news[4],
        moms[0],
        moms[1],
        moms[2],
        moms[3],
        moms[4],
        secs[0],
        secs[1],
        secs[2],
        secs[3],
        secs[4],
        grad_norm.reshape(1),
    )


MESH = pl.DeviceIdType.MESH
F32, BF16 = jnp.float32, jnp.bfloat16
GELU_C = math.sqrt(2.0 / math.pi)
NT = (((1,), (1,)), ((), ()))
TN = (((0,), (0,)), ((), ()))


def dot(a, b):
    return jnp.dot(a, b, preferred_element_type=F32)


def dot_nt(a, b):
    return lax.dot_general(a, b, NT, preferred_element_type=F32)


def dot_tn(a, b):
    return lax.dot_general(a, b, TN, preferred_element_type=F32)


def remote(src, dst, sems, k, dev):
    return pltpu.make_async_remote_copy(
        src_ref=src, dst_ref=dst, send_sem=sems[0].at[k], recv_sem=sems[1].at[k], device_id=dev, device_id_type=MESH
    )


class Place:
    def __init__(self):
        self.w = lax.axis_index("win")
        self.s = s = lax.axis_index("seq")
        self.c = c = s % 2
        x = (s // 2) % 2
        y = s // 4
        dx, dy = 2 - 4 * x, 4 - 8 * y
        self.turn = 1 - 2 * c
        self.n1 = s + (1 - c) * dx + c * dy
        self.n2 = s + (1 - c) * dy + c * dx
        self.nd = s + dx + dy
        self.par = s + self.turn
        self.roles = (s, self.n1, self.n2, self.nd)
        self.par_roles = tuple(r + self.turn for r in (s, self.n2, self.n1, self.nd))
        self.x, self.y = x, y
        self.mate = (self.w + 1 - 2 * (self.w % 2), s)

    def chip(self, k):
        x = self.x + (1 - k % 2) * (1 - 2 * self.x)
        y = self.y + (1 - k // 2) * (1 - 2 * self.y)
        return 2 * y + x

    def role_for_partner(self, chip):
        dx = (chip % 2 - self.x) * (chip % 2 - self.x)
        dy = (chip // 2 - self.y) * (chip // 2 - self.y)
        return self.c * (dx + 2 * dy) + (1 - self.c) * (dy + 2 * dx)


class Blocks:
    def __init__(self, buf, seq_first=False, start=0, count=None):
        self.buf, self.seq_first, self.rows = buf, seq_first, pl.ds(start, buf.shape[3] if count is None else count)

    def block(self, w, s):
        return self.buf.at[(s // 2, s % 2, w, self.rows) if self.seq_first else (w, s // 2, s % 2, self.rows)]

    def read(self, w, s):
        return self.buf[(s // 2, s % 2, w, self.rows) if self.seq_first else (w, s // 2, s % 2, self.rows)]

    def group(self, s):
        every = slice(None)
        return self.buf.at[(s // 2, s % 2, every, self.rows) if self.seq_first else (every, s // 2, s % 2, self.rows)]


class Gather:
    def __init__(self, place, blocks, sems, staged=None):
        self.p, self.b, self.sems, self.staged = place, blocks, sems, staged

    def push(self, s, k, to):
        remote(self.b.group(s), self.b.group(s), self.sems, k, (self.p.w, to)).start()

    def got(self, s, k):
        remote(self.b.group(s), self.b.group(s), self.sems, k, (self.p.w, self.p.par)).wait_recv()

    def along(self, dz, w):
        p, block = self.p, self.b.block(w, self.p.s)
        source = block if self.staged is None else self.staged.at[(p.w + dz) % 2, self.b.rows]
        return remote(source, block, self.sems, dz - 1, ((p.w + dz) % 4, p.s))

    def z_send(self):
        for dz in (1, 2, 3):
            self.along(dz, self.p.w).start()

    def stage1(self):
        p = self.p
        for dz in (1, 2, 3):
            self.along(dz, (p.w + 4 - dz) % 4).wait_recv()
        self.push(p.s, 3, p.n1)
        self.push(p.s, 4, p.n2)
        self.push(p.s, 6, p.par)

    def stage2(self):
        p = self.p
        self.got(p.n1, 3)
        self.push(p.n1, 5, p.n2)
        self.push(p.n1, 7, p.par)

    def stage3(self):
        p = self.p
        self.got(p.n2, 4)
        self.push(p.n2, 8, p.par)
        self.got(p.nd, 5)
        self.push(p.nd, 9, p.par)

    def finish(self):
        for k in range(4):
            self.got(self.p.par_roles[k], 6 + k)

    def drain(self):
        p = self.p
        for dz in (1, 2, 3):
            self.along(dz, p.w).wait_send()
        for k, s in ((3, p.s), (4, p.s), (6, p.s), (5, p.n1), (7, p.n1), (8, p.n2), (9, p.nd)):
            remote(self.b.group(s), self.b.group(s), self.sems, k, (p.w, p.par)).wait_send()


class Scatter:
    def __init__(self, place, blocks, space, sems):
        self.p, self.b, self.sems = place, blocks, sems
        self.c, self.d, self.e, self.f = space

    def copies_c(self):
        p = self.p
        return [remote(self.b.group(p.par_roles[k]), self.c.at[k], self.sems, k, (p.w, p.par)) for k in range(4)]

    def copies_d(self):
        p = self.p
        return [remote(self.c.at[2 + k], self.d.at[k], self.sems, 4 + k, (p.w, p.n2)) for k in range(2)]

    def copy_e(self):
        p = self.p
        return remote(self.c.at[1], self.e, self.sems, 6, (p.w, p.n1))

    def copies_f(self):
        p = self.p
        return [
            remote(self.c.at[0, (p.w + dz) % 4], self.f.at[dz - 1], self.sems, 6 + dz, ((p.w + dz) % 4, p.s))
            for dz in (1, 2, 3)
        ]

    def stage_c(self):
        for copy in self.copies_c():
            copy.start()

    def stage_c_of(self, chip):
        p = self.p
        role = p.role_for_partner(chip)
        remote(self.b.group(2 * chip + 1 - p.c), self.c.at[role], self.sems, role, (p.w, p.par)).start()

    def stage_d(self):
        waits, sends = self.copies_c(), self.copies_d()
        for k in (2, 3, 0, 1):
            waits[k].wait_recv()
            for w in range(4):
                self.c[k, w] = self.c[k, w] + self.b.read(w, self.p.roles[k])
            if k >= 2:
                sends[k - 2].start()

    def stage_e(self):
        waits = self.copies_d()
        for k in (1, 0):
            waits[k].wait_recv()
            for w in range(4):
                self.c[k, w] = self.c[k, w] + self.d[k, w]
            if k == 1:
                self.copy_e().start()

    def stage_f(self):
        self.copy_e().wait_recv()
        for w in range(4):
            self.c[0, w] = self.c[0, w] + self.e[w]
        for copy in self.copies_f():
            copy.start()

    def finish(self):
        total = self.c[0, self.p.w].astype(F32)
        for k, copy in enumerate(self.copies_f()):
            copy.wait_recv()
            total = total + self.f[k].astype(F32)
        return total

    def finish_halves(self):
        p = self.p
        for copy in self.copies_f():
            copy.wait_recv()
        alike = self.c[0, p.w].astype(F32) + self.f[1].astype(F32)
        other = self.f[0].astype(F32) + self.f[2].astype(F32)
        even = p.w % 2 == 0
        return jnp.where(even, alike, other), jnp.where(even, other, alike)

    def drain(self):
        for copy in (*self.copies_c(), *self.copies_d(), self.copy_e(), *self.copies_f()):
            copy.wait_send()


class Exchange:
    def __init__(self, place, src, dst, sems):
        self.p, self.src, self.dst, self.sems = place, src, dst, sems

    def copy(self, ds):
        p = self.p
        to = (p.s + ds) % 8
        return remote(self.src.at[to], self.dst.at[p.s], self.sems, ds, (p.w, to))

    def own(self):
        return pltpu.make_async_copy(self.src.at[self.p.s], self.dst.at[self.p.s], self.sems[1].at[0])

    def start(self):
        for ds in (6, 5, 3, 7, 4, 2, 1):
            self.copy(ds).start()
        self.own().start()

    def wait(self):
        p = self.p
        self.own().wait()
        for ds in range(1, 8):
            back = (p.s + 8 - ds) % 8
            remote(self.src.at[back], self.dst.at[back], self.sems, ds, (p.w, back)).wait_recv()

    def drain(self):
        for ds in range(1, 8):
            self.copy(ds).wait_send()


def norm_stats(values):
    centre = values - jnp.mean(values, axis=-1, keepdims=True)
    rstd = lax.rsqrt(jnp.mean(centre * centre, axis=-1, keepdims=True) + ln_eps)
    return centre * rstd, rstd


def norm_back(grad, hat, rstd, gain):
    scaled = grad * gain
    return rstd * (
        scaled - jnp.mean(scaled, axis=-1, keepdims=True) - hat * jnp.mean(scaled * hat, axis=-1, keepdims=True)
    )


def rows_of(ref, index, rows):
    value = ref[index]
    return value.reshape(rows, value.shape[-1])


def turned(value):
    return jnp.transpose(value.astype(F32)).astype(BF16)


GIVEN = (
    ((256, 768), BF16), ((256, 768), BF16), ((96, 576), F32), ((96, 192), F32), ((96, 768), F32), ((192, 384), F32), ((1, 96), F32),
)
KEPT = (
    ((256, 768), BF16), ((256, 768), F32), ((96, 576), F32), ((48, 384), F32), ((96, 768), F32), ((192, 384), F32), ((8, 128), F32), ((8, 128), F32),
)


class Space(NamedTuple):
    gn: Any
    gq: Any
    go: Any
    gu: Any
    gd: Any
    rn: Any
    sn: Any
    sq: Any
    so: Any
    su: Any
    sd: Any
    half_u: Any
    half_d: Any
    wd: Any
    gather_sems: Any
    scatter_sems: Any
    exchange_sems: Any
    sum_sems: Any
    count_out: Any
    counts: Any
    bias: Any
    sb: Any
    rb: Any
    qh: Any
    kh: Any
    vh: Any
    prob: Any
    share: Any
    kept_o: Any
    ab: Any
    at: Any
    gor: Any
    gb: Any
    att: Any
    wout: Any
    turned: Any
    turned_i: Any
    turned_h: Any
    turned_g: Any
    gains: Any
    hat_a: Any
    hat_b: Any
    rstd_a: Any
    rstd_b: Any
    h: Any
    hb: Any
    hs: Any
    gys: Any
    back_out: Any
    back_in: Any
    y_out: Any
    y_in: Any
    mate_sems: Any
    wide: Any
    y: Any
    back: Any
    mid_grad: Any
    gk: Any
    gv: Any
    act: Any
    slope: Any
    square: Any
    squares: Any
    given: Any
    kept: Any
    io_sems: Any


def scratch():
    def scatter(*block, kind=BF16):
        return tuple(pltpu.VMEM((*lead, *block), kind) for lead in ((4, 4), (2, 4), (4,), (3,)))

    def sems(count):
        return (pltpu.SemaphoreType.DMA((count,)),) * 2

    rows, wide = (256, 768), (3, 8, 64, 384)
    return Space(
        gn=pltpu.VMEM((4, 4, 2, 8, 128), F32),
        gq=pltpu.VMEM((4, 4, 2, 96, 576), BF16),
        go=pltpu.VMEM((4, 4, 2, 48, 384), BF16),
        gu=pltpu.VMEM((4, 4, 2, 96, 384), BF16),
        gd=pltpu.VMEM((4, 2, 4, 96, 384), BF16),
        rn=pltpu.VMEM((4, 4, 2, 8, 128), F32),
        sn=scatter(8, 128, kind=F32),
        sq=tuple(scatter(32, 576) for _ in range(3)),
        so=scatter(48, 384),
        su=tuple(scatter(48, 384) for _ in range(2)),
        sd=tuple(scatter(48, 384) for _ in range(2)),
        half_u=pltpu.VMEM((2, 96, 384), BF16),
        half_d=pltpu.VMEM((2, 96, 384), BF16),
        wd=pltpu.VMEM((2, 4, 2, 96, 768), BF16),
        gather_sems=tuple(sems(10) for _ in range(9)),
        scatter_sems=tuple(sems(10) for _ in range(9)),
        exchange_sems=tuple(sems(8) for _ in range(9)),
        sum_sems=sems(32),
        count_out=pltpu.VMEM((8, 8, 128), F32),
        counts=pltpu.VMEM((8, 8, 128), F32),
        bias=pltpu.VMEM((3, 4, 4, 1024), F32),
        sb=pltpu.VMEM(wide, BF16),
        rb=pltpu.VMEM(wide, BF16),
        qh=pltpu.VMEM((3, 1024, 64), BF16),
        kh=pltpu.VMEM((3, 1024, 64), BF16),
        vh=pltpu.VMEM((3, 1024, 64), BF16),
        prob=pltpu.VMEM((3, 1024, 1024), BF16),
        share=pltpu.VMEM((3, 1024, 1), F32),
        kept_o=pltpu.VMEM((3, 1024, 64), BF16),
        ab=pltpu.VMEM((8, 64, 384), BF16),
        at=pltpu.VMEM((8, 64, 384), BF16),
        gor=pltpu.VMEM((8, 64, 384), BF16),
        gb=pltpu.VMEM(wide, BF16),
        att=pltpu.VMEM(rows, BF16),
        wout=pltpu.VMEM((4, 2, 2, 48, 768), BF16),
        turned=pltpu.VMEM((768, 256), BF16),
        turned_i=pltpu.VMEM((768, 256), BF16),
        turned_h=pltpu.VMEM((768, 512), BF16),
        turned_g=pltpu.VMEM((768, 512), BF16),
        gains=pltpu.VMEM((32, 768), F32),
        hat_a=pltpu.VMEM(rows, F32),
        hat_b=pltpu.VMEM(rows, F32),
        rstd_a=pltpu.VMEM((256, 1), F32),
        rstd_b=pltpu.VMEM((256, 1), F32),
        h=pltpu.VMEM(rows, BF16),
        hb=pltpu.VMEM(rows, BF16),
        hs=pltpu.VMEM((2, *rows), BF16),
        gys=pltpu.VMEM((2, *rows), BF16),
        back_out=pltpu.VMEM(rows, BF16),
        back_in=pltpu.VMEM(rows, BF16),
        y_out=pltpu.VMEM(rows, BF16),
        y_in=pltpu.VMEM(rows, BF16),
        mate_sems=sems(4),
        wide=pltpu.VMEM((256, 2304), BF16),
        y=pltpu.VMEM((512, 768), F32),
        back=pltpu.VMEM((512, 768), F32),
        mid_grad=pltpu.VMEM(rows, F32),
        gk=pltpu.VMEM((64, 1024), F32),
        gv=pltpu.VMEM((64, 1024), F32),
        act=pltpu.VMEM((2, 512, 768), BF16),
        slope=pltpu.VMEM((2, 512, 768), BF16),
        square=pltpu.VMEM((8, 128), F32),
        squares=pltpu.VMEM((32, 8, 128), F32),
        given=tuple(pltpu.VMEM(dims, kind) for dims, kind in GIVEN),
        kept=tuple(pltpu.VMEM(dims, kind) for dims, kind in KEPT),
        io_sems=pltpu.SemaphoreType.DMA((15,)),
    )


def kernel(tree, live, rand_ids, *refs):
    r = jax.tree.unflatten(tree, refs[15:])
    x, d_out, w_qkv, w_out, w_up, w_down, norm = r.given
    output, d_input, red_q, red_o, red_u, red_d, red_n, total = r.kept
    loads = [pltpu.make_async_copy(a, b, r.io_sems.at[k]) for k, (a, b) in enumerate(zip(refs[:7], r.given))]
    stores = [pltpu.make_async_copy(a, b, r.io_sems.at[7 + k]) for k, (a, b) in enumerate(zip(r.kept, refs[7:15]))]
    for k in (6, 2, 5, 3, 4, 0, 1):
        loads[k].start()
    p = Place()
    barrier = pltpu.get_barrier_semaphore()

    def greet(k, _):
        to = ((p.w + k // 8) % 4, (p.s + k % 8) % 8)
        pl.semaphore_signal(barrier, inc=1, device_id=to, device_id_type=MESH)
        return 0

    lax.fori_loop(1, 32, greet, 0)

    blocks_q = [Blocks(r.gq, start=32 * k, count=32) for k in range(3)]
    blocks_u = [Blocks(r.gu, start=48 * k, count=48) for k in range(2)]
    blocks_d = [Blocks(r.gd, True, start=48 * k, count=48) for k in range(2)]
    every = (*blocks_q, Blocks(r.go), *blocks_u, *blocks_d)
    staged = (None,) * 4 + (r.half_u,) * 2 + (r.half_d,) * 2
    gathers = [Gather(p, Blocks(r.gn), r.gather_sems[8])]
    gathers += [Gather(p, b, m, half) for b, m, half in zip(every, r.gather_sems, staged)]
    gn, gq0, gq1, gq2, go, gu0, gu1, gd0, gd1 = gathers
    scatters = [Scatter(p, Blocks(r.rn), r.sn, r.scatter_sems[8])]
    scatters += [Scatter(p, b, space, m) for b, space, m in zip(every, (*r.sq, r.so, *r.su, *r.sd), r.scatter_sems)]
    sn, sq0, sq1, sq2, so, su0, su1, sd0, sd1 = scatters
    mate_h = remote(r.hs.at[0], r.hs.at[1], r.mate_sems, 0, p.mate)
    mate_g = remote(r.gys.at[0], r.gys.at[1], r.mate_sems, 1, p.mate)
    mate_back = remote(r.back_out, r.back_in, r.mate_sems, 2, p.mate)
    mate_y = remote(r.y_out, r.y_in, r.mate_sems, 3, p.mate)
    count_x = Exchange(p, r.count_out, r.counts, r.exchange_sems[0])
    att_x = Exchange(p, r.ab, r.at, r.exchange_sems[1])
    gro_x = Exchange(p, r.ab, r.gor, r.exchange_sems[2])
    qkv_x = [Exchange(p, r.sb.at[h], r.rb.at[h], r.exchange_sems[3 + h]) for h in range(3)]
    gqkv_x = [Exchange(p, r.sb.at[h], r.gb.at[h], r.exchange_sems[6 + h]) for h in range(3)]
    chip, core = p.s // 2, p.c

    r.gn[p.w, chip, core] = jnp.zeros((8, 128), F32)
    loads[6].wait()
    r.gn[p.w, chip, core, 0:1, 0:96] = norm[...].astype(BF16).astype(F32)
    loads[2].wait()
    r.gq[p.w, chip, core] = w_qkv[...].astype(BF16)
    pl.semaphore_wait(barrier, 31)
    gq0.z_send()
    gn.z_send()
    gq1.z_send()
    gq2.z_send()
    loads[3].wait()
    for k in range(2):
        r.go[p.w, chip, core, :, 192 * k : 192 * k + 192] = w_out[48 * k : 48 * k + 48].astype(BF16)

    lane = lax.broadcasted_iota(jnp.int32, (8, 128), 1)
    sub = lax.broadcasted_iota(jnp.int32, (8, 128), 0)
    here = 2 * p.s + sub % 2
    fixed = (jnp.abs(lane - here) <= 1).astype(F32) + (lane == 0).astype(F32) + (lane == 15).astype(F32)
    for v in range(2):
        for group in range(4):
            counts = fixed
            for row in range(6):
                head = 3 * group + row // 2
                for k in range(3):
                    drawn = rand_ids[v * 12 + head, 2 * k + row % 2]
                    counts = counts + ((sub == row) & (lane == drawn)).astype(F32)
            r.count_out[4 * v + group] = counts
    count_x.start()
    loads[4].wait()
    loads[5].wait()
    for half in range(2):
        for k in range(2):
            at, row = slice(192 * k, 192 * k + 192), 96 * k
            r.half_u[half, :, at] = w_up[:, 384 * k + 192 * half : 384 * k + 192 * half + 192].astype(BF16)
            r.half_d[half, :, at] = w_down[row : row + 96, 192 * half : 192 * half + 192].astype(BF16)
    r.gu[p.w, chip, core] = r.half_u[p.w % 2]
    r.gd[chip, core, p.w] = r.half_d[p.w % 2]
    gq0.stage1()
    loads[0].wait()
    hat, rstd = norm_stats(x[...].astype(F32))
    r.hat_a[...] = hat
    r.rstd_a[...] = rstd
    loads[1].wait()
    for v in range(2):
        rows = slice(128 * v, 128 * v + 128)
        r.gys[0, rows] = (d_out[rows].astype(F32) * live[v].astype(F32)).astype(BF16)
    gn.stage1()
    gq1.stage1()
    gq0.stage2()
    go.z_send()

    count_x.wait()
    spread = (
        lax.broadcasted_iota(jnp.int32, (128, 1024), 1) // 64 == lax.broadcasted_iota(jnp.int32, (128, 1024), 0)
    ).astype(BF16)
    wide = dot(r.counts[...].reshape(64, 128).astype(BF16), spread)
    wide = jnp.where(wide > 0.5, jnp.log(jnp.maximum(wide, 1.0)), NEG)
    for src in range(8):
        for head in range(3):
            row = src * 8 + head * 2
            at = 2 * (src % 2)
            r.bias[head, src // 2, at : at + 2] = wide[row : row + 2]

    gu0.z_send()
    gq2.stage1()
    gn.stage2()
    gq1.stage2()
    gq0.stage3()
    gn.stage3()
    gq2.stage2()
    gn.finish()
    mate_g.start()
    lane = lax.broadcasted_iota(jnp.int32, (128, 768), 1)
    sub = lax.broadcasted_iota(jnp.int32, (128, 768), 0)
    gains = jnp.zeros((32, 768), F32)
    for s in range(8):
        place = ((lane == sub + 96 * s) & (sub < 96)).astype(BF16)
        gains = gains + dot(r.gn[:, s // 2, s % 2].reshape(32, 128).astype(BF16), place)
    r.gains[...] = gains
    r.h[...] = (r.hat_a[...] * r.gains[0:1] + r.gains[8:9]).astype(BF16)
    go.stage1()
    gq1.stage3()
    gq2.stage3()
    gq0.finish()
    gu0.stage1()
    gd1.z_send()
    gq1.finish()
    gq2.finish()
    go.stage2()

    for w in range(4):
        part = dot(r.h[...], rows_of(r.gq, w, 768)).astype(BF16)
        for k in range(3):
            kind, group = divmod(3 * w + k, 4)
            for v in range(2):
                for j in range(2):
                    for head in range(3):
                        row, at, col = 128 * v + 64 * j, 192 * j + 64 * kind, 192 * k + 64 * head
                        r.sb[head, 4 * v + group, :, at : at + 64] = part[row : row + 64, col : col + 64]
    gu1.z_send()
    qkv_x[0].start()
    go.stage3()
    qkv_x[1].start()
    qkv_x[2].start()

    for head in range(3):
        qkv_x[head].wait()
        for src in range(8):
            for kind, ref in enumerate((r.qh, r.kh, r.vh)):
                for j in range(2):
                    row, at = 128 * src + 64 * j, 192 * j + 64 * kind
                    part = r.rb[head, src, :, at : at + 64]
                    ref[head, row : row + 64] = part * jnp.asarray(1.0 / math.sqrt(HD), BF16) if kind == 0 else part

        def attend(c, _, head=head):
            q0 = pl.multiple_of(c * 256, 256)
            raw = dot_nt(r.qh[head, pl.ds(q0, 256)], r.kh[head])
            score = (raw.reshape(4, 64, 1024) + r.bias[head, c][:, None, :]).reshape(256, 1024)
            weight = jnp.exp(score - jnp.max(score, axis=-1, keepdims=True))
            share = 1.0 / jnp.sum(weight, axis=-1, keepdims=True)
            weight = weight.astype(BF16)
            r.prob[head, pl.ds(q0, 256)] = weight
            r.share[head, pl.ds(q0, 256)] = share
            got = (dot(weight, r.vh[head]) * share).astype(BF16)
            r.kept_o[head, pl.ds(q0, 256)] = got
            got = got.reshape(2, 2, 64, 64)
            for j in range(2):
                at = 192 * j + 64 * head
                r.ab[pl.ds(2 * c, 2), :, at : at + 64] = got[:, j]
            return 0

        lax.fori_loop(0, 4, attend, 0, unroll=True)
        if head == 0:
            go.finish()
            gd0.z_send()
        if head == 1:
            gu1.stage1()
    att_x.start()
    gu0.stage2()
    gu1.stage2()
    for w in range(4):
        for k in range(2):
            r.wout[:, :, k, :, 192 * w : 192 * w + 192] = r.go[w, :, :, :, 192 * k : 192 * k + 192]
    gd0.stage1()
    mate_g.wait_recv()
    for k in range(2):
        r.turned_g[:, 256 * k : 256 * k + 256] = turned(r.gys[k])
    att_x.wait()
    for v in range(2):
        for group in range(4):
            for j in range(2):
                row = 128 * v + 64 * j
                r.att[row : row + 64, 192 * group : 192 * group + 192] = r.at[4 * v + group, :, 192 * j : 192 * j + 192]
    mid = x[...].astype(F32) + dot(r.att[...], r.wout[...].reshape(768, 768))
    r.y[0:256] = mid
    r.y[256:512] = jnp.zeros((256, 768), F32)
    hat, rstd = norm_stats(mid)
    r.hat_b[...] = hat
    r.rstd_b[...] = rstd
    r.hs[0] = (hat * r.gains[16:17] + r.gains[24:25]).astype(BF16)
    mate_h.start()
    gd0.stage2()
    gu1.stage3()
    gd1.stage1()
    gu0.stage3()
    r.back[...] = jnp.zeros((512, 768), F32)
    r.turned_h[:, 0:256] = turned(r.hs[0])
    gu0.finish()
    gu1.finish()

    def up_weights(f):
        return jnp.concatenate([rows_of(r.gu, 2 * f + k, 768) for k in range(2)], axis=1)

    for k in range(2):
        if k == 1:
            gd0.stage3()
            gd1.stage2()
            gd0.finish()
            mate_h.wait_recv()
            gd1.stage3()
            r.turned_h[:, 256:512] = turned(r.hs[1])

        def feed_up(f, _, k=k):
            up = dot(r.hs[k], up_weights(f))
            square = up * up
            bend = jnp.tanh(GELU_C * (up + 0.044715 * up * square))
            slope = 0.5 * (1.0 + bend) + 0.5 * up * (1.0 - bend * bend) * (GELU_C * (1.0 + 0.134145 * square))
            r.act[f, 256 * k : 256 * k + 256] = (0.5 * up * (1.0 + bend)).astype(BF16)
            r.slope[f, 256 * k : 256 * k + 256] = slope.astype(BF16)
            return 0

        lax.fori_loop(0, 2, feed_up, 0, unroll=True)
    gd1.finish()
    for g in gathers:
        g.drain()

    for f in range(4):
        for c in range(2):
            for j in range(2):
                at = 384 * (f % 2) + 192 * c
                r.wd[f // 2, :, j, :, at : at + 192] = r.gd[f, c, :, :, 192 * j : 192 * j + 192]
    for k in (1, 0):

        def feed_back(f, _, k=k):
            rows = slice(256 * k, 256 * k + 256)
            grad_up = (dot(r.gys[k], rows_of(r.wd, f, 768)) * r.slope[f, rows].astype(F32)).astype(BF16)
            r.slope[f, rows] = grad_up
            r.back[rows] += dot_nt(grad_up, up_weights(f))
            return 0

        lax.fori_loop(0, 2, feed_back, 0, unroll=True)
        if k == 1:
            r.back_out[...] = r.back[256:512].astype(BF16)
            mate_back.start()

    def feed_raw(k, _):
        f = p.chip(2 * k) // 2
        act = r.act[f]
        r.y[...] += dot_nt(act, rows_of(r.wd, f, 768))
        raw_down = dot(r.turned_g[...], act).astype(BF16).reshape(4, 2, 96, 768)
        for i in range(2):
            for c in range(2):
                for j in range(2):
                    at = 384 * i + 192 * c
                    r.gd[2 * f + i, c, :, :, 192 * j : 192 * j + 192] = raw_down[:, j, :, at : at + 192]
            sd0.stage_c_of(2 * f + i)
            sd1.stage_c_of(2 * f + i)
        raw_up = dot(r.turned_h[...], r.slope[f]).astype(BF16)
        for i in range(2):
            r.gu[2 * f + i] = raw_up[:, 384 * i : 384 * i + 384].reshape(4, 2, 96, 384)
        return 0

    lax.fori_loop(0, 2, feed_raw, 0, unroll=True)
    sd0.stage_d()
    r.turned[...] = turned(r.att[...])
    r.y_out[...] = r.y[256:512].astype(BF16)
    sd1.stage_d()
    r.turned_i[...] = turned(r.hat_a[...] * r.gains[0:1] + r.gains[8:9])
    su1.stage_c()
    mate_back.wait_recv()

    r.back[0:256] += r.back_in[...].astype(F32)
    mid_grad = norm_back(r.back[0:256], r.hat_b[...], r.rstd_b[...], r.gains[16:17])
    for v in range(2):
        rows = slice(128 * v, 128 * v + 128)
        r.mid_grad[rows] = mid_grad[rows] + d_out[rows].astype(F32) * live[v].astype(F32)
    r.hb[...] = r.mid_grad[...].astype(BF16)
    att_x.drain()
    grad_o = dot_nt(r.hb[...], r.wout[...].reshape(768, 768)).astype(BF16)
    for v in range(2):
        for group in range(4):
            for j in range(2):
                row = 128 * v + 64 * j
                r.ab[4 * v + group, :, 192 * j : 192 * j + 192] = grad_o[row : row + 64, 192 * group : 192 * group + 192]
    gro_x.start()
    r.rn[...] = jnp.zeros((4, 4, 2, 8, 128), F32)

    def put_norm(w, row):
        for s in range(8):
            r.rn[w, s // 2, s % 2, 0:1, 0:96] = row[:, 96 * s : 96 * s + 96]

    put_norm(2, jnp.sum(r.back[0:256] * r.hat_b[...], axis=0, keepdims=True))
    put_norm(3, jnp.sum(r.back[0:256], axis=0, keepdims=True))
    for w in range(4):
        raw = dot(r.turned[...], r.hb[:, 192 * w : 192 * w + 192]).astype(BF16).reshape(4, 2, 2, 48, 192)
        for k in range(2):
            r.go[w, :, :, :, 192 * k : 192 * k + 192] = raw[:, :, k]
    for exchange in qkv_x:
        exchange.drain()
    sd0.stage_e()
    sd1.stage_e()
    gro_x.wait()
    su1.stage_d()

    for head in range(3):
        r.gk[...] = jnp.zeros((64, 1024), F32)
        r.gv[...] = jnp.zeros((64, 1024), F32)

        def attend_back(c, _, head=head):
            q0 = pl.multiple_of(c * 256, 256)
            halves = []
            for j in range(2):
                at = 192 * j + 64 * head
                halves.append(r.gor[pl.ds(2 * c, 2), :, at : at + 64].reshape(2, 1, 64, 64))
            grad = jnp.concatenate(halves, axis=1).reshape(256, 64)
            grad = (grad.astype(F32) * r.share[head, pl.ds(q0, 256)]).astype(BF16)
            inner = jnp.sum(grad.astype(F32) * r.kept_o[head, pl.ds(q0, 256)].astype(F32), axis=-1, keepdims=True)
            weight = r.prob[head, pl.ds(q0, 256)]
            grad_s = (weight.astype(F32) * (dot_nt(grad, r.vh[head]) - inner)).astype(BF16)
            grad_q = (dot(grad_s, r.kh[head]) * (1.0 / math.sqrt(HD))).astype(BF16).reshape(2, 2, 64, 64)
            for j in range(2):
                r.sb[head, pl.ds(2 * c, 2), :, 192 * j : 192 * j + 64] = grad_q[:, j]
            r.gk[...] += dot_tn(r.qh[head, pl.ds(q0, 256)], grad_s)
            r.gv[...] += dot_tn(grad, weight)
            return 0

        lax.fori_loop(0, 4, attend_back, 0, unroll=True)
        for kind, grad in ((1, r.gk[...]), (2, r.gv[...])):
            grad = jnp.transpose(grad).astype(BF16).reshape(8, 2, 64, 64)
            for j in range(2):
                at = 192 * j + 64 * kind
                r.sb[head, :, :, at : at + 64] = grad[:, j]
        if head == 1:
            mate_y.start()
            sd1.stage_f()
            sd0.stage_f()
            so.stage_c()
        gqkv_x[head].start()
    su0.stage_c()
    su1.stage_e()
    r.back[0:256] = jnp.zeros((256, 768), F32)
    for head in range(3):
        gqkv_x[head].wait()
        for v in range(2):
            for group in range(4):
                for kind in range(3):
                    for j in range(2):
                        row, at, to = 128 * v + 64 * j, 192 * j + 64 * kind, 768 * kind + 192 * group + 64 * head
                        r.wide[row : row + 64, to : to + 64] = r.gb[head, 4 * v + group, :, at : at + 64]
        if head == 1:
            su0.stage_d()
    so.stage_d()
    for w in range(4):
        grad = r.wide[:, 576 * w : 576 * w + 576]
        r.back[0:256] += dot_nt(grad, rows_of(r.gq, w, 768))
        r.gq[w] = dot(r.turned_i[...], grad).astype(BF16).reshape(4, 2, 96, 576)
    sq2.stage_c()
    su0.stage_e()
    sq0.stage_c()
    sq2.stage_d()
    su1.stage_f()
    sq1.stage_c()
    grad_h = r.back[0:256]
    put_norm(0, jnp.sum(grad_h * r.hat_a[...], axis=0, keepdims=True))
    put_norm(1, jnp.sum(grad_h, axis=0, keepdims=True))
    so.stage_e()
    su0.stage_f()
    sq1.stage_d()

    def put_down(k, halves):
        for half, value in enumerate(halves):
            for j in range(2):
                row, at = 96 * j + 48 * k, 192 * half
                red_d[row : row + 48, at : at + 192] = value[:, 192 * j : 192 * j + 192]

    def put_up(k, halves):
        for half, value in enumerate(halves):
            for j in range(2):
                at = 384 * j + 192 * half
                red_u[48 * k : 48 * k + 48, at : at + 192] = value[:, 192 * j : 192 * j + 192]

    def squares(ref):
        return jnp.sum(ref[...] * ref[...])

    put_down(1, sd1.finish_halves())
    so.stage_f()
    sq0.stage_d()
    mate_y.wait_recv()
    output[...] = (r.y[0:256] + r.y_in[...].astype(F32)).astype(BF16)
    stores[0].start()
    sq2.stage_e()
    put_down(0, sd0.finish_halves())
    stores[5].start()
    red_o[...] = so.finish()
    stores[3].start()
    put_up(0, su0.finish_halves())
    sq1.stage_e()
    sn.stage_c()
    sq2.stage_f()
    sq0.stage_e()
    put_up(1, su1.finish_halves())
    stores[4].start()
    sn.stage_d()
    sq1.stage_f()
    red_q[64:96] = sq2.finish()
    sn.stage_e()
    local = squares(red_o) + squares(red_u) + squares(red_d)
    sq0.stage_f()
    d_input[...] = r.mid_grad[...] + norm_back(grad_h, r.hat_a[...], r.rstd_a[...], r.gains[0:1])
    stores[1].start()
    red_q[32:64] = sq1.finish()
    sn.stage_f()
    red_q[0:32] = sq0.finish()
    stores[2].start()
    red_n[...] = sn.finish()
    stores[6].start()
    local = jnp.zeros((8, 128), F32) + (local + squares(red_q) + squares(red_n))
    r.square[...] = local
    r.squares[0] = local

    def share(k):
        to = ((p.w + k // 8) % 4, (p.s + k % 8) % 8)
        return remote(r.square, r.squares.at[k], r.sum_sems, k, to)

    def share_start(k, _):
        share(k).start()
        return 0

    def share_wait(k, _):
        share(k).wait()
        return 0

    lax.fori_loop(1, 32, share_start, 0)
    for part in (count_x, gro_x, *gqkv_x, *scatters):
        part.drain()
    for copy in (mate_h, mate_g, mate_back, mate_y):
        copy.wait_send()
    lax.fori_loop(1, 32, share_wait, 0)
    total[...] = jnp.sum(r.squares[...], axis=0)
    stores[7].start()
    for copy in stores:
        copy.wait()


def adam_kernel(*refs):
    given, made, here, there, sems = refs[0:23], refs[23:46], refs[46:69], refs[69:90], refs[90]
    loads = [pltpu.make_async_copy(a, b, sems.at[k]) for k, (a, b) in enumerate(zip(given, here))]
    stores = [pltpu.make_async_copy(a, b, sems.at[23 + k]) for k, (a, b) in enumerate(zip((*there, *here[21:23]), made))]
    order = (2, 3, 0, 1, 4)
    loads[20].start()
    for k in order:
        for part in range(4):
            loads[5 * part + k].start()
    for k in (22, 21):
        loads[k].start()
    fix_one = 1.0 - beta_one**STEP
    fix_two = 1.0 - beta_two**STEP
    rates = (rate_matrix, rate_output, rate_matrix, rate_matrix, rate_norm)
    loads[20].wait()
    norm = jnp.sqrt(here[20][0:1, 0:1])
    factor = 1.0 / jnp.maximum(norm, 1.0)
    there[20][...] = norm
    stores[20].start()
    for k in order:
        for part in range(4):
            loads[5 * part + k].wait()
        raw = here[k][...]
        if k == 1:
            raw = jnp.concatenate([raw[:, 0:192], raw[:, 192:384]], axis=0)
        if k == 4:
            raw = raw[0:1, 0:96]
        grad = raw * factor
        weight = here[5 + k][...]
        first = beta_one * here[10 + k][...] + (1.0 - beta_one) * grad
        second = beta_two * here[15 + k][...] + (1.0 - beta_two) * grad * grad
        stride = first / fix_one / (jnp.sqrt(second / fix_two) + adam_eps)
        decay = 0.0 if k == 4 else decay_rate
        there[k][...] = grad
        there[5 + k][...] = weight - rates[k] * (stride + decay * weight)
        there[10 + k][...] = first
        there[15 + k][...] = second
        for part in range(4):
            stores[5 * part + k].start()
        if k == 2:
            for j in (22, 21):
                loads[j].wait()
                stores[j].start()
    for copy in stores:
        copy.wait()


def fused_device(
    layer_input, d_out, rand_ids, live_mask, w_qkv, w_out, w_up, w_down, norm_params,
    m_qkv, m_out, m_up, m_down, m_norm, v_qkv, v_out, v_up, v_down, v_norm,
):
    smem, anywhere = (pl.BlockSpec(memory_space=kind) for kind in (pltpu.SMEM, pl.ANY))
    ids = rand_ids.transpose(0, 2, 3, 1).reshape(24, 6)
    leaves, tree = jax.tree.flatten(scratch())
    shape = jax.ShapeDtypeStruct
    output, d_input, *grads, total = pl.pallas_call(
        functools.partial(kernel, tree),
        out_shape=[shape(*leaf) for leaf in KEPT],
        in_specs=[smem, smem] + [anywhere] * 7,
        out_specs=[anywhere] * 8,
        scratch_shapes=leaves,
        compiler_params=pltpu.CompilerParams(collective_id=0, has_side_effects=True, vmem_limit_bytes=VMEM_LIMIT),
    )(
        live_mask, ids, layer_input.reshape(256, 768), d_out.reshape(256, 768), w_qkv, w_out, w_up, w_down.T,
        norm_params.reshape(1, 96),
    )
    state = (
        *grads,
        w_qkv, w_out, w_up, w_down.T, norm_params.reshape(1, 96),
        m_qkv, m_out, m_up, m_down.T, m_norm.reshape(1, 96),
        v_qkv, v_out, v_up, v_down.T, v_norm.reshape(1, 96),
        total, output, d_input,
    )
    results = [shape(w.shape, F32) for w in state[5:10]] * 4
    results += [shape((1, 1), F32), shape(output.shape, BF16), shape(d_input.shape, F32)]
    made = pl.pallas_call(
        adam_kernel,
        out_shape=results,
        in_specs=[anywhere] * 23,
        out_specs=[anywhere] * 23,
        scratch_shapes=[pltpu.VMEM(a.shape, a.dtype) for a in (*state, *results[:21])] + [pltpu.SemaphoreType.DMA((46,))],
        compiler_params=pltpu.CompilerParams(vmem_limit_bytes=VMEM_LIMIT),
    )(*state)
    updated = [m.T if k % 5 == 3 else m.reshape(-1) if k % 5 == 4 else m for k, m in enumerate(made[:20])]
    return (made[21].reshape(2, 128, 768), made[22].reshape(2, 128, 768), *updated, made[20].reshape(1))


def solution(mesh):
    placed = (
        P("win", "seq", None),
        P("win", "seq", None),
        P("win", "seq", None, None),
        P("win"),
        P("seq", "win"),
        P("seq", "win"),
        P("seq", "win"),
        P("seq", "win"),
        P(("win", "seq")),
        P("seq", "win"),
        P("seq", "win"),
        P("seq", "win"),
        P("seq", "win"),
        P(("win", "seq")),
        P("seq", "win"),
        P("seq", "win"),
        P("seq", "win"),
        P("seq", "win"),
        P(("win", "seq")),
    )
    fused = mesh.shape["win"] == 4 and mesh.shape["seq"] == 8
    return jax.shard_map(
        fused_device if fused else per_device,
        mesh=mesh,
        in_specs=placed,
        out_specs=(
            P("win", "seq", None),
            P("win", "seq", None),
            P("seq", "win"),
            P("seq", "win"),
            P("seq", "win"),
            P("seq", "win"),
            P(("win", "seq")),
            P("seq", "win"),
            P("seq", "win"),
            P("seq", "win"),
            P("seq", "win"),
            P(("win", "seq")),
            P("seq", "win"),
            P("seq", "win"),
            P("seq", "win"),
            P("seq", "win"),
            P(("win", "seq")),
            P("seq", "win"),
            P("seq", "win"),
            P("seq", "win"),
            P("seq", "win"),
            P(("win", "seq")),
            P(),
        ),
        check_vma=False,
    )
```

```python
import functools
import math
from typing import Any, NamedTuple

import jax
import jax.numpy as jnp
from jax import lax
from jax.experimental import pallas as pl
from jax.experimental.pallas import tpu as pltpu
from jax.sharding import PartitionSpec as P

H = 12
HD = 64
BLK = 64
STEP = 3


NEG = -1e30
ln_eps = 1e-05
beta_one = 0.5
beta_two = 0.5
adam_eps = 1e-08
decay_rate = 0.1
rate_matrix = 0.04
rate_output = 0.16
rate_norm = 0.6
VMEM_LIMIT = 63 << 20


def layer_norm(values, gain, shift):
    centre = values - jnp.mean(values, axis=-1, keepdims=True)
    spread = jnp.mean(centre * centre, axis=-1, keepdims=True)
    return centre * lax.rsqrt(spread + ln_eps) * gain + shift


def slot_counts(rand_ids, first_block, block_count):
    blocks_dev = rand_ids.shape[1]
    here = (first_block + jnp.arange(blocks_dev, dtype=jnp.int32))[:, None]
    every = jnp.arange(block_count, dtype=jnp.int32)[None, :]
    near = (jnp.abs(here - every) <= 1).astype(jnp.float32)
    ends = (every == 0).astype(jnp.float32) + (every == block_count - 1).astype(jnp.float32)
    drawn = jnp.sum((rand_ids[..., None] == every[0]).astype(jnp.float32), axis=3)
    return (near + ends)[None, :, None, :] + drawn


def adam_update(weight, grad, first, second, rate, decay, fix_one, fix_two):
    first_new = beta_one * first + (1.0 - beta_one) * grad
    second_new = beta_two * second + (1.0 - beta_two) * grad * grad
    stride = first_new / fix_one / (jnp.sqrt(second_new / fix_two) + adam_eps)
    return (weight - rate * (stride + decay * weight), first_new, second_new)


def per_device(
    layer_input,
    d_out,
    rand_ids,
    live_mask,
    w_qkv,
    w_out,
    w_up,
    w_down,
    norm_params,
    m_qkv,
    m_out,
    m_up,
    m_down,
    m_norm,
    v_qkv,
    v_out,
    v_up,
    v_down,
    v_norm,
):
    wins, local_len, width = layer_input.shape
    blocks_dev = local_len // BLK
    block_count = blocks_dev * lax.axis_size("seq")
    first_block = lax.axis_index("seq") * blocks_dev
    inv_root = 1.0 / math.sqrt(HD)
    rows = wins * local_len
    low_qkv = w_qkv.astype(jnp.bfloat16)
    low_out = w_out.astype(jnp.bfloat16)
    low_up = w_up.astype(jnp.bfloat16)
    low_down = w_down.astype(jnp.bfloat16)
    low_norm = norm_params.astype(jnp.bfloat16)
    full_qkv, full_out, full_up, full_down = (
        lax.all_gather(lax.all_gather(low, "win", axis=1, tiled=True), "seq", axis=0, tiled=True)
        for low in (low_qkv, low_out, low_up, low_down)
    )
    full_norm = lax.all_gather(low_norm, ("win", "seq"), axis=0, tiled=True)
    gains = full_norm.astype(jnp.float32).reshape(4, width)
    loss_weight = live_mask.astype(jnp.float32)
    counts = slot_counts(rand_ids, first_block, block_count)
    bias = jnp.where(counts > 0, jnp.log(jnp.maximum(counts, 1.0)), NEG)
    bias = jnp.repeat(bias, BLK, axis=3)[:, :, :, None, :]
    tokens = layer_input.astype(jnp.float32).reshape(rows, width)
    h_one = layer_norm(tokens, gains[0], gains[1]).astype(jnp.bfloat16)
    qkv = jnp.dot(h_one, full_qkv, preferred_element_type=jnp.float32)
    q_heads = qkv[:, :width].astype(jnp.bfloat16).reshape(wins, blocks_dev, BLK, H, HD)
    keyval = qkv[:, width:].astype(jnp.bfloat16).reshape(wins, local_len, 2 * width)
    window = lax.all_gather(keyval, "seq", axis=1, tiled=True)
    shaped = window.reshape(wins, block_count * BLK, 2, H, HD)
    keys, values = shaped[:, :, 0], shaped[:, :, 1]
    scores = (
        jnp.einsum("wbqhd,wkhd->wbhqk", q_heads, keys, preferred_element_type=jnp.float32)
        * inv_root
        + bias
    )
    top = jnp.max(scores, axis=-1, keepdims=True)
    log_total = top + jnp.log(jnp.sum(jnp.exp(scores - top), axis=-1, keepdims=True))
    prob = jnp.exp(scores - log_total).astype(jnp.bfloat16)
    heads_out = jnp.einsum("wbhqk,wkhd->wbqhd", prob, values, preferred_element_type=jnp.float32)
    attended = heads_out.astype(jnp.bfloat16).reshape(rows, width)
    middle = tokens + jnp.dot(attended, full_out, preferred_element_type=jnp.float32)
    h_two = layer_norm(middle, gains[2], gains[3]).astype(jnp.bfloat16)
    up_proj = jnp.dot(h_two, full_up, preferred_element_type=jnp.float32)
    active = jax.nn.gelu(up_proj).astype(jnp.bfloat16)
    result = middle + jnp.dot(active, full_down, preferred_element_type=jnp.float32)
    output = result.astype(jnp.bfloat16).reshape(wins, local_len, width)
    grad_y = (d_out.astype(jnp.float32) * loss_weight[:, None, None]).reshape(rows, width)
    grad_ffn = grad_y.astype(jnp.bfloat16)
    raw_down = jnp.einsum("tf,td->fd", active, grad_ffn, preferred_element_type=jnp.float32)
    grad_act = jnp.einsum("td,fd->tf", grad_ffn, full_down, preferred_element_type=jnp.float32)
    gelu_pull = jax.vjp(jax.nn.gelu, up_proj)[1]
    grad_up = gelu_pull(grad_act)[0].astype(jnp.bfloat16)
    raw_up = jnp.einsum("td,tf->df", h_two, grad_up, preferred_element_type=jnp.float32)
    grad_h_two = jnp.einsum("tf,df->td", grad_up, full_up, preferred_element_type=jnp.float32)
    norm_pull = jax.vjp(layer_norm, middle, gains[2], gains[3])[1]
    grad_mid_ln, raw_gain_two, raw_shift_two = norm_pull(grad_h_two)
    grad_mid = grad_y + grad_mid_ln
    grad_att = grad_mid.astype(jnp.bfloat16)
    raw_out = jnp.einsum("td,te->de", attended, grad_att, preferred_element_type=jnp.float32)
    grad_o = jnp.einsum("te,de->td", grad_att, full_out, preferred_element_type=jnp.float32)
    grad_o = grad_o.astype(jnp.bfloat16).reshape(wins, blocks_dev, BLK, H, HD)
    grad_p = jnp.einsum("wbqhd,wkhd->wbhqk", grad_o, values, preferred_element_type=jnp.float32)
    prob_f = prob.astype(jnp.float32)
    inner = jnp.sum(prob_f * grad_p, axis=-1, keepdims=True)
    grad_s = (prob_f * (grad_p - inner)).astype(jnp.bfloat16)
    grad_q = (
        jnp.einsum("wbhqk,wkhd->wbqhd", grad_s, keys, preferred_element_type=jnp.float32)
        * inv_root
    )
    grad_v = jnp.einsum("wbhqk,wbqhd->wkhd", prob, grad_o, preferred_element_type=jnp.float32)
    grad_k = (
        jnp.einsum("wbhqk,wbqhd->wkhd", grad_s, q_heads, preferred_element_type=jnp.float32)
        * inv_root
    )
    grad_kv = jnp.stack([grad_k, grad_v], axis=2).astype(jnp.bfloat16)
    grad_kv = lax.psum_scatter(
        grad_kv.reshape(wins, block_count * BLK, 2 * width),
        "seq",
        scatter_dimension=1,
        tiled=True,
    ).reshape(rows, 2 * width)
    grad_qkv = jnp.concatenate(
        [grad_q.reshape(rows, width).astype(jnp.bfloat16), grad_kv], axis=1
    )
    raw_qkv = jnp.einsum("td,te->de", h_one, grad_qkv, preferred_element_type=jnp.float32)
    grad_h_one = jnp.einsum("te,de->td", grad_qkv, full_qkv, preferred_element_type=jnp.float32)
    first_pull = jax.vjp(layer_norm, tokens, gains[0], gains[1])[1]
    grad_tok_ln, raw_gain_one, raw_shift_one = first_pull(grad_h_one)
    d_input = (grad_mid + grad_tok_ln).reshape(wins, local_len, width)
    raw_norm = jnp.concatenate([raw_gain_one, raw_shift_one, raw_gain_two, raw_shift_two])
    red_qkv, red_out, red_up, red_down = (
        lax.psum_scatter(
            lax.psum_scatter(raw.astype(jnp.bfloat16), "seq", scatter_dimension=0, tiled=True),
            "win",
            scatter_dimension=1,
            tiled=True,
        ).astype(jnp.float32)
        for raw in (raw_qkv, raw_out, raw_up, raw_down)
    )
    red_norm = lax.psum_scatter(raw_norm, ("win", "seq"), scatter_dimension=0, tiled=True)
    reduced = (red_qkv, red_out, red_up, red_down, red_norm)
    local_squares = jnp.float32(0.0)
    for grad in reduced:
        local_squares = local_squares + jnp.sum(grad * grad)
    grad_norm = jnp.sqrt(lax.psum(local_squares, ("win", "seq")))
    factor = 1.0 / jnp.maximum(grad_norm, 1.0)
    clipped = tuple((grad * factor for grad in reduced))
    count = jnp.float32(STEP)
    fix_one = 1.0 - jnp.power(jnp.float32(beta_one), count)
    fix_two = 1.0 - jnp.power(jnp.float32(beta_two), count)
    params = (w_qkv, w_out, w_up, w_down, norm_params)
    firsts = (m_qkv, m_out, m_up, m_down, m_norm)
    seconds = (v_qkv, v_out, v_up, v_down, v_norm)
    rates = (rate_matrix, rate_output, rate_matrix, rate_matrix, rate_norm)
    news, moms, secs = ([], [], [])
    for index in range(5):
        decay = 0.0 if index == 4 else decay_rate
        new_w, new_m, new_v = adam_update(
            params[index],
            clipped[index],
            firsts[index],
            seconds[index],
            rates[index],
            decay,
            fix_one,
            fix_two,
        )
        news.append(new_w)
        moms.append(new_m)
        secs.append(new_v)
    return (
        output,
        d_input,
        clipped[0],
        clipped[1],
        clipped[2],
        clipped[3],
        clipped[4],
        news[0],
        news[1],
        news[2],
        news[3],
        news[4],
        moms[0],
        moms[1],
        moms[2],
        moms[3],
        moms[4],
        secs[0],
        secs[1],
        secs[2],
        secs[3],
        secs[4],
        grad_norm.reshape(1),
    )


MESH = pl.DeviceIdType.MESH
F32, BF16 = jnp.float32, jnp.bfloat16
GELU_C = math.sqrt(2.0 / math.pi)
NT = (((1,), (1,)), ((), ()))
TN = (((0,), (0,)), ((), ()))


def dot(a, b):
    return jnp.dot(a, b, preferred_element_type=F32)


def dot_nt(a, b):
    return lax.dot_general(a, b, NT, preferred_element_type=F32)


def dot_tn(a, b):
    return lax.dot_general(a, b, TN, preferred_element_type=F32)


def remote(src, dst, sems, k, dev):
    return pltpu.make_async_remote_copy(
        src_ref=src, dst_ref=dst, send_sem=sems[0].at[k], recv_sem=sems[1].at[k], device_id=dev, device_id_type=MESH
    )


class Place:
    def __init__(self):
        self.w = lax.axis_index("win")
        self.s = s = lax.axis_index("seq")
        self.c = c = s % 2
        x = (s // 2) % 2
        y = s // 4
        dx, dy = 2 - 4 * x, 4 - 8 * y
        self.turn = 1 - 2 * c
        self.n1 = s + (1 - c) * dx + c * dy
        self.n2 = s + (1 - c) * dy + c * dx
        self.nd = s + dx + dy
        self.par = s + self.turn
        self.roles = (s, self.n1, self.n2, self.nd)
        self.par_roles = tuple(r + self.turn for r in (s, self.n2, self.n1, self.nd))
        self.x, self.y = x, y
        self.mate = (self.w + 1 - 2 * (self.w % 2), s)

    def chip(self, k):
        x = self.x + (1 - k % 2) * (1 - 2 * self.x)
        y = self.y + (1 - k // 2) * (1 - 2 * self.y)
        return 2 * y + x

    def role_for_partner(self, chip):
        dx = (chip % 2 - self.x) * (chip % 2 - self.x)
        dy = (chip // 2 - self.y) * (chip // 2 - self.y)
        return self.c * (dx + 2 * dy) + (1 - self.c) * (dy + 2 * dx)


class Blocks:
    def __init__(self, buf, seq_first=False, start=0, count=None):
        self.buf, self.seq_first, self.rows = buf, seq_first, pl.ds(start, buf.shape[3] if count is None else count)

    def block(self, w, s):
        return self.buf.at[(s // 2, s % 2, w, self.rows) if self.seq_first else (w, s // 2, s % 2, self.rows)]

    def read(self, w, s):
        return self.buf[(s // 2, s % 2, w, self.rows) if self.seq_first else (w, s // 2, s % 2, self.rows)]

    def group(self, s):
        every = slice(None)
        return self.buf.at[(s // 2, s % 2, every, self.rows) if self.seq_first else (every, s // 2, s % 2, self.rows)]


class Gather:
    def __init__(self, place, blocks, sems, staged=None):
        self.p, self.b, self.sems, self.staged = place, blocks, sems, staged

    def push(self, s, k, to):
        remote(self.b.group(s), self.b.group(s), self.sems, k, (self.p.w, to)).start()

    def got(self, s, k):
        remote(self.b.group(s), self.b.group(s), self.sems, k, (self.p.w, self.p.par)).wait_recv()

    def along(self, dz, w):
        p, block = self.p, self.b.block(w, self.p.s)
        source = block if self.staged is None else self.staged.at[(p.w + dz) % 2, self.b.rows]
        return remote(source, block, self.sems, dz - 1, ((p.w + dz) % 4, p.s))

    def z_send(self):
        for dz in (1, 2, 3):
            self.along(dz, self.p.w).start()

    def stage1(self):
        p = self.p
        for dz in (1, 2, 3):
            self.along(dz, (p.w + 4 - dz) % 4).wait_recv()
        self.push(p.s, 3, p.n1)
        self.push(p.s, 4, p.n2)
        self.push(p.s, 6, p.par)

    def stage2(self):
        p = self.p
        self.got(p.n1, 3)
        self.push(p.n1, 5, p.n2)
        self.push(p.n1, 7, p.par)

    def stage3(self):
        p = self.p
        self.got(p.n2, 4)
        self.push(p.n2, 8, p.par)
        self.got(p.nd, 5)
        self.push(p.nd, 9, p.par)

    def finish(self):
        for k in range(4):
            self.got(self.p.par_roles[k], 6 + k)

    def drain(self):
        p = self.p
        for dz in (1, 2, 3):
            self.along(dz, p.w).wait_send()
        for k, s in ((3, p.s), (4, p.s), (6, p.s), (5, p.n1), (7, p.n1), (8, p.n2), (9, p.nd)):
            remote(self.b.group(s), self.b.group(s), self.sems, k, (p.w, p.par)).wait_send()


class Scatter:
    def __init__(self, place, blocks, space, sems):
        self.p, self.b, self.sems = place, blocks, sems
        self.c, self.d, self.e, self.f = space

    def copies_c(self):
        p = self.p
        return [remote(self.b.group(p.par_roles[k]), self.c.at[k], self.sems, k, (p.w, p.par)) for k in range(4)]

    def copies_d(self):
        p = self.p
        return [remote(self.c.at[2 + k], self.d.at[k], self.sems, 4 + k, (p.w, p.n2)) for k in range(2)]

    def copy_e(self):
        p = self.p
        return remote(self.c.at[1], self.e, self.sems, 6, (p.w, p.n1))

    def copies_f(self):
        p = self.p
        return [
            remote(self.c.at[0, (p.w + dz) % 4], self.f.at[dz - 1], self.sems, 6 + dz, ((p.w + dz) % 4, p.s))
            for dz in (1, 2, 3)
        ]

    def add(self, k, term):
        def one(w, _):
            self.c[k, w] = self.c[k, w] + term(w)
            return 0

        lax.fori_loop(0, 4, one, 0)

    def stage_c(self):
        for copy in self.copies_c():
            copy.start()

    def stage_c_of(self, chip):
        p = self.p
        role = p.role_for_partner(chip)
        remote(self.b.group(2 * chip + 1 - p.c), self.c.at[role], self.sems, role, (p.w, p.par)).start()

    def stage_d(self):
        waits, sends = self.copies_c(), self.copies_d()
        for k in (2, 3, 0, 1):
            waits[k].wait_recv()
            self.add(k, lambda w, k=k: self.b.read(w, self.p.roles[k]))
            if k >= 2:
                sends[k - 2].start()

    def stage_e(self):
        waits = self.copies_d()
        for k in (1, 0):
            waits[k].wait_recv()
            self.add(k, lambda w, k=k: self.d[k, w])
            if k == 1:
                self.copy_e().start()

    def stage_f(self):
        self.copy_e().wait_recv()
        self.add(0, lambda w: self.e[w])
        for copy in self.copies_f():
            copy.start()

    def finish(self):
        total = self.c[0, self.p.w].astype(F32)
        for k, copy in enumerate(self.copies_f()):
            copy.wait_recv()
            total = total + self.f[k].astype(F32)
        return total

    def finish_halves(self):
        p = self.p
        for copy in self.copies_f():
            copy.wait_recv()
        alike = self.c[0, p.w].astype(F32) + self.f[1].astype(F32)
        other = self.f[0].astype(F32) + self.f[2].astype(F32)
        even = p.w % 2 == 0
        return jnp.where(even, alike, other), jnp.where(even, other, alike)

    def drain(self):
        for copy in (*self.copies_c(), *self.copies_d(), self.copy_e(), *self.copies_f()):
            copy.wait_send()


class Exchange:
    def __init__(self, place, src, dst, sems):
        self.p, self.src, self.dst, self.sems = place, src, dst, sems

    def copy(self, ds):
        p = self.p
        to = (p.s + ds) % 8
        return remote(self.src.at[to], self.dst.at[p.s], self.sems, ds, (p.w, to))

    def own(self):
        return pltpu.make_async_copy(self.src.at[self.p.s], self.dst.at[self.p.s], self.sems[1].at[0])

    def start(self):
        for ds in (6, 5, 3, 7, 4, 2, 1):
            self.copy(ds).start()
        self.own().start()

    def wait(self):
        p = self.p
        self.own().wait()
        for ds in range(1, 8):
            back = (p.s + 8 - ds) % 8
            remote(self.src.at[back], self.dst.at[back], self.sems, ds, (p.w, back)).wait_recv()

    def drain(self):
        for ds in range(1, 8):
            self.copy(ds).wait_send()


def norm_stats(values):
    centre = values - jnp.mean(values, axis=-1, keepdims=True)
    rstd = lax.rsqrt(jnp.mean(centre * centre, axis=-1, keepdims=True) + ln_eps)
    return centre * rstd, rstd


def norm_back(grad, hat, rstd, gain):
    scaled = grad * gain
    return rstd * (
        scaled - jnp.mean(scaled, axis=-1, keepdims=True) - hat * jnp.mean(scaled * hat, axis=-1, keepdims=True)
    )


def rows_of(ref, index, rows):
    value = ref[index]
    return value.reshape(rows, value.shape[-1])


def turned(value):
    return jnp.transpose(value.astype(F32)).astype(BF16)


GIVEN = (
    ((256, 768), BF16), ((256, 768), BF16), ((96, 576), F32), ((96, 192), F32), ((96, 768), F32), ((192, 384), F32), ((1, 96), F32),
)
KEPT = (
    ((256, 768), BF16), ((256, 768), F32), ((96, 576), F32), ((48, 384), F32), ((96, 768), F32), ((192, 384), F32), ((8, 128), F32), ((8, 128), F32),
)


class Space(NamedTuple):
    gn: Any
    gq: Any
    go: Any
    gu: Any
    gd: Any
    rn: Any
    sn: Any
    sq: Any
    so: Any
    su: Any
    sd: Any
    half_u: Any
    half_d: Any
    wd: Any
    gather_sems: Any
    scatter_sems: Any
    exchange_sems: Any
    sum_sems: Any
    count_out: Any
    counts: Any
    bias: Any
    sb: Any
    rb: Any
    qh: Any
    kh: Any
    vh: Any
    prob: Any
    share: Any
    kept_o: Any
    ab: Any
    at: Any
    gor: Any
    gb: Any
    att: Any
    wout: Any
    turned: Any
    turned_i: Any
    turned_h: Any
    turned_g: Any
    gains: Any
    hat_a: Any
    hat_b: Any
    rstd_a: Any
    rstd_b: Any
    h: Any
    hb: Any
    hs: Any
    gys: Any
    back_out: Any
    back_in: Any
    y_out: Any
    y_in: Any
    mate_sems: Any
    wide: Any
    y: Any
    back: Any
    mid_grad: Any
    gk: Any
    gv: Any
    act: Any
    slope: Any
    square: Any
    squares: Any
    given: Any
    kept: Any
    io_sems: Any


def scratch():
    def scatter(*block, kind=BF16):
        return tuple(pltpu.VMEM((*lead, *block), kind) for lead in ((4, 4), (2, 4), (4,), (3,)))

    def sems(count):
        return (pltpu.SemaphoreType.DMA((count,)),) * 2

    rows, wide = (256, 768), (3, 8, 64, 384)
    return Space(
        gn=pltpu.VMEM((4, 4, 2, 8, 128), F32),
        gq=pltpu.VMEM((4, 4, 2, 96, 576), BF16),
        go=pltpu.VMEM((4, 4, 2, 48, 384), BF16),
        gu=pltpu.VMEM((4, 4, 2, 96, 384), BF16),
        gd=pltpu.VMEM((4, 2, 4, 96, 384), BF16),
        rn=pltpu.VMEM((4, 4, 2, 8, 128), F32),
        sn=scatter(8, 128, kind=F32),
        sq=tuple(scatter(32, 576) for _ in range(3)),
        so=scatter(48, 384),
        su=tuple(scatter(48, 384) for _ in range(2)),
        sd=tuple(scatter(48, 384) for _ in range(2)),
        half_u=pltpu.VMEM((2, 96, 384), BF16),
        half_d=pltpu.VMEM((2, 96, 384), BF16),
        wd=pltpu.VMEM((2, 4, 2, 96, 768), BF16),
        gather_sems=tuple(sems(10) for _ in range(9)),
        scatter_sems=tuple(sems(10) for _ in range(9)),
        exchange_sems=tuple(sems(8) for _ in range(9)),
        sum_sems=sems(32),
        count_out=pltpu.VMEM((8, 8, 128), F32),
        counts=pltpu.VMEM((8, 8, 128), F32),
        bias=pltpu.VMEM((3, 4, 4, 1024), F32),
        sb=pltpu.VMEM(wide, BF16),
        rb=pltpu.VMEM(wide, BF16),
        qh=pltpu.VMEM((3, 1024, 64), BF16),
        kh=pltpu.VMEM((3, 1024, 64), BF16),
        vh=pltpu.VMEM((3, 1024, 64), BF16),
        prob=pltpu.VMEM((3, 1024, 1024), BF16),
        share=pltpu.VMEM((3, 1024, 1), F32),
        kept_o=pltpu.VMEM((3, 1024, 64), BF16),
        ab=pltpu.VMEM((8, 64, 384), BF16),
        at=pltpu.VMEM((8, 64, 384), BF16),
        gor=pltpu.VMEM((8, 64, 384), BF16),
        gb=pltpu.VMEM(wide, BF16),
        att=pltpu.VMEM(rows, BF16),
        wout=pltpu.VMEM((4, 2, 2, 48, 768), BF16),
        turned=pltpu.VMEM((768, 256), BF16),
        turned_i=pltpu.VMEM((768, 256), BF16),
        turned_h=pltpu.VMEM((768, 512), BF16),
        turned_g=pltpu.VMEM((768, 512), BF16),
        gains=pltpu.VMEM((32, 768), F32),
        hat_a=pltpu.VMEM(rows, F32),
        hat_b=pltpu.VMEM(rows, F32),
        rstd_a=pltpu.VMEM((256, 1), F32),
        rstd_b=pltpu.VMEM((256, 1), F32),
        h=pltpu.VMEM(rows, BF16),
        hb=pltpu.VMEM(rows, BF16),
        hs=pltpu.VMEM((2, *rows), BF16),
        gys=pltpu.VMEM((2, *rows), BF16),
        back_out=pltpu.VMEM(rows, BF16),
        back_in=pltpu.VMEM(rows, BF16),
        y_out=pltpu.VMEM(rows, BF16),
        y_in=pltpu.VMEM(rows, BF16),
        mate_sems=sems(4),
        wide=pltpu.VMEM((256, 2304), BF16),
        y=pltpu.VMEM((512, 768), F32),
        back=pltpu.VMEM((512, 768), F32),
        mid_grad=pltpu.VMEM(rows, F32),
        gk=pltpu.VMEM((64, 1024), F32),
        gv=pltpu.VMEM((64, 1024), F32),
        act=pltpu.VMEM((2, 512, 768), BF16),
        slope=pltpu.VMEM((2, 512, 768), BF16),
        square=pltpu.VMEM((8, 128), F32),
        squares=pltpu.VMEM((32, 8, 128), F32),
        given=tuple(pltpu.VMEM(dims, kind) for dims, kind in GIVEN),
        kept=tuple(pltpu.VMEM(dims, kind) for dims, kind in KEPT),
        io_sems=pltpu.SemaphoreType.DMA((15,)),
    )


def kernel(tree, live, rand_ids, *refs):
    r = jax.tree.unflatten(tree, refs[15:])
    x, d_out, w_qkv, w_out, w_up, w_down, norm = r.given
    output, d_input, red_q, red_o, red_u, red_d, red_n, total = r.kept
    loads = [pltpu.make_async_copy(a, b, r.io_sems.at[k]) for k, (a, b) in enumerate(zip(refs[:7], r.given))]
    stores = [pltpu.make_async_copy(a, b, r.io_sems.at[7 + k]) for k, (a, b) in enumerate(zip(r.kept, refs[7:15]))]
    for k in (6, 2, 5, 3, 4, 0, 1):
        loads[k].start()
    p = Place()
    barrier = pltpu.get_barrier_semaphore()

    def greet(k, _):
        to = ((p.w + k // 8) % 4, (p.s + k % 8) % 8)
        pl.semaphore_signal(barrier, inc=1, device_id=to, device_id_type=MESH)
        return 0

    lax.fori_loop(1, 32, greet, 0)

    blocks_q = [Blocks(r.gq, start=32 * k, count=32) for k in range(3)]
    blocks_u = [Blocks(r.gu, start=48 * k, count=48) for k in range(2)]
    blocks_d = [Blocks(r.gd, True, start=48 * k, count=48) for k in range(2)]
    every = (*blocks_q, Blocks(r.go), *blocks_u, *blocks_d)
    staged = (None,) * 4 + (r.half_u,) * 2 + (r.half_d,) * 2
    gathers = [Gather(p, Blocks(r.gn), r.gather_sems[8])]
    gathers += [Gather(p, b, m, half) for b, m, half in zip(every, r.gather_sems, staged)]
    gn, gq0, gq1, gq2, go, gu0, gu1, gd0, gd1 = gathers
    scatters = [Scatter(p, Blocks(r.rn), r.sn, r.scatter_sems[8])]
    scatters += [Scatter(p, b, space, m) for b, space, m in zip(every, (*r.sq, r.so, *r.su, *r.sd), r.scatter_sems)]
    sn, sq0, sq1, sq2, so, su0, su1, sd0, sd1 = scatters
    mate_h = remote(r.hs.at[0], r.hs.at[1], r.mate_sems, 0, p.mate)
    mate_g = remote(r.gys.at[0], r.gys.at[1], r.mate_sems, 1, p.mate)
    mate_back = remote(r.back_out, r.back_in, r.mate_sems, 2, p.mate)
    mate_y = remote(r.y_out, r.y_in, r.mate_sems, 3, p.mate)
    count_x = Exchange(p, r.count_out, r.counts, r.exchange_sems[0])
    att_x = Exchange(p, r.ab, r.at, r.exchange_sems[1])
    gro_x = Exchange(p, r.ab, r.gor, r.exchange_sems[2])
    qkv_x = [Exchange(p, r.sb.at[h], r.rb.at[h], r.exchange_sems[3 + h]) for h in range(3)]
    gqkv_x = [Exchange(p, r.sb.at[h], r.gb.at[h], r.exchange_sems[6 + h]) for h in range(3)]
    chip, core = p.s // 2, p.c

    r.gn[p.w, chip, core] = jnp.zeros((8, 128), F32)
    loads[6].wait()
    r.gn[p.w, chip, core, 0:1, 0:96] = norm[...].astype(BF16).astype(F32)
    loads[2].wait()
    r.gq[p.w, chip, core] = w_qkv[...].astype(BF16)
    pl.semaphore_wait(barrier, 31)
    gq0.z_send()
    gn.z_send()
    gq1.z_send()
    gq2.z_send()
    loads[3].wait()
    for k in range(2):
        r.go[p.w, chip, core, :, 192 * k : 192 * k + 192] = w_out[48 * k : 48 * k + 48].astype(BF16)

    lane = lax.broadcasted_iota(jnp.int32, (8, 128), 1)
    sub = lax.broadcasted_iota(jnp.int32, (8, 128), 0)
    here = 2 * p.s + sub % 2
    fixed = (jnp.abs(lane - here) <= 1).astype(F32) + (lane == 0).astype(F32) + (lane == 15).astype(F32)
    for v in range(2):
        for group in range(4):
            counts = fixed
            for row in range(6):
                head = 3 * group + row // 2
                for k in range(3):
                    drawn = rand_ids[v * 12 + head, 2 * k + row % 2]
                    counts = counts + ((sub == row) & (lane == drawn)).astype(F32)
            r.count_out[4 * v + group] = counts
    count_x.start()
    loads[4].wait()
    loads[5].wait()
    for half in range(2):
        for k in range(2):
            at, row = slice(192 * k, 192 * k + 192), 96 * k
            r.half_u[half, :, at] = w_up[:, 384 * k + 192 * half : 384 * k + 192 * half + 192].astype(BF16)
            r.half_d[half, :, at] = w_down[row : row + 96, 192 * half : 192 * half + 192].astype(BF16)
    r.gu[p.w, chip, core] = r.half_u[p.w % 2]
    r.gd[chip, core, p.w] = r.half_d[p.w % 2]
    gq0.stage1()
    loads[0].wait()
    hat, rstd = norm_stats(x[...].astype(F32))
    r.hat_a[...] = hat
    r.rstd_a[...] = rstd
    loads[1].wait()
    for v in range(2):
        rows = slice(128 * v, 128 * v + 128)
        r.gys[0, rows] = (d_out[rows].astype(F32) * live[v].astype(F32)).astype(BF16)
    gn.stage1()
    gq1.stage1()
    gq0.stage2()
    go.z_send()

    count_x.wait()
    spread = (
        lax.broadcasted_iota(jnp.int32, (128, 1024), 1) // 64 == lax.broadcasted_iota(jnp.int32, (128, 1024), 0)
    ).astype(BF16)
    wide = dot(r.counts[...].reshape(64, 128).astype(BF16), spread)
    wide = jnp.where(wide > 0.5, jnp.log(jnp.maximum(wide, 1.0)), NEG)
    for src in range(8):
        for head in range(3):
            row = src * 8 + head * 2
            at = 2 * (src % 2)
            r.bias[head, src // 2, at : at + 2] = wide[row : row + 2]

    gu0.z_send()
    gq2.stage1()
    gn.stage2()
    gq1.stage2()
    gq0.stage3()
    gn.stage3()
    gq2.stage2()
    gn.finish()
    mate_g.start()
    lane = lax.broadcasted_iota(jnp.int32, (128, 768), 1)
    sub = lax.broadcasted_iota(jnp.int32, (128, 768), 0)
    gains = jnp.zeros((32, 768), F32)
    for s in range(8):
        place = ((lane == sub + 96 * s) & (sub < 96)).astype(BF16)
        gains = gains + dot(r.gn[:, s // 2, s % 2].reshape(32, 128).astype(BF16), place)
    r.gains[...] = gains
    r.h[...] = (r.hat_a[...] * r.gains[0:1] + r.gains[8:9]).astype(BF16)
    go.stage1()
    gq1.stage3()
    gq2.stage3()
    gq0.finish()
    gu0.stage1()
    gd1.z_send()
    gq1.finish()
    gq2.finish()
    go.stage2()

    for w in range(4):
        part = dot(r.h[...], rows_of(r.gq, w, 768)).astype(BF16)
        for k in range(3):
            kind, group = divmod(3 * w + k, 4)
            for v in range(2):
                for j in range(2):
                    for head in range(3):
                        row, at, col = 128 * v + 64 * j, 192 * j + 64 * kind, 192 * k + 64 * head
                        r.sb[head, 4 * v + group, :, at : at + 64] = part[row : row + 64, col : col + 64]
    gu1.z_send()
    qkv_x[0].start()
    go.stage3()
    qkv_x[1].start()
    qkv_x[2].start()

    for head in range(3):
        qkv_x[head].wait()
        for src in range(8):
            for kind, ref in enumerate((r.qh, r.kh, r.vh)):
                for j in range(2):
                    row, at = 128 * src + 64 * j, 192 * j + 64 * kind
                    part = r.rb[head, src, :, at : at + 64]
                    ref[head, row : row + 64] = part * jnp.asarray(1.0 / math.sqrt(HD), BF16) if kind == 0 else part

        def attend(c, _, head=head):
            q0 = pl.multiple_of(c * 256, 256)
            raw = dot_nt(r.qh[head, pl.ds(q0, 256)], r.kh[head])
            score = (raw.reshape(4, 64, 1024) + r.bias[head, c][:, None, :]).reshape(256, 1024)
            weight = jnp.exp(score - jnp.max(score, axis=-1, keepdims=True))
            share = 1.0 / jnp.sum(weight, axis=-1, keepdims=True)
            weight = weight.astype(BF16)
            r.prob[head, pl.ds(q0, 256)] = weight
            r.share[head, pl.ds(q0, 256)] = share
            got = (dot(weight, r.vh[head]) * share).astype(BF16)
            r.kept_o[head, pl.ds(q0, 256)] = got
            got = got.reshape(2, 2, 64, 64)
            for j in range(2):
                at = 192 * j + 64 * head
                r.ab[pl.ds(2 * c, 2), :, at : at + 64] = got[:, j]
            return 0

        lax.fori_loop(0, 4, attend, 0, unroll=2)
        if head == 0:
            go.finish()
            gd0.z_send()
        if head == 1:
            gu1.stage1()
    att_x.start()
    gu0.stage2()
    gu1.stage2()
    for w in range(4):
        for k in range(2):
            r.wout[:, :, k, :, 192 * w : 192 * w + 192] = r.go[w, :, :, :, 192 * k : 192 * k + 192]
    gd0.stage1()
    mate_g.wait_recv()
    for k in range(2):
        r.turned_g[:, 256 * k : 256 * k + 256] = turned(r.gys[k])
    att_x.wait()
    for v in range(2):
        for group in range(4):
            for j in range(2):
                row = 128 * v + 64 * j
                r.att[row : row + 64, 192 * group : 192 * group + 192] = r.at[4 * v + group, :, 192 * j : 192 * j + 192]
    mid = x[...].astype(F32) + dot(r.att[...], r.wout[...].reshape(768, 768))
    r.y[0:256] = mid
    r.y[256:512] = jnp.zeros((256, 768), F32)
    hat, rstd = norm_stats(mid)
    r.hat_b[...] = hat
    r.rstd_b[...] = rstd
    r.hs[0] = (hat * r.gains[16:17] + r.gains[24:25]).astype(BF16)
    mate_h.start()
    gd0.stage2()
    gu1.stage3()
    gd1.stage1()
    gu0.stage3()
    r.back[...] = jnp.zeros((512, 768), F32)
    r.turned_h[:, 0:256] = turned(r.hs[0])
    gu0.finish()
    gu1.finish()

    def up_weights(f):
        return jnp.concatenate([rows_of(r.gu, 2 * f + k, 768) for k in range(2)], axis=1)

    for k in range(2):
        if k == 1:
            gd0.stage3()
            gd1.stage2()
            gd0.finish()
            mate_h.wait_recv()
            gd1.stage3()
            r.turned_h[:, 256:512] = turned(r.hs[1])

        def feed_up(f, _, k=k):
            up = dot(r.hs[k], up_weights(f))
            square = up * up
            bend = jnp.tanh(GELU_C * (up + 0.044715 * up * square))
            slope = 0.5 * (1.0 + bend) + 0.5 * up * (1.0 - bend * bend) * (GELU_C * (1.0 + 0.134145 * square))
            r.act[f, 256 * k : 256 * k + 256] = (0.5 * up * (1.0 + bend)).astype(BF16)
            r.slope[f, 256 * k : 256 * k + 256] = slope.astype(BF16)
            return 0

        lax.fori_loop(0, 2, feed_up, 0, unroll=True)
    gd1.finish()
    for g in gathers:
        g.drain()

    for f in range(4):
        for c in range(2):
            for j in range(2):
                at = 384 * (f % 2) + 192 * c
                r.wd[f // 2, :, j, :, at : at + 192] = r.gd[f, c, :, :, 192 * j : 192 * j + 192]
    for k in (1, 0):

        def feed_back(f, _, k=k):
            rows = slice(256 * k, 256 * k + 256)
            grad_up = (dot(r.gys[k], rows_of(r.wd, f, 768)) * r.slope[f, rows].astype(F32)).astype(BF16)
            r.slope[f, rows] = grad_up
            r.back[rows] += dot_nt(grad_up, up_weights(f))
            return 0

        lax.fori_loop(0, 2, feed_back, 0, unroll=True)
        if k == 1:
            r.back_out[...] = r.back[256:512].astype(BF16)
            mate_back.start()

    def feed_raw(k, _):
        f = p.chip(2 * k) // 2
        act = r.act[f]
        r.y[...] += dot_nt(act, rows_of(r.wd, f, 768))
        raw_down = dot(r.turned_g[...], act).astype(BF16).reshape(4, 2, 96, 768)
        for i in range(2):
            for c in range(2):
                for j in range(2):
                    at = 384 * i + 192 * c
                    r.gd[2 * f + i, c, :, :, 192 * j : 192 * j + 192] = raw_down[:, j, :, at : at + 192]
            sd0.stage_c_of(2 * f + i)
            sd1.stage_c_of(2 * f + i)
        raw_up = dot(r.turned_h[...], r.slope[f]).astype(BF16)
        for i in range(2):
            r.gu[2 * f + i] = raw_up[:, 384 * i : 384 * i + 384].reshape(4, 2, 96, 384)
        return 0

    lax.fori_loop(0, 2, feed_raw, 0)
    sd0.stage_d()
    r.turned[...] = turned(r.att[...])
    r.y_out[...] = r.y[256:512].astype(BF16)
    sd1.stage_d()
    r.turned_i[...] = turned(r.hat_a[...] * r.gains[0:1] + r.gains[8:9])
    su1.stage_c()
    mate_back.wait_recv()

    r.back[0:256] += r.back_in[...].astype(F32)
    mid_grad = norm_back(r.back[0:256], r.hat_b[...], r.rstd_b[...], r.gains[16:17])
    for v in range(2):
        rows = slice(128 * v, 128 * v + 128)
        r.mid_grad[rows] = mid_grad[rows] + d_out[rows].astype(F32) * live[v].astype(F32)
    r.hb[...] = r.mid_grad[...].astype(BF16)
    att_x.drain()
    grad_o = dot_nt(r.hb[...], r.wout[...].reshape(768, 768)).astype(BF16)
    for v in range(2):
        for group in range(4):
            for j in range(2):
                row = 128 * v + 64 * j
                r.ab[4 * v + group, :, 192 * j : 192 * j + 192] = grad_o[row : row + 64, 192 * group : 192 * group + 192]
    gro_x.start()
    r.rn[...] = jnp.zeros((4, 4, 2, 8, 128), F32)

    def put_norm(w, row):
        for s in range(8):
            r.rn[w, s // 2, s % 2, 0:1, 0:96] = row[:, 96 * s : 96 * s + 96]

    put_norm(2, jnp.sum(r.back[0:256] * r.hat_b[...], axis=0, keepdims=True))
    put_norm(3, jnp.sum(r.back[0:256], axis=0, keepdims=True))
    for w in range(4):
        raw = dot(r.turned[...], r.hb[:, 192 * w : 192 * w + 192]).astype(BF16).reshape(4, 2, 2, 48, 192)
        for k in range(2):
            r.go[w, :, :, :, 192 * k : 192 * k + 192] = raw[:, :, k]
    for exchange in qkv_x:
        exchange.drain()
    sd0.stage_e()
    sd1.stage_e()
    gro_x.wait()
    su1.stage_d()

    for head in range(3):
        r.gk[...] = jnp.zeros((64, 1024), F32)
        r.gv[...] = jnp.zeros((64, 1024), F32)

        def attend_back(c, _, head=head):
            q0 = pl.multiple_of(c * 256, 256)
            halves = []
            for j in range(2):
                at = 192 * j + 64 * head
                halves.append(r.gor[pl.ds(2 * c, 2), :, at : at + 64].reshape(2, 1, 64, 64))
            grad = jnp.concatenate(halves, axis=1).reshape(256, 64)
            grad = (grad.astype(F32) * r.share[head, pl.ds(q0, 256)]).astype(BF16)
            inner = jnp.sum(grad.astype(F32) * r.kept_o[head, pl.ds(q0, 256)].astype(F32), axis=-1, keepdims=True)
            weight = r.prob[head, pl.ds(q0, 256)]
            grad_s = (weight.astype(F32) * (dot_nt(grad, r.vh[head]) - inner)).astype(BF16)
            grad_q = (dot(grad_s, r.kh[head]) * (1.0 / math.sqrt(HD))).astype(BF16).reshape(2, 2, 64, 64)
            for j in range(2):
                r.sb[head, pl.ds(2 * c, 2), :, 192 * j : 192 * j + 64] = grad_q[:, j]
            r.gk[...] += dot_tn(r.qh[head, pl.ds(q0, 256)], grad_s)
            r.gv[...] += dot_tn(grad, weight)
            return 0

        lax.fori_loop(0, 4, attend_back, 0, unroll=2)
        for kind, grad in ((1, r.gk[...]), (2, r.gv[...])):
            grad = jnp.transpose(grad).astype(BF16).reshape(8, 2, 64, 64)
            for j in range(2):
                at = 192 * j + 64 * kind
                r.sb[head, :, :, at : at + 64] = grad[:, j]
        if head == 1:
            mate_y.start()
            sd1.stage_f()
            sd0.stage_f()
            so.stage_c()
        gqkv_x[head].start()
    su0.stage_c()
    su1.stage_e()
    r.back[0:256] = jnp.zeros((256, 768), F32)
    for head in range(3):
        gqkv_x[head].wait()
        for v in range(2):
            for group in range(4):
                for kind in range(3):
                    for j in range(2):
                        row, at, to = 128 * v + 64 * j, 192 * j + 64 * kind, 768 * kind + 192 * group + 64 * head
                        r.wide[row : row + 64, to : to + 64] = r.gb[head, 4 * v + group, :, at : at + 64]
        if head == 1:
            su0.stage_d()
    so.stage_d()
    for w in range(4):
        grad = r.wide[:, 576 * w : 576 * w + 576]
        r.back[0:256] += dot_nt(grad, rows_of(r.gq, w, 768))
        r.gq[w] = dot(r.turned_i[...], grad).astype(BF16).reshape(4, 2, 96, 576)
    sq2.stage_c()
    su0.stage_e()
    sq0.stage_c()
    sq2.stage_d()
    su1.stage_f()
    sq1.stage_c()
    grad_h = r.back[0:256]
    put_norm(0, jnp.sum(grad_h * r.hat_a[...], axis=0, keepdims=True))
    put_norm(1, jnp.sum(grad_h, axis=0, keepdims=True))
    so.stage_e()
    su0.stage_f()
    sq1.stage_d()

    def put_down(k, halves):
        for half, value in enumerate(halves):
            for j in range(2):
                row, at = 96 * j + 48 * k, 192 * half
                red_d[row : row + 48, at : at + 192] = value[:, 192 * j : 192 * j + 192]

    def put_up(k, halves):
        for half, value in enumerate(halves):
            for j in range(2):
                at = 384 * j + 192 * half
                red_u[48 * k : 48 * k + 48, at : at + 192] = value[:, 192 * j : 192 * j + 192]

    def squares(ref):
        return jnp.sum(ref[...] * ref[...])

    put_down(1, sd1.finish_halves())
    so.stage_f()
    sq0.stage_d()
    mate_y.wait_recv()
    output[...] = (r.y[0:256] + r.y_in[...].astype(F32)).astype(BF16)
    stores[0].start()
    sq2.stage_e()
    put_down(0, sd0.finish_halves())
    stores[5].start()
    red_o[...] = so.finish()
    stores[3].start()
    put_up(0, su0.finish_halves())
    sq1.stage_e()
    sn.stage_c()
    sq2.stage_f()
    sq0.stage_e()
    put_up(1, su1.finish_halves())
    stores[4].start()
    sn.stage_d()
    sq1.stage_f()
    red_q[64:96] = sq2.finish()
    sn.stage_e()
    local = squares(red_o) + squares(red_u) + squares(red_d)
    sq0.stage_f()
    d_input[...] = r.mid_grad[...] + norm_back(grad_h, r.hat_a[...], r.rstd_a[...], r.gains[0:1])
    stores[1].start()
    red_q[32:64] = sq1.finish()
    sn.stage_f()
    red_q[0:32] = sq0.finish()
    stores[2].start()
    red_n[...] = sn.finish()
    stores[6].start()
    local = jnp.zeros((8, 128), F32) + (local + squares(red_q) + squares(red_n))
    r.square[...] = local
    r.squares[0] = local

    def share(k):
        to = ((p.w + k // 8) % 4, (p.s + k % 8) % 8)
        return remote(r.square, r.squares.at[k], r.sum_sems, k, to)

    def share_start(k, _):
        share(k).start()
        return 0

    def share_wait(k, _):
        share(k).wait()
        return 0

    lax.fori_loop(1, 32, share_start, 0)
    for part in (count_x, gro_x, *gqkv_x, *scatters):
        part.drain()
    for copy in (mate_h, mate_g, mate_back, mate_y):
        copy.wait_send()
    lax.fori_loop(1, 32, share_wait, 0)
    total[...] = jnp.sum(r.squares[...], axis=0)
    stores[7].start()
    for copy in stores:
        copy.wait()


def adam_kernel(*refs):
    given, made, here, there, sems = refs[0:23], refs[23:46], refs[46:69], refs[69:90], refs[90]
    loads = [pltpu.make_async_copy(a, b, sems.at[k]) for k, (a, b) in enumerate(zip(given, here))]
    stores = [pltpu.make_async_copy(a, b, sems.at[23 + k]) for k, (a, b) in enumerate(zip((*there, *here[21:23]), made))]
    order = (2, 3, 0, 1, 4)
    loads[20].start()
    for k in order:
        for part in range(4):
            loads[5 * part + k].start()
    for k in (22, 21):
        loads[k].start()
    fix_one = 1.0 - beta_one**STEP
    fix_two = 1.0 - beta_two**STEP
    rates = (rate_matrix, rate_output, rate_matrix, rate_matrix, rate_norm)
    loads[20].wait()
    norm = jnp.sqrt(here[20][0:1, 0:1])
    factor = 1.0 / jnp.maximum(norm, 1.0)
    there[20][...] = norm
    stores[20].start()
    for k in order:
        for part in range(4):
            loads[5 * part + k].wait()
        raw = here[k][...]
        if k == 1:
            raw = jnp.concatenate([raw[:, 0:192], raw[:, 192:384]], axis=0)
        if k == 4:
            raw = raw[0:1, 0:96]
        grad = raw * factor
        weight = here[5 + k][...]
        first = beta_one * here[10 + k][...] + (1.0 - beta_one) * grad
        second = beta_two * here[15 + k][...] + (1.0 - beta_two) * grad * grad
        stride = first / fix_one / (jnp.sqrt(second / fix_two) + adam_eps)
        decay = 0.0 if k == 4 else decay_rate
        there[k][...] = grad
        there[5 + k][...] = weight - rates[k] * (stride + decay * weight)
        there[10 + k][...] = first
        there[15 + k][...] = second
        for part in range(4):
            stores[5 * part + k].start()
        if k == 2:
            for j in (22, 21):
                loads[j].wait()
                stores[j].start()
    for copy in stores:
        copy.wait()


def fused_device(
    layer_input, d_out, rand_ids, live_mask, w_qkv, w_out, w_up, w_down, norm_params,
    m_qkv, m_out, m_up, m_down, m_norm, v_qkv, v_out, v_up, v_down, v_norm,
):
    smem, anywhere = (pl.BlockSpec(memory_space=kind) for kind in (pltpu.SMEM, pl.ANY))
    ids = rand_ids.transpose(0, 2, 3, 1).reshape(24, 6)
    leaves, tree = jax.tree.flatten(scratch())
    shape = jax.ShapeDtypeStruct
    output, d_input, *grads, total = pl.pallas_call(
        functools.partial(kernel, tree),
        out_shape=[shape(*leaf) for leaf in KEPT],
        in_specs=[smem, smem] + [anywhere] * 7,
        out_specs=[anywhere] * 8,
        scratch_shapes=leaves,
        compiler_params=pltpu.CompilerParams(collective_id=0, has_side_effects=True, vmem_limit_bytes=VMEM_LIMIT),
    )(
        live_mask, ids, layer_input.reshape(256, 768), d_out.reshape(256, 768), w_qkv, w_out, w_up, w_down.T,
        norm_params.reshape(1, 96),
    )
    state = (
        *grads,
        w_qkv, w_out, w_up, w_down.T, norm_params.reshape(1, 96),
        m_qkv, m_out, m_up, m_down.T, m_norm.reshape(1, 96),
        v_qkv, v_out, v_up, v_down.T, v_norm.reshape(1, 96),
        total, output, d_input,
    )
    results = [shape(w.shape, F32) for w in state[5:10]] * 4
    results += [shape((1, 1), F32), shape(output.shape, BF16), shape(d_input.shape, F32)]
    made = pl.pallas_call(
        adam_kernel,
        out_shape=results,
        in_specs=[anywhere] * 23,
        out_specs=[anywhere] * 23,
        scratch_shapes=[pltpu.VMEM(a.shape, a.dtype) for a in (*state, *results[:21])] + [pltpu.SemaphoreType.DMA((46,))],
        compiler_params=pltpu.CompilerParams(vmem_limit_bytes=VMEM_LIMIT),
    )(*state)
    updated = [m.T if k % 5 == 3 else m.reshape(-1) if k % 5 == 4 else m for k, m in enumerate(made[:20])]
    return (made[21].reshape(2, 128, 768), made[22].reshape(2, 128, 768), *updated, made[20].reshape(1))


def solution(mesh):
    placed = (
        P("win", "seq", None),
        P("win", "seq", None),
        P("win", "seq", None, None),
        P("win"),
        P("seq", "win"),
        P("seq", "win"),
        P("seq", "win"),
        P("seq", "win"),
        P(("win", "seq")),
        P("seq", "win"),
        P("seq", "win"),
        P("seq", "win"),
        P("seq", "win"),
        P(("win", "seq")),
        P("seq", "win"),
        P("seq", "win"),
        P("seq", "win"),
        P("seq", "win"),
        P(("win", "seq")),
    )
    fused = mesh.shape["win"] == 4 and mesh.shape["seq"] == 8
    return jax.shard_map(
        fused_device if fused else per_device,
        mesh=mesh,
        in_specs=placed,
        out_specs=(
            P("win", "seq", None),
            P("win", "seq", None),
            P("seq", "win"),
            P("seq", "win"),
            P("seq", "win"),
            P("seq", "win"),
            P(("win", "seq")),
            P("seq", "win"),
            P("seq", "win"),
            P("seq", "win"),
            P("seq", "win"),
            P(("win", "seq")),
            P("seq", "win"),
            P("seq", "win"),
            P("seq", "win"),
            P("seq", "win"),
            P(("win", "seq")),
            P("seq", "win"),
            P("seq", "win"),
            P("seq", "win"),
            P("seq", "win"),
            P(("win", "seq")),
            P(),
        ),
        check_vma=False,
    )
```

```python
import functools
import math
from typing import Any, NamedTuple

import jax
import jax.numpy as jnp
from jax import lax
from jax.experimental import pallas as pl
from jax.experimental.pallas import tpu as pltpu
from jax.sharding import PartitionSpec as P

H = 12
HD = 64
BLK = 64
STEP = 3


NEG = -1e30
ln_eps = 1e-05
beta_one = 0.5
beta_two = 0.5
adam_eps = 1e-08
decay_rate = 0.1
rate_matrix = 0.04
rate_output = 0.16
rate_norm = 0.6
VMEM_LIMIT = 63 << 20


def layer_norm(values, gain, shift):
    centre = values - jnp.mean(values, axis=-1, keepdims=True)
    spread = jnp.mean(centre * centre, axis=-1, keepdims=True)
    return centre * lax.rsqrt(spread + ln_eps) * gain + shift


def slot_counts(rand_ids, first_block, block_count):
    blocks_dev = rand_ids.shape[1]
    here = (first_block + jnp.arange(blocks_dev, dtype=jnp.int32))[:, None]
    every = jnp.arange(block_count, dtype=jnp.int32)[None, :]
    near = (jnp.abs(here - every) <= 1).astype(jnp.float32)
    ends = (every == 0).astype(jnp.float32) + (every == block_count - 1).astype(jnp.float32)
    drawn = jnp.sum((rand_ids[..., None] == every[0]).astype(jnp.float32), axis=3)
    return (near + ends)[None, :, None, :] + drawn


def adam_update(weight, grad, first, second, rate, decay, fix_one, fix_two):
    first_new = beta_one * first + (1.0 - beta_one) * grad
    second_new = beta_two * second + (1.0 - beta_two) * grad * grad
    stride = first_new / fix_one / (jnp.sqrt(second_new / fix_two) + adam_eps)
    return (weight - rate * (stride + decay * weight), first_new, second_new)


def per_device(
    layer_input,
    d_out,
    rand_ids,
    live_mask,
    w_qkv,
    w_out,
    w_up,
    w_down,
    norm_params,
    m_qkv,
    m_out,
    m_up,
    m_down,
    m_norm,
    v_qkv,
    v_out,
    v_up,
    v_down,
    v_norm,
):
    wins, local_len, width = layer_input.shape
    blocks_dev = local_len // BLK
    block_count = blocks_dev * lax.axis_size("seq")
    first_block = lax.axis_index("seq") * blocks_dev
    inv_root = 1.0 / math.sqrt(HD)
    rows = wins * local_len
    low_qkv = w_qkv.astype(jnp.bfloat16)
    low_out = w_out.astype(jnp.bfloat16)
    low_up = w_up.astype(jnp.bfloat16)
    low_down = w_down.astype(jnp.bfloat16)
    low_norm = norm_params.astype(jnp.bfloat16)
    full_qkv, full_out, full_up, full_down = (
        lax.all_gather(lax.all_gather(low, "win", axis=1, tiled=True), "seq", axis=0, tiled=True)
        for low in (low_qkv, low_out, low_up, low_down)
    )
    full_norm = lax.all_gather(low_norm, ("win", "seq"), axis=0, tiled=True)
    gains = full_norm.astype(jnp.float32).reshape(4, width)
    loss_weight = live_mask.astype(jnp.float32)
    counts = slot_counts(rand_ids, first_block, block_count)
    bias = jnp.where(counts > 0, jnp.log(jnp.maximum(counts, 1.0)), NEG)
    bias = jnp.repeat(bias, BLK, axis=3)[:, :, :, None, :]
    tokens = layer_input.astype(jnp.float32).reshape(rows, width)
    h_one = layer_norm(tokens, gains[0], gains[1]).astype(jnp.bfloat16)
    qkv = jnp.dot(h_one, full_qkv, preferred_element_type=jnp.float32)
    q_heads = qkv[:, :width].astype(jnp.bfloat16).reshape(wins, blocks_dev, BLK, H, HD)
    keyval = qkv[:, width:].astype(jnp.bfloat16).reshape(wins, local_len, 2 * width)
    window = lax.all_gather(keyval, "seq", axis=1, tiled=True)
    shaped = window.reshape(wins, block_count * BLK, 2, H, HD)
    keys, values = shaped[:, :, 0], shaped[:, :, 1]
    scores = (
        jnp.einsum("wbqhd,wkhd->wbhqk", q_heads, keys, preferred_element_type=jnp.float32)
        * inv_root
        + bias
    )
    top = jnp.max(scores, axis=-1, keepdims=True)
    log_total = top + jnp.log(jnp.sum(jnp.exp(scores - top), axis=-1, keepdims=True))
    prob = jnp.exp(scores - log_total).astype(jnp.bfloat16)
    heads_out = jnp.einsum("wbhqk,wkhd->wbqhd", prob, values, preferred_element_type=jnp.float32)
    attended = heads_out.astype(jnp.bfloat16).reshape(rows, width)
    middle = tokens + jnp.dot(attended, full_out, preferred_element_type=jnp.float32)
    h_two = layer_norm(middle, gains[2], gains[3]).astype(jnp.bfloat16)
    up_proj = jnp.dot(h_two, full_up, preferred_element_type=jnp.float32)
    active = jax.nn.gelu(up_proj).astype(jnp.bfloat16)
    result = middle + jnp.dot(active, full_down, preferred_element_type=jnp.float32)
    output = result.astype(jnp.bfloat16).reshape(wins, local_len, width)
    grad_y = (d_out.astype(jnp.float32) * loss_weight[:, None, None]).reshape(rows, width)
    grad_ffn = grad_y.astype(jnp.bfloat16)
    raw_down = jnp.einsum("tf,td->fd", active, grad_ffn, preferred_element_type=jnp.float32)
    grad_act = jnp.einsum("td,fd->tf", grad_ffn, full_down, preferred_element_type=jnp.float32)
    gelu_pull = jax.vjp(jax.nn.gelu, up_proj)[1]
    grad_up = gelu_pull(grad_act)[0].astype(jnp.bfloat16)
    raw_up = jnp.einsum("td,tf->df", h_two, grad_up, preferred_element_type=jnp.float32)
    grad_h_two = jnp.einsum("tf,df->td", grad_up, full_up, preferred_element_type=jnp.float32)
    norm_pull = jax.vjp(layer_norm, middle, gains[2], gains[3])[1]
    grad_mid_ln, raw_gain_two, raw_shift_two = norm_pull(grad_h_two)
    grad_mid = grad_y + grad_mid_ln
    grad_att = grad_mid.astype(jnp.bfloat16)
    raw_out = jnp.einsum("td,te->de", attended, grad_att, preferred_element_type=jnp.float32)
    grad_o = jnp.einsum("te,de->td", grad_att, full_out, preferred_element_type=jnp.float32)
    grad_o = grad_o.astype(jnp.bfloat16).reshape(wins, blocks_dev, BLK, H, HD)
    grad_p = jnp.einsum("wbqhd,wkhd->wbhqk", grad_o, values, preferred_element_type=jnp.float32)
    prob_f = prob.astype(jnp.float32)
    inner = jnp.sum(prob_f * grad_p, axis=-1, keepdims=True)
    grad_s = (prob_f * (grad_p - inner)).astype(jnp.bfloat16)
    grad_q = (
        jnp.einsum("wbhqk,wkhd->wbqhd", grad_s, keys, preferred_element_type=jnp.float32)
        * inv_root
    )
    grad_v = jnp.einsum("wbhqk,wbqhd->wkhd", prob, grad_o, preferred_element_type=jnp.float32)
    grad_k = (
        jnp.einsum("wbhqk,wbqhd->wkhd", grad_s, q_heads, preferred_element_type=jnp.float32)
        * inv_root
    )
    grad_kv = jnp.stack([grad_k, grad_v], axis=2).astype(jnp.bfloat16)
    grad_kv = lax.psum_scatter(
        grad_kv.reshape(wins, block_count * BLK, 2 * width),
        "seq",
        scatter_dimension=1,
        tiled=True,
    ).reshape(rows, 2 * width)
    grad_qkv = jnp.concatenate(
        [grad_q.reshape(rows, width).astype(jnp.bfloat16), grad_kv], axis=1
    )
    raw_qkv = jnp.einsum("td,te->de", h_one, grad_qkv, preferred_element_type=jnp.float32)
    grad_h_one = jnp.einsum("te,de->td", grad_qkv, full_qkv, preferred_element_type=jnp.float32)
    first_pull = jax.vjp(layer_norm, tokens, gains[0], gains[1])[1]
    grad_tok_ln, raw_gain_one, raw_shift_one = first_pull(grad_h_one)
    d_input = (grad_mid + grad_tok_ln).reshape(wins, local_len, width)
    raw_norm = jnp.concatenate([raw_gain_one, raw_shift_one, raw_gain_two, raw_shift_two])
    red_qkv, red_out, red_up, red_down = (
        lax.psum_scatter(
            lax.psum_scatter(raw.astype(jnp.bfloat16), "seq", scatter_dimension=0, tiled=True),
            "win",
            scatter_dimension=1,
            tiled=True,
        ).astype(jnp.float32)
        for raw in (raw_qkv, raw_out, raw_up, raw_down)
    )
    red_norm = lax.psum_scatter(raw_norm, ("win", "seq"), scatter_dimension=0, tiled=True)
    reduced = (red_qkv, red_out, red_up, red_down, red_norm)
    local_squares = jnp.float32(0.0)
    for grad in reduced:
        local_squares = local_squares + jnp.sum(grad * grad)
    grad_norm = jnp.sqrt(lax.psum(local_squares, ("win", "seq")))
    factor = 1.0 / jnp.maximum(grad_norm, 1.0)
    clipped = tuple((grad * factor for grad in reduced))
    count = jnp.float32(STEP)
    fix_one = 1.0 - jnp.power(jnp.float32(beta_one), count)
    fix_two = 1.0 - jnp.power(jnp.float32(beta_two), count)
    params = (w_qkv, w_out, w_up, w_down, norm_params)
    firsts = (m_qkv, m_out, m_up, m_down, m_norm)
    seconds = (v_qkv, v_out, v_up, v_down, v_norm)
    rates = (rate_matrix, rate_output, rate_matrix, rate_matrix, rate_norm)
    news, moms, secs = ([], [], [])
    for index in range(5):
        decay = 0.0 if index == 4 else decay_rate
        new_w, new_m, new_v = adam_update(
            params[index],
            clipped[index],
            firsts[index],
            seconds[index],
            rates[index],
            decay,
            fix_one,
            fix_two,
        )
        news.append(new_w)
        moms.append(new_m)
        secs.append(new_v)
    return (
        output,
        d_input,
        clipped[0],
        clipped[1],
        clipped[2],
        clipped[3],
        clipped[4],
        news[0],
        news[1],
        news[2],
        news[3],
        news[4],
        moms[0],
        moms[1],
        moms[2],
        moms[3],
        moms[4],
        secs[0],
        secs[1],
        secs[2],
        secs[3],
        secs[4],
        grad_norm.reshape(1),
    )


MESH = pl.DeviceIdType.MESH
F32, BF16 = jnp.float32, jnp.bfloat16
GELU_C = math.sqrt(2.0 / math.pi)
NT = (((1,), (1,)), ((), ()))
TN = (((0,), (0,)), ((), ()))


def dot(a, b):
    return jnp.dot(a, b, preferred_element_type=F32)


def dot_nt(a, b):
    return lax.dot_general(a, b, NT, preferred_element_type=F32)


def dot_tn(a, b):
    return lax.dot_general(a, b, TN, preferred_element_type=F32)


def remote(src, dst, sems, k, dev):
    return pltpu.make_async_remote_copy(
        src_ref=src, dst_ref=dst, send_sem=sems[0].at[k], recv_sem=sems[1].at[k], device_id=dev, device_id_type=MESH
    )


class Place:
    def __init__(self):
        self.w = lax.axis_index("win")
        self.s = s = lax.axis_index("seq")
        self.c = c = s % 2
        x = (s // 2) % 2
        y = s // 4
        dx, dy = 2 - 4 * x, 4 - 8 * y
        self.turn = 1 - 2 * c
        self.n1 = s + (1 - c) * dx + c * dy
        self.n2 = s + (1 - c) * dy + c * dx
        self.nd = s + dx + dy
        self.par = s + self.turn
        self.roles = (s, self.n1, self.n2, self.nd)
        self.par_roles = tuple(r + self.turn for r in (s, self.n2, self.n1, self.nd))
        self.x, self.y = x, y
        self.mate = (self.w + 1 - 2 * (self.w % 2), s)

    def chip(self, k):
        x = self.x + (1 - k % 2) * (1 - 2 * self.x)
        y = self.y + (1 - k // 2) * (1 - 2 * self.y)
        return 2 * y + x

    def role_for_partner(self, chip):
        dx = (chip % 2 - self.x) * (chip % 2 - self.x)
        dy = (chip // 2 - self.y) * (chip // 2 - self.y)
        return self.c * (dx + 2 * dy) + (1 - self.c) * (dy + 2 * dx)


class Blocks:
    def __init__(self, buf, seq_first=False, start=0, count=None):
        self.buf, self.seq_first, self.rows = buf, seq_first, pl.ds(start, buf.shape[3] if count is None else count)

    def block(self, w, s):
        return self.buf.at[(s // 2, s % 2, w, self.rows) if self.seq_first else (w, s // 2, s % 2, self.rows)]

    def read(self, w, s):
        return self.buf[(s // 2, s % 2, w, self.rows) if self.seq_first else (w, s // 2, s % 2, self.rows)]

    def group(self, s):
        every = slice(None)
        return self.buf.at[(s // 2, s % 2, every, self.rows) if self.seq_first else (every, s // 2, s % 2, self.rows)]


class Gather:
    def __init__(self, place, blocks, sems, staged=None):
        self.p, self.b, self.sems, self.staged = place, blocks, sems, staged

    def push(self, s, k, to):
        remote(self.b.group(s), self.b.group(s), self.sems, k, (self.p.w, to)).start()

    def got(self, s, k):
        remote(self.b.group(s), self.b.group(s), self.sems, k, (self.p.w, self.p.par)).wait_recv()

    def along(self, dz, w):
        p, block = self.p, self.b.block(w, self.p.s)
        source = block if self.staged is None else self.staged.at[(p.w + dz) % 2, self.b.rows]
        return remote(source, block, self.sems, dz - 1, ((p.w + dz) % 4, p.s))

    def z_send(self):
        for dz in (1, 2, 3):
            self.along(dz, self.p.w).start()

    def stage1(self):
        p = self.p
        for dz in (1, 2, 3):
            self.along(dz, (p.w + 4 - dz) % 4).wait_recv()
        self.push(p.s, 3, p.n1)
        self.push(p.s, 4, p.n2)
        self.push(p.s, 6, p.par)

    def stage2(self):
        p = self.p
        self.got(p.n1, 3)
        self.push(p.n1, 5, p.n2)
        self.push(p.n1, 7, p.par)

    def stage3(self):
        p = self.p
        self.got(p.n2, 4)
        self.push(p.n2, 8, p.par)
        self.got(p.nd, 5)
        self.push(p.nd, 9, p.par)

    def finish(self):
        for k in range(4):
            self.got(self.p.par_roles[k], 6 + k)

    def drain(self):
        p = self.p
        for dz in (1, 2, 3):
            self.along(dz, p.w).wait_send()
        for k, s in ((3, p.s), (4, p.s), (6, p.s), (5, p.n1), (7, p.n1), (8, p.n2), (9, p.nd)):
            remote(self.b.group(s), self.b.group(s), self.sems, k, (p.w, p.par)).wait_send()


class Scatter:
    def __init__(self, place, blocks, space, sems):
        self.p, self.b, self.sems = place, blocks, sems
        self.c, self.d, self.e, self.f = space

    def copies_c(self):
        p = self.p
        return [remote(self.b.group(p.par_roles[k]), self.c.at[k], self.sems, k, (p.w, p.par)) for k in range(4)]

    def copies_d(self):
        p = self.p
        return [remote(self.c.at[2 + k], self.d.at[k], self.sems, 4 + k, (p.w, p.n2)) for k in range(2)]

    def copy_e(self):
        p = self.p
        return remote(self.c.at[1], self.e, self.sems, 6, (p.w, p.n1))

    def copies_f(self):
        p = self.p
        return [
            remote(self.c.at[0, (p.w + dz) % 4], self.f.at[dz - 1], self.sems, 6 + dz, ((p.w + dz) % 4, p.s))
            for dz in (1, 2, 3)
        ]

    def stage_c(self):
        for copy in self.copies_c():
            copy.start()

    def stage_c_of(self, chip):
        p = self.p
        role = p.role_for_partner(chip)
        remote(self.b.group(2 * chip + 1 - p.c), self.c.at[role], self.sems, role, (p.w, p.par)).start()

    def stage_d(self):
        waits, sends = self.copies_c(), self.copies_d()
        for k in (2, 3, 0, 1):
            waits[k].wait_recv()
            for w in range(4):
                self.c[k, w] = self.c[k, w] + self.b.read(w, self.p.roles[k])
            if k >= 2:
                sends[k - 2].start()

    def stage_e(self):
        waits = self.copies_d()
        for k in (1, 0):
            waits[k].wait_recv()
            for w in range(4):
                self.c[k, w] = self.c[k, w] + self.d[k, w]
            if k == 1:
                self.copy_e().start()

    def stage_f(self):
        self.copy_e().wait_recv()
        for w in range(4):
            self.c[0, w] = self.c[0, w] + self.e[w]
        for copy in self.copies_f():
            copy.start()

    def finish(self):
        total = self.c[0, self.p.w].astype(F32)
        for k, copy in enumerate(self.copies_f()):
            copy.wait_recv()
            total = total + self.f[k].astype(F32)
        return total

    def finish_halves(self):
        p = self.p
        for copy in self.copies_f():
            copy.wait_recv()
        alike = self.c[0, p.w].astype(F32) + self.f[1].astype(F32)
        other = self.f[0].astype(F32) + self.f[2].astype(F32)
        even = p.w % 2 == 0
        return jnp.where(even, alike, other), jnp.where(even, other, alike)

    def drain(self):
        for copy in (*self.copies_c(), *self.copies_d(), self.copy_e(), *self.copies_f()):
            copy.wait_send()


class Exchange:
    def __init__(self, place, src, dst, sems):
        self.p, self.src, self.dst, self.sems = place, src, dst, sems

    def copy(self, ds):
        p = self.p
        to = (p.s + ds) % 8
        return remote(self.src.at[to], self.dst.at[p.s], self.sems, ds, (p.w, to))

    def own(self):
        return pltpu.make_async_copy(self.src.at[self.p.s], self.dst.at[self.p.s], self.sems[1].at[0])

    def start(self):
        for ds in (6, 5, 3, 7, 4, 2, 1):
            self.copy(ds).start()
        self.own().start()

    def wait(self):
        p = self.p
        self.own().wait()
        for ds in range(1, 8):
            back = (p.s + 8 - ds) % 8
            remote(self.src.at[back], self.dst.at[back], self.sems, ds, (p.w, back)).wait_recv()

    def drain(self):
        for ds in range(1, 8):
            self.copy(ds).wait_send()


def norm_stats(values):
    centre = values - jnp.mean(values, axis=-1, keepdims=True)
    rstd = lax.rsqrt(jnp.mean(centre * centre, axis=-1, keepdims=True) + ln_eps)
    return centre * rstd, rstd


def norm_back(grad, hat, rstd, gain):
    scaled = grad * gain
    return rstd * (
        scaled - jnp.mean(scaled, axis=-1, keepdims=True) - hat * jnp.mean(scaled * hat, axis=-1, keepdims=True)
    )


def rows_of(ref, index, rows):
    value = ref[index]
    return value.reshape(rows, value.shape[-1])


def turned(value):
    return jnp.transpose(value.astype(F32)).astype(BF16)


GIVEN = (
    ((256, 768), BF16), ((256, 768), BF16), ((96, 576), F32), ((96, 192), F32), ((96, 768), F32), ((192, 384), F32), ((1, 96), F32),
)
KEPT = (
    ((256, 768), BF16), ((256, 768), F32), ((96, 576), F32), ((48, 384), F32), ((96, 768), F32), ((192, 384), F32), ((8, 128), F32), ((8, 128), F32),
)


class Space(NamedTuple):
    gn: Any
    gq: Any
    go: Any
    gu: Any
    gd: Any
    rn: Any
    sn: Any
    sq: Any
    so: Any
    su: Any
    sd: Any
    half_u: Any
    half_d: Any
    wd: Any
    gather_sems: Any
    scatter_sems: Any
    exchange_sems: Any
    sum_sems: Any
    count_out: Any
    counts: Any
    bias: Any
    sb: Any
    rb: Any
    qh: Any
    kh: Any
    vh: Any
    prob: Any
    share: Any
    kept_o: Any
    ab: Any
    at: Any
    gor: Any
    gb: Any
    att: Any
    wout: Any
    turned: Any
    turned_i: Any
    turned_h: Any
    turned_g: Any
    gains: Any
    hat_a: Any
    hat_b: Any
    rstd_a: Any
    rstd_b: Any
    h: Any
    hb: Any
    hs: Any
    gys: Any
    back_out: Any
    back_in: Any
    y_out: Any
    y_in: Any
    mate_sems: Any
    wide: Any
    y: Any
    back: Any
    mid_grad: Any
    gk: Any
    gv: Any
    act: Any
    slope: Any
    square: Any
    squares: Any
    given: Any
    kept: Any
    io_sems: Any


def scratch():
    def scatter(*block, kind=BF16):
        return tuple(pltpu.VMEM((*lead, *block), kind) for lead in ((4, 4), (2, 4), (4,), (3,)))

    def sems(count):
        return (pltpu.SemaphoreType.DMA((count,)),) * 2

    rows, wide = (256, 768), (3, 8, 64, 384)
    return Space(
        gn=pltpu.VMEM((4, 4, 2, 8, 128), F32),
        gq=pltpu.VMEM((4, 4, 2, 96, 576), BF16),
        go=pltpu.VMEM((4, 4, 2, 48, 384), BF16),
        gu=pltpu.VMEM((4, 4, 2, 96, 384), BF16),
        gd=pltpu.VMEM((4, 2, 4, 96, 384), BF16),
        rn=pltpu.VMEM((4, 4, 2, 8, 128), F32),
        sn=scatter(8, 128, kind=F32),
        sq=tuple(scatter(32, 576) for _ in range(3)),
        so=scatter(48, 384),
        su=tuple(scatter(48, 384) for _ in range(2)),
        sd=tuple(scatter(48, 384) for _ in range(2)),
        half_u=pltpu.VMEM((2, 96, 384), BF16),
        half_d=pltpu.VMEM((2, 96, 384), BF16),
        wd=pltpu.VMEM((2, 4, 2, 96, 768), BF16),
        gather_sems=tuple(sems(10) for _ in range(9)),
        scatter_sems=tuple(sems(10) for _ in range(9)),
        exchange_sems=tuple(sems(8) for _ in range(9)),
        sum_sems=sems(32),
        count_out=pltpu.VMEM((8, 8, 128), F32),
        counts=pltpu.VMEM((8, 8, 128), F32),
        bias=pltpu.VMEM((3, 4, 4, 1024), F32),
        sb=pltpu.VMEM(wide, BF16),
        rb=pltpu.VMEM(wide, BF16),
        qh=pltpu.VMEM((3, 1024, 64), BF16),
        kh=pltpu.VMEM((3, 1024, 64), BF16),
        vh=pltpu.VMEM((3, 1024, 64), BF16),
        prob=pltpu.VMEM((3, 1024, 1024), BF16),
        share=pltpu.VMEM((3, 1024, 1), F32),
        kept_o=pltpu.VMEM((3, 1024, 64), BF16),
        ab=pltpu.VMEM((8, 64, 384), BF16),
        at=pltpu.VMEM((8, 64, 384), BF16),
        gor=pltpu.VMEM((8, 64, 384), BF16),
        gb=pltpu.VMEM(wide, BF16),
        att=pltpu.VMEM(rows, BF16),
        wout=pltpu.VMEM((4, 2, 2, 48, 768), BF16),
        turned=pltpu.VMEM((768, 256), BF16),
        turned_i=pltpu.VMEM((768, 256), BF16),
        turned_h=pltpu.VMEM((768, 512), BF16),
        turned_g=pltpu.VMEM((768, 512), BF16),
        gains=pltpu.VMEM((32, 768), F32),
        hat_a=pltpu.VMEM(rows, F32),
        hat_b=pltpu.VMEM(rows, F32),
        rstd_a=pltpu.VMEM((256, 1), F32),
        rstd_b=pltpu.VMEM((256, 1), F32),
        h=pltpu.VMEM(rows, BF16),
        hb=pltpu.VMEM(rows, BF16),
        hs=pltpu.VMEM((2, *rows), BF16),
        gys=pltpu.VMEM((2, *rows), BF16),
        back_out=pltpu.VMEM(rows, BF16),
        back_in=pltpu.VMEM(rows, BF16),
        y_out=pltpu.VMEM(rows, BF16),
        y_in=pltpu.VMEM(rows, BF16),
        mate_sems=sems(4),
        wide=pltpu.VMEM((256, 2304), BF16),
        y=pltpu.VMEM((512, 768), F32),
        back=pltpu.VMEM((512, 768), F32),
        mid_grad=pltpu.VMEM(rows, F32),
        gk=pltpu.VMEM((64, 1024), F32),
        gv=pltpu.VMEM((64, 1024), F32),
        act=pltpu.VMEM((2, 512, 768), BF16),
        slope=pltpu.VMEM((2, 512, 768), BF16),
        square=pltpu.VMEM((8, 128), F32),
        squares=pltpu.VMEM((32, 8, 128), F32),
        given=tuple(pltpu.VMEM(dims, kind) for dims, kind in GIVEN),
        kept=tuple(pltpu.VMEM(dims, kind) for dims, kind in KEPT),
        io_sems=pltpu.SemaphoreType.DMA((15,)),
    )


def kernel(tree, live, rand_ids, *refs):
    r = jax.tree.unflatten(tree, refs[15:])
    x, d_out, w_qkv, w_out, w_up, w_down, norm = r.given
    output, d_input, red_q, red_o, red_u, red_d, red_n, total = r.kept
    loads = [pltpu.make_async_copy(a, b, r.io_sems.at[k]) for k, (a, b) in enumerate(zip(refs[:7], r.given))]
    stores = [pltpu.make_async_copy(a, b, r.io_sems.at[7 + k]) for k, (a, b) in enumerate(zip(r.kept, refs[7:15]))]
    for k in (6, 2, 5, 3, 4, 0, 1):
        loads[k].start()
    p = Place()
    barrier = pltpu.get_barrier_semaphore()

    def greet(k, _):
        to = ((p.w + k // 8) % 4, (p.s + k % 8) % 8)
        pl.semaphore_signal(barrier, inc=1, device_id=to, device_id_type=MESH)
        return 0

    lax.fori_loop(1, 32, greet, 0)

    blocks_q = [Blocks(r.gq, start=32 * k, count=32) for k in range(3)]
    blocks_u = [Blocks(r.gu, start=48 * k, count=48) for k in range(2)]
    blocks_d = [Blocks(r.gd, True, start=48 * k, count=48) for k in range(2)]
    every = (*blocks_q, Blocks(r.go), *blocks_u, *blocks_d)
    staged = (None,) * 4 + (r.half_u,) * 2 + (r.half_d,) * 2
    gathers = [Gather(p, Blocks(r.gn), r.gather_sems[8])]
    gathers += [Gather(p, b, m, half) for b, m, half in zip(every, r.gather_sems, staged)]
    gn, gq0, gq1, gq2, go, gu0, gu1, gd0, gd1 = gathers
    scatters = [Scatter(p, Blocks(r.rn), r.sn, r.scatter_sems[8])]
    scatters += [Scatter(p, b, space, m) for b, space, m in zip(every, (*r.sq, r.so, *r.su, *r.sd), r.scatter_sems)]
    sn, sq0, sq1, sq2, so, su0, su1, sd0, sd1 = scatters
    mate_h = remote(r.hs.at[0], r.hs.at[1], r.mate_sems, 0, p.mate)
    mate_g = remote(r.gys.at[0], r.gys.at[1], r.mate_sems, 1, p.mate)
    mate_back = remote(r.back_out, r.back_in, r.mate_sems, 2, p.mate)
    mate_y = remote(r.y_out, r.y_in, r.mate_sems, 3, p.mate)
    count_x = Exchange(p, r.count_out, r.counts, r.exchange_sems[0])
    att_x = Exchange(p, r.ab, r.at, r.exchange_sems[1])
    gro_x = Exchange(p, r.ab, r.gor, r.exchange_sems[2])
    qkv_x = [Exchange(p, r.sb.at[h], r.rb.at[h], r.exchange_sems[3 + h]) for h in range(3)]
    gqkv_x = [Exchange(p, r.sb.at[h], r.gb.at[h], r.exchange_sems[6 + h]) for h in range(3)]
    chip, core = p.s // 2, p.c

    r.gn[p.w, chip, core] = jnp.zeros((8, 128), F32)
    loads[6].wait()
    r.gn[p.w, chip, core, 0:1, 0:96] = norm[...].astype(BF16).astype(F32)
    loads[2].wait()
    r.gq[p.w, chip, core] = w_qkv[...].astype(BF16)
    pl.semaphore_wait(barrier, 31)
    gq0.z_send()
    gn.z_send()
    gq1.z_send()
    gq2.z_send()
    loads[3].wait()
    for k in range(2):
        r.go[p.w, chip, core, :, 192 * k : 192 * k + 192] = w_out[48 * k : 48 * k + 48].astype(BF16)

    lane = lax.broadcasted_iota(jnp.int32, (8, 128), 1)
    sub = lax.broadcasted_iota(jnp.int32, (8, 128), 0)
    here = 2 * p.s + sub % 2
    fixed = (jnp.abs(lane - here) <= 1).astype(F32) + (lane == 0).astype(F32) + (lane == 15).astype(F32)
    for v in range(2):
        for group in range(4):
            counts = fixed
            for row in range(6):
                head = 3 * group + row // 2
                for k in range(3):
                    drawn = rand_ids[v * 12 + head, 2 * k + row % 2]
                    counts = counts + ((sub == row) & (lane == drawn)).astype(F32)
            r.count_out[4 * v + group] = counts
    count_x.start()
    loads[4].wait()
    loads[5].wait()
    for half in range(2):
        for k in range(2):
            at, row = slice(192 * k, 192 * k + 192), 96 * k
            r.half_u[half, :, at] = w_up[:, 384 * k + 192 * half : 384 * k + 192 * half + 192].astype(BF16)
            r.half_d[half, :, at] = w_down[row : row + 96, 192 * half : 192 * half + 192].astype(BF16)
    r.gu[p.w, chip, core] = r.half_u[p.w % 2]
    r.gd[chip, core, p.w] = r.half_d[p.w % 2]
    gq0.stage1()
    loads[0].wait()
    hat, rstd = norm_stats(x[...].astype(F32))
    r.hat_a[...] = hat
    r.rstd_a[...] = rstd
    loads[1].wait()
    for v in range(2):
        rows = slice(128 * v, 128 * v + 128)
        r.gys[0, rows] = (d_out[rows].astype(F32) * live[v].astype(F32)).astype(BF16)
    gn.stage1()
    gq1.stage1()
    gq0.stage2()
    go.z_send()

    count_x.wait()
    spread = (
        lax.broadcasted_iota(jnp.int32, (128, 1024), 1) // 64 == lax.broadcasted_iota(jnp.int32, (128, 1024), 0)
    ).astype(BF16)
    wide = dot(r.counts[...].reshape(64, 128).astype(BF16), spread)
    wide = jnp.where(wide > 0.5, jnp.log(jnp.maximum(wide, 1.0)), NEG)
    for src in range(8):
        for head in range(3):
            row = src * 8 + head * 2
            at = 2 * (src % 2)
            r.bias[head, src // 2, at : at + 2] = wide[row : row + 2]

    gu0.z_send()
    gq2.stage1()
    gn.stage2()
    gq1.stage2()
    gq0.stage3()
    gn.stage3()
    gq2.stage2()
    gn.finish()
    mate_g.start()
    lane = lax.broadcasted_iota(jnp.int32, (128, 768), 1)
    sub = lax.broadcasted_iota(jnp.int32, (128, 768), 0)
    gains = jnp.zeros((32, 768), F32)
    for s in range(8):
        place = ((lane == sub + 96 * s) & (sub < 96)).astype(BF16)
        gains = gains + dot(r.gn[:, s // 2, s % 2].reshape(32, 128).astype(BF16), place)
    r.gains[...] = gains
    r.h[...] = (r.hat_a[...] * r.gains[0:1] + r.gains[8:9]).astype(BF16)
    go.stage1()
    gq1.stage3()
    gq2.stage3()
    gq0.finish()
    gu0.stage1()
    gd1.z_send()
    gq1.finish()
    gq2.finish()
    go.stage2()

    for w in range(4):
        part = dot(r.h[...], rows_of(r.gq, w, 768)).astype(BF16)
        for k in range(3):
            kind, group = divmod(3 * w + k, 4)
            for v in range(2):
                for j in range(2):
                    for head in range(3):
                        row, at, col = 128 * v + 64 * j, 192 * j + 64 * kind, 192 * k + 64 * head
                        r.sb[head, 4 * v + group, :, at : at + 64] = part[row : row + 64, col : col + 64]
    gu1.z_send()
    qkv_x[0].start()
    go.stage3()
    qkv_x[1].start()
    qkv_x[2].start()

    for head in range(3):
        qkv_x[head].wait()
        for src in range(8):
            for kind, ref in enumerate((r.qh, r.kh, r.vh)):
                for j in range(2):
                    row, at = 128 * src + 64 * j, 192 * j + 64 * kind
                    part = r.rb[head, src, :, at : at + 64]
                    ref[head, row : row + 64] = part * jnp.asarray(1.0 / math.sqrt(HD), BF16) if kind == 0 else part

        def attend(c, _, head=head):
            q0 = pl.multiple_of(c * 256, 256)
            raw = dot_nt(r.qh[head, pl.ds(q0, 256)], r.kh[head])
            score = (raw.reshape(4, 64, 1024) + r.bias[head, c][:, None, :]).reshape(256, 1024)
            weight = jnp.exp(score - jnp.max(score, axis=-1, keepdims=True))
            share = 1.0 / jnp.sum(weight, axis=-1, keepdims=True)
            weight = weight.astype(BF16)
            r.prob[head, pl.ds(q0, 256)] = weight
            r.share[head, pl.ds(q0, 256)] = share
            got = (dot(weight, r.vh[head]) * share).astype(BF16)
            r.kept_o[head, pl.ds(q0, 256)] = got
            got = got.reshape(2, 2, 64, 64)
            for j in range(2):
                at = 192 * j + 64 * head
                r.ab[pl.ds(2 * c, 2), :, at : at + 64] = got[:, j]
            return 0

        lax.fori_loop(0, 4, attend, 0, unroll=True)
        if head == 0:
            go.finish()
            gd0.z_send()
        if head == 1:
            gu1.stage1()
    att_x.start()
    gu0.stage2()
    gu1.stage2()
    for w in range(4):
        for k in range(2):
            r.wout[:, :, k, :, 192 * w : 192 * w + 192] = r.go[w, :, :, :, 192 * k : 192 * k + 192]
    gd0.stage1()
    mate_g.wait_recv()
    for k in range(2):
        r.turned_g[:, 256 * k : 256 * k + 256] = turned(r.gys[k])
    att_x.wait()
    for v in range(2):
        for group in range(4):
            for j in range(2):
                row = 128 * v + 64 * j
                r.att[row : row + 64, 192 * group : 192 * group + 192] = r.at[4 * v + group, :, 192 * j : 192 * j + 192]
    mid = x[...].astype(F32) + dot(r.att[...], r.wout[...].reshape(768, 768))
    r.y[0:256] = mid
    r.y[256:512] = jnp.zeros((256, 768), F32)
    hat, rstd = norm_stats(mid)
    r.hat_b[...] = hat
    r.rstd_b[...] = rstd
    r.hs[0] = (hat * r.gains[16:17] + r.gains[24:25]).astype(BF16)
    mate_h.start()
    gd0.stage2()
    gu1.stage3()
    gd1.stage1()
    gu0.stage3()
    r.back[...] = jnp.zeros((512, 768), F32)
    r.turned_h[:, 0:256] = turned(r.hs[0])
    gu0.finish()
    gu1.finish()

    def up_weights(f):
        return jnp.concatenate([rows_of(r.gu, 2 * f + k, 768) for k in range(2)], axis=1)

    for k in range(2):
        if k == 1:
            gd0.stage3()
            gd1.stage2()
            gd0.finish()
            mate_h.wait_recv()
            gd1.stage3()
            r.turned_h[:, 256:512] = turned(r.hs[1])

        def feed_up(f, _, k=k):
            up = dot(r.hs[k], up_weights(f))
            square = up * up
            bend = jnp.tanh(GELU_C * (up + 0.044715 * up * square))
            slope = 0.5 * (1.0 + bend) + 0.5 * up * (1.0 - bend * bend) * (GELU_C * (1.0 + 0.134145 * square))
            r.act[f, 256 * k : 256 * k + 256] = (0.5 * up * (1.0 + bend)).astype(BF16)
            r.slope[f, 256 * k : 256 * k + 256] = slope.astype(BF16)
            return 0

        lax.fori_loop(0, 2, feed_up, 0, unroll=True)
    gd1.finish()
    for g in gathers:
        g.drain()

    for f in range(4):
        for c in range(2):
            for j in range(2):
                at = 384 * (f % 2) + 192 * c
                r.wd[f // 2, :, j, :, at : at + 192] = r.gd[f, c, :, :, 192 * j : 192 * j + 192]
    for k in (1, 0):

        def feed_back(f, _, k=k):
            rows = slice(256 * k, 256 * k + 256)
            grad_up = (dot(r.gys[k], rows_of(r.wd, f, 768)) * r.slope[f, rows].astype(F32)).astype(BF16)
            r.slope[f, rows] = grad_up
            r.back[rows] += dot_nt(grad_up, up_weights(f))
            return 0

        lax.fori_loop(0, 2, feed_back, 0, unroll=True)
        if k == 1:
            r.back_out[...] = r.back[256:512].astype(BF16)
            mate_back.start()

    def feed_raw(k, _):
        f = p.chip(2 * k) // 2
        act = r.act[f]
        r.y[...] += dot_nt(act, rows_of(r.wd, f, 768))
        raw_down = dot(r.turned_g[...], act).astype(BF16).reshape(4, 2, 96, 768)
        for i in range(2):
            for c in range(2):
                for j in range(2):
                    at = 384 * i + 192 * c
                    r.gd[2 * f + i, c, :, :, 192 * j : 192 * j + 192] = raw_down[:, j, :, at : at + 192]
            sd0.stage_c_of(2 * f + i)
            sd1.stage_c_of(2 * f + i)
        raw_up = dot(r.turned_h[...], r.slope[f]).astype(BF16)
        for i in range(2):
            r.gu[2 * f + i] = raw_up[:, 384 * i : 384 * i + 384].reshape(4, 2, 96, 384)
        return 0

    lax.fori_loop(0, 2, feed_raw, 0, unroll=True)
    sd0.stage_d()
    r.turned[...] = turned(r.att[...])
    r.y_out[...] = r.y[256:512].astype(BF16)
    sd1.stage_d()
    r.turned_i[...] = turned(r.hat_a[...] * r.gains[0:1] + r.gains[8:9])
    su1.stage_c()
    mate_back.wait_recv()

    r.back[0:256] += r.back_in[...].astype(F32)
    mid_grad = norm_back(r.back[0:256], r.hat_b[...], r.rstd_b[...], r.gains[16:17])
    for v in range(2):
        rows = slice(128 * v, 128 * v + 128)
        r.mid_grad[rows] = mid_grad[rows] + d_out[rows].astype(F32) * live[v].astype(F32)
    r.hb[...] = r.mid_grad[...].astype(BF16)
    att_x.drain()
    grad_o = dot_nt(r.hb[...], r.wout[...].reshape(768, 768)).astype(BF16)
    for v in range(2):
        for group in range(4):
            for j in range(2):
                row = 128 * v + 64 * j
                r.ab[4 * v + group, :, 192 * j : 192 * j + 192] = grad_o[row : row + 64, 192 * group : 192 * group + 192]
    gro_x.start()
    r.rn[...] = jnp.zeros((4, 4, 2, 8, 128), F32)

    def put_norm(w, row):
        for s in range(8):
            r.rn[w, s // 2, s % 2, 0:1, 0:96] = row[:, 96 * s : 96 * s + 96]

    put_norm(2, jnp.sum(r.back[0:256] * r.hat_b[...], axis=0, keepdims=True))
    put_norm(3, jnp.sum(r.back[0:256], axis=0, keepdims=True))
    for w in range(4):
        raw = dot(r.turned[...], r.hb[:, 192 * w : 192 * w + 192]).astype(BF16).reshape(4, 2, 2, 48, 192)
        for k in range(2):
            r.go[w, :, :, :, 192 * k : 192 * k + 192] = raw[:, :, k]
    for exchange in qkv_x:
        exchange.drain()
    sd0.stage_e()
    sd1.stage_e()
    gro_x.wait()
    su1.stage_d()

    for head in range(3):
        r.gk[...] = jnp.zeros((64, 1024), F32)
        r.gv[...] = jnp.zeros((64, 1024), F32)

        def attend_back(c, _, head=head):
            q0 = pl.multiple_of(c * 256, 256)
            halves = []
            for j in range(2):
                at = 192 * j + 64 * head
                halves.append(r.gor[pl.ds(2 * c, 2), :, at : at + 64].reshape(2, 1, 64, 64))
            grad = jnp.concatenate(halves, axis=1).reshape(256, 64)
            grad = (grad.astype(F32) * r.share[head, pl.ds(q0, 256)]).astype(BF16)
            inner = jnp.sum(grad.astype(F32) * r.kept_o[head, pl.ds(q0, 256)].astype(F32), axis=-1, keepdims=True)
            weight = r.prob[head, pl.ds(q0, 256)]
            grad_s = (weight.astype(F32) * (dot_nt(grad, r.vh[head]) - inner)).astype(BF16)
            grad_q = (dot(grad_s, r.kh[head]) * (1.0 / math.sqrt(HD))).astype(BF16).reshape(2, 2, 64, 64)
            for j in range(2):
                r.sb[head, pl.ds(2 * c, 2), :, 192 * j : 192 * j + 64] = grad_q[:, j]
            r.gk[...] += dot_tn(r.qh[head, pl.ds(q0, 256)], grad_s)
            r.gv[...] += dot_tn(grad, weight)
            return 0

        lax.fori_loop(0, 4, attend_back, 0, unroll=2)
        for kind, grad in ((1, r.gk[...]), (2, r.gv[...])):
            grad = jnp.transpose(grad).astype(BF16).reshape(8, 2, 64, 64)
            for j in range(2):
                at = 192 * j + 64 * kind
                r.sb[head, :, :, at : at + 64] = grad[:, j]
        if head == 1:
            mate_y.start()
            sd1.stage_f()
            sd0.stage_f()
            so.stage_c()
        gqkv_x[head].start()
    su0.stage_c()
    su1.stage_e()
    r.back[0:256] = jnp.zeros((256, 768), F32)
    for head in range(3):
        gqkv_x[head].wait()
        for v in range(2):
            for group in range(4):
                for kind in range(3):
                    for j in range(2):
                        row, at, to = 128 * v + 64 * j, 192 * j + 64 * kind, 768 * kind + 192 * group + 64 * head
                        r.wide[row : row + 64, to : to + 64] = r.gb[head, 4 * v + group, :, at : at + 64]
        if head == 1:
            su0.stage_d()
    so.stage_d()
    for w in range(4):
        grad = r.wide[:, 576 * w : 576 * w + 576]
        r.back[0:256] += dot_nt(grad, rows_of(r.gq, w, 768))
        r.gq[w] = dot(r.turned_i[...], grad).astype(BF16).reshape(4, 2, 96, 576)
    sq2.stage_c()
    su0.stage_e()
    sq0.stage_c()
    sq2.stage_d()
    su1.stage_f()
    sq1.stage_c()
    grad_h = r.back[0:256]
    put_norm(0, jnp.sum(grad_h * r.hat_a[...], axis=0, keepdims=True))
    put_norm(1, jnp.sum(grad_h, axis=0, keepdims=True))
    so.stage_e()
    su0.stage_f()
    sq1.stage_d()

    def put_down(k, halves):
        for half, value in enumerate(halves):
            for j in range(2):
                row, at = 96 * j + 48 * k, 192 * half
                red_d[row : row + 48, at : at + 192] = value[:, 192 * j : 192 * j + 192]

    def put_up(k, halves):
        for half, value in enumerate(halves):
            for j in range(2):
                at = 384 * j + 192 * half
                red_u[48 * k : 48 * k + 48, at : at + 192] = value[:, 192 * j : 192 * j + 192]

    def squares(ref):
        return jnp.sum(ref[...] * ref[...])

    put_down(1, sd1.finish_halves())
    so.stage_f()
    sq0.stage_d()
    mate_y.wait_recv()
    output[...] = (r.y[0:256] + r.y_in[...].astype(F32)).astype(BF16)
    stores[0].start()
    sq2.stage_e()
    put_down(0, sd0.finish_halves())
    stores[5].start()
    red_o[...] = so.finish()
    stores[3].start()
    put_up(0, su0.finish_halves())
    sq1.stage_e()
    sn.stage_c()
    sq2.stage_f()
    sq0.stage_e()
    put_up(1, su1.finish_halves())
    stores[4].start()
    sn.stage_d()
    sq1.stage_f()
    red_q[64:96] = sq2.finish()
    sn.stage_e()
    local = squares(red_o) + squares(red_u) + squares(red_d)
    sq0.stage_f()
    d_input[...] = r.mid_grad[...] + norm_back(grad_h, r.hat_a[...], r.rstd_a[...], r.gains[0:1])
    stores[1].start()
    red_q[32:64] = sq1.finish()
    sn.stage_f()
    red_q[0:32] = sq0.finish()
    stores[2].start()
    red_n[...] = sn.finish()
    stores[6].start()
    local = jnp.zeros((8, 128), F32) + (local + squares(red_q) + squares(red_n))
    r.square[...] = local
    r.squares[0] = local

    def share(k):
        to = ((p.w + k // 8) % 4, (p.s + k % 8) % 8)
        return remote(r.square, r.squares.at[k], r.sum_sems, k, to)

    def share_start(k, _):
        share(k).start()
        return 0

    def share_wait(k, _):
        share(k).wait()
        return 0

    lax.fori_loop(1, 32, share_start, 0)
    for part in (count_x, gro_x, *gqkv_x, *scatters):
        part.drain()
    for copy in (mate_h, mate_g, mate_back, mate_y):
        copy.wait_send()
    lax.fori_loop(1, 32, share_wait, 0)
    total[...] = jnp.sum(r.squares[...], axis=0)
    stores[7].start()
    for copy in stores:
        copy.wait()


def adam_kernel(*refs):
    given, made, here, there, sems = refs[0:23], refs[23:46], refs[46:69], refs[69:90], refs[90]
    loads = [pltpu.make_async_copy(a, b, sems.at[k]) for k, (a, b) in enumerate(zip(given, here))]
    stores = [pltpu.make_async_copy(a, b, sems.at[23 + k]) for k, (a, b) in enumerate(zip((*there, *here[21:23]), made))]
    order = (2, 3, 0, 1, 4)
    loads[20].start()
    for k in order:
        for part in range(4):
            loads[5 * part + k].start()
    for k in (22, 21):
        loads[k].start()
    fix_one = 1.0 - beta_one**STEP
    fix_two = 1.0 - beta_two**STEP
    rates = (rate_matrix, rate_output, rate_matrix, rate_matrix, rate_norm)
    loads[20].wait()
    norm = jnp.sqrt(here[20][0:1, 0:1])
    factor = 1.0 / jnp.maximum(norm, 1.0)
    there[20][...] = norm
    stores[20].start()
    for k in order:
        for part in range(4):
            loads[5 * part + k].wait()
        raw = here[k][...]
        if k == 1:
            raw = jnp.concatenate([raw[:, 0:192], raw[:, 192:384]], axis=0)
        if k == 4:
            raw = raw[0:1, 0:96]
        grad = raw * factor
        weight = here[5 + k][...]
        first = beta_one * here[10 + k][...] + (1.0 - beta_one) * grad
        second = beta_two * here[15 + k][...] + (1.0 - beta_two) * grad * grad
        stride = first / fix_one / (jnp.sqrt(second / fix_two) + adam_eps)
        decay = 0.0 if k == 4 else decay_rate
        there[k][...] = grad
        there[5 + k][...] = weight - rates[k] * (stride + decay * weight)
        there[10 + k][...] = first
        there[15 + k][...] = second
        for part in range(4):
            stores[5 * part + k].start()
        if k == 2:
            for j in (22, 21):
                loads[j].wait()
                stores[j].start()
    for copy in stores:
        copy.wait()


def fused_device(
    layer_input, d_out, rand_ids, live_mask, w_qkv, w_out, w_up, w_down, norm_params,
    m_qkv, m_out, m_up, m_down, m_norm, v_qkv, v_out, v_up, v_down, v_norm,
):
    smem, anywhere = (pl.BlockSpec(memory_space=kind) for kind in (pltpu.SMEM, pl.ANY))
    ids = rand_ids.transpose(0, 2, 3, 1).reshape(24, 6)
    leaves, tree = jax.tree.flatten(scratch())
    shape = jax.ShapeDtypeStruct
    output, d_input, *grads, total = pl.pallas_call(
        functools.partial(kernel, tree),
        out_shape=[shape(*leaf) for leaf in KEPT],
        in_specs=[smem, smem] + [anywhere] * 7,
        out_specs=[anywhere] * 8,
        scratch_shapes=leaves,
        compiler_params=pltpu.CompilerParams(collective_id=0, has_side_effects=True, vmem_limit_bytes=VMEM_LIMIT),
    )(
        live_mask, ids, layer_input.reshape(256, 768), d_out.reshape(256, 768), w_qkv, w_out, w_up, w_down.T,
        norm_params.reshape(1, 96),
    )
    state = (
        *grads,
        w_qkv, w_out, w_up, w_down.T, norm_params.reshape(1, 96),
        m_qkv, m_out, m_up, m_down.T, m_norm.reshape(1, 96),
        v_qkv, v_out, v_up, v_down.T, v_norm.reshape(1, 96),
        total, output, d_input,
    )
    results = [shape(w.shape, F32) for w in state[5:10]] * 4
    results += [shape((1, 1), F32), shape(output.shape, BF16), shape(d_input.shape, F32)]
    made = pl.pallas_call(
        adam_kernel,
        out_shape=results,
        in_specs=[anywhere] * 23,
        out_specs=[anywhere] * 23,
        scratch_shapes=[pltpu.VMEM(a.shape, a.dtype) for a in (*state, *results[:21])] + [pltpu.SemaphoreType.DMA((46,))],
        compiler_params=pltpu.CompilerParams(vmem_limit_bytes=VMEM_LIMIT),
    )(*state)
    updated = [m.T if k % 5 == 3 else m.reshape(-1) if k % 5 == 4 else m for k, m in enumerate(made[:20])]
    return (made[21].reshape(2, 128, 768), made[22].reshape(2, 128, 768), *updated, made[20].reshape(1))


def solution(mesh):
    placed = (
        P("win", "seq", None),
        P("win", "seq", None),
        P("win", "seq", None, None),
        P("win"),
        P("seq", "win"),
        P("seq", "win"),
        P("seq", "win"),
        P("seq", "win"),
        P(("win", "seq")),
        P("seq", "win"),
        P("seq", "win"),
        P("seq", "win"),
        P("seq", "win"),
        P(("win", "seq")),
        P("seq", "win"),
        P("seq", "win"),
        P("seq", "win"),
        P("seq", "win"),
        P(("win", "seq")),
    )
    fused = mesh.shape["win"] == 4 and mesh.shape["seq"] == 8
    return jax.shard_map(
        fused_device if fused else per_device,
        mesh=mesh,
        in_specs=placed,
        out_specs=(
            P("win", "seq", None),
            P("win", "seq", None),
            P("seq", "win"),
            P("seq", "win"),
            P("seq", "win"),
            P("seq", "win"),
            P(("win", "seq")),
            P("seq", "win"),
            P("seq", "win"),
            P("seq", "win"),
            P("seq", "win"),
            P(("win", "seq")),
            P("seq", "win"),
            P("seq", "win"),
            P("seq", "win"),
            P("seq", "win"),
            P(("win", "seq")),
            P("seq", "win"),
            P("seq", "win"),
            P("seq", "win"),
            P("seq", "win"),
            P(("win", "seq")),
            P(),
        ),
        check_vma=False,
    )
```
